256 devices in a mesh: cells: 64 (over y, z, core), rank: 4 (over x).
Axes of the slice: x: 4, y: 4, z: 8, core: 2. Of those that a mesh axis runs over, the one named last changes fastest.
Arguments:
- x_emb: bfloat16 [32768, 256], P('cells'), may hold values from -40 to 40, as said below
- y_emb: bfloat16 [32768, 256], P('cells'), may hold values from -40 to 40, as said below
- q_factor: float32 [32768, 512], P('cells', 'rank'), may hold values from 0 to 45, as said below
- r_factor: float32 [32768, 512], P('cells', 'rank'), may hold values from 0 to 45, as said below
- g_weights: float32 [512], P('rank'), may hold values from 16384 to 65536
- a_mass: float32 [32768], P('cells'), may hold values from 128 to 512
- b_mass: float32 [32768], P('cells'), may hold values from 128 to 512
- expr: bfloat16 [32768, 2048], P('cells', 'rank'), may hold values from -9 to 9, as said below
Outputs:
- q_new: float32 [32768, 512], P('cells', 'rank')
- r_new: float32 [32768, 512], P('cells', 'rank')
- rank_share: float32 [512], P('rank')
- predicted: bfloat16 [32768, 2048], P('cells', 'rank')
The draws below stay inside these ranges and needn't reach their ends.
Inputs may be any that keep to these rules, and one draw needn't show every extreme that they name: `x_emb`: finite embedding values. `y_emb`: finite embedding values. `q_factor`: every entry is positive. `r_factor`: every entry is positive. `expr`: finite expression values.
All inputs are finite; a program needn't handle non-finite values. Where the reference program divides by a largest or mean magnitude, that divisor is 1e-20 or more.
Results may differ from the reference program's by a relative error of at most 0.0075.
Values may be sent and summed in bfloat16 or wider, within the bound.
No kernel may reach another device: no remote copies, remote signals or barrier semaphores. Data moves between devices by JAX's collectives and lax.ppermute only.
A program may use at most 64 MiB of HBM per device.

```python
import math
import jax
import jax.numpy as jnp

DIM = 256
RANK = 512
GENES = 2048
PASSES = 10
CELLS = 32768


def ramp_factor(count):
    ramp = jnp.arange(count, dtype=jnp.float32) / max(count - 1, 1)
    return 1.0 + 2.0 * ramp


def embedding_rows(key, offset):
    rows = ramp_factor(CELLS)
    base = jnp.clip(jax.random.normal(key, (CELLS, DIM), jnp.float32), -6.0, 6.0)
    jitter = jnp.exp(jax.random.uniform(jax.random.fold_in(key, 5), (CELLS,), jnp.float32, -0.4, 0.4))
    values = (base + offset) * (rows * jitter)[:, None]
    return jnp.clip(values, -40.0, 40.0)


def draw_x_emb(key, part):
    return embedding_rows(jax.random.fold_in(key, 11), 0.0).astype(jnp.bfloat16)


def draw_y_emb(key, part):
    offset = jax.random.uniform(jax.random.fold_in(key, 23), (DIM,), jnp.float32, -1.0, 1.0)
    return embedding_rows(jax.random.fold_in(key, 29), offset[None, :]).astype(jnp.bfloat16)


def cluster_labels(key, salt):
    return jax.random.randint(jax.random.fold_in(key, salt), (CELLS,), 0, RANK)


def factor_entries(key, salt):
    labels = cluster_labels(key, salt)
    member = (labels[:, None] == jnp.arange(RANK)[None, :]).astype(jnp.float32)
    rows = ramp_factor(CELLS)
    noise = jax.random.uniform(jax.random.fold_in(key, salt + 1), (CELLS, RANK), jnp.float32, 0.25, 1.0)
    return noise * (1.0 + 4.0 * member) * rows[:, None]


def draw_q_factor(key, part):
    return factor_entries(key, 101)


def draw_r_factor(key, part):
    return factor_entries(key, 201)


def draw_expr(key, part):
    labels = cluster_labels(key, 201)
    profile = jnp.clip(jax.random.normal(jax.random.fold_in(key, 301), (RANK, GENES), jnp.float32), -6.0, 6.0)
    noise = 0.5 * jnp.clip(jax.random.normal(jax.random.fold_in(key, 302), (CELLS, GENES), jnp.float32), -6.0, 6.0)
    return (profile[labels] + noise).astype(jnp.bfloat16)


def levels(stream_key, extent, shards, smallest, largest):
    def one(position, shards_of):
        steps = jax.random.uniform(jax.random.fold_in(jax.random.fold_in(stream_key, 6), position), (shards_of,), jnp.float32, smallest / len(shards), largest / len(shards))
        return jnp.repeat(jnp.exp(steps), extent[position] // shards_of).reshape((-1,) + (1,) * (len(extent) - position - 1))

    loudness = one(*shards[0])
    for cut in shards[1:]:
        loudness = loudness * one(*cut)
    return loudness


def setup_inputs(seed: int = 0) -> dict:
    seeds = jax.random.split(jax.random.key(seed), 9)
    x_emb = draw_x_emb(jax.random.fold_in(seeds[8], 71), 0)
    y_emb = draw_y_emb(jax.random.fold_in(seeds[8], 71), 0)
    q_factor = draw_q_factor(jax.random.fold_in(seeds[8], 71), 0)
    r_factor = draw_r_factor(jax.random.fold_in(seeds[8], 71), 0)
    g_weights = jnp.clip(jnp.exp(math.log(65536.0) - 1.3862944 * jax.random.uniform(seeds[4], (RANK,), jnp.float32) ** levels(seeds[4], (RANK,), ((0, 4),), -0.2, 0.2)), 16384.0, 65536.0)
    a_mass = jnp.clip(jnp.exp(math.log(512.0) - 1.3862944 * jax.random.uniform(seeds[5], (CELLS,), jnp.float32) ** levels(seeds[5], (CELLS,), ((0, 64),), -0.2, 0.2)), 128.0, 512.0)
    b_mass = jnp.clip(jnp.exp(math.log(512.0) - 1.3862944 * jax.random.uniform(seeds[6], (CELLS,), jnp.float32) ** levels(seeds[6], (CELLS,), ((0, 64),), -0.2, 0.2)), 128.0, 512.0)
    expr = draw_expr(jax.random.fold_in(seeds[8], 71), 0)
    return dict(x_emb=x_emb, y_emb=y_emb, q_factor=q_factor, r_factor=r_factor, g_weights=g_weights, a_mass=a_mass, b_mass=b_mass, expr=expr)


SCALE = 0.0625
GAMMA = 10.0
POWER = 0.8


def reference(x_emb, y_emb, q_factor, r_factor, g_weights, a_mass, b_mass, expr):
    norms_one = jnp.sum(jnp.square(x_emb.astype(jnp.float32)), axis=1)
    norms_two = jnp.sum(jnp.square(y_emb.astype(jnp.float32)), axis=1)
    q_round = q_factor.astype(jnp.bfloat16)
    r_round = r_factor.astype(jnp.bfloat16)
    cross_xq = jnp.dot(x_emb.T, q_round, preferred_element_type=jnp.float32)
    cross_yr = jnp.dot(y_emb.T, r_round, preferred_element_type=jnp.float32)
    xq_vec = jnp.sum(norms_one[:, None] * q_factor, axis=0)
    cq_vec = jnp.sum(q_factor, axis=0)
    yr_vec = jnp.sum(norms_two[:, None] * r_factor, axis=0)
    cr_vec = jnp.sum(r_factor, axis=0)
    grad_q = SCALE * (norms_one[:, None] * cr_vec[None, :] + yr_vec[None, :]
                      - 2.0 * jnp.dot(x_emb, cross_yr.astype(jnp.bfloat16), preferred_element_type=jnp.float32)) / g_weights[None, :]
    grad_r = SCALE * (norms_two[:, None] * cq_vec[None, :] + xq_vec[None, :]
                      - 2.0 * jnp.dot(y_emb, cross_xq.astype(jnp.bfloat16), preferred_element_type=jnp.float32)) / g_weights[None, :]
    curvature = SCALE * (xq_vec * cr_vec + cq_vec * yr_vec - 2.0 * jnp.sum(cross_xq * cross_yr, axis=0))
    grad_g = -curvature / jnp.square(g_weights)
    peak = jnp.maximum(jnp.max(jnp.abs(grad_q)), jnp.maximum(jnp.max(jnp.abs(grad_r)), jnp.max(jnp.abs(grad_g))))
    eta = GAMMA / (peak + 1e-6)
    kern_q = q_factor * jnp.exp(-eta * grad_q)
    kern_r = r_factor * jnp.exp(-eta * grad_r)
    kern_g = g_weights * jnp.exp(-eta * grad_g)
    v_q = jnp.ones((RANK,), jnp.float32)
    v_r = jnp.ones((RANK,), jnp.float32)
    u_q = jnp.ones((CELLS,), jnp.float32)
    u_r = jnp.ones((CELLS,), jnp.float32)
    weights = kern_g
    for step in range(PASSES):
        s_q = jnp.sum(kern_q * v_q[None, :], axis=1)
        s_r = jnp.sum(kern_r * v_r[None, :], axis=1)
        u_q = (a_mass / s_q) ** POWER
        u_r = (b_mass / s_r) ** POWER
        t_q = jnp.sum(kern_q * u_q[:, None], axis=0)
        t_r = jnp.sum(kern_r * u_r[:, None], axis=0)
        weights = jnp.exp((jnp.log(kern_g) + jnp.log(v_q * t_q) + jnp.log(v_r * t_r)) / 3.0)
        v_q = weights / t_q
        v_r = weights / t_r
    q_new = u_q[:, None] * kern_q * v_q[None, :]
    r_new = u_r[:, None] * kern_r * v_r[None, :]
    row_mass = jnp.sum(q_new, axis=1)
    scaled = (q_new / weights[None, :]).astype(jnp.bfloat16)
    profiles = jnp.dot(r_new.astype(jnp.bfloat16).T, expr, preferred_element_type=jnp.float32)
    mixed = jnp.dot(scaled, profiles.astype(jnp.bfloat16), preferred_element_type=jnp.float32)
    predicted = (mixed / row_mass[:, None]).astype(jnp.bfloat16)
    return q_new, r_new, weights / CELLS, predicted
```

```python
import jax
import jax.numpy as jnp
from jax import lax
from jax.sharding import Mesh
from jax.sharding import PartitionSpec as P

PASSES = 10
SCALE = 0.0625
GAMMA = 10.0
POWER = 0.8

CELLS = ("y", "z", "c")
EVERY = ("y", "z", "c", "x")
F32 = jnp.float32
BF16 = jnp.bfloat16


def contract_rows(left, right):
    return lax.dot_general(
        left, right, (((0,), (0,)), ((), ())), preferred_element_type=F32
    )


def exchange(chunks, axes):
    return lax.all_to_all(chunks, axes, 0, 0, tiled=False)


def to_all(value, axes):
    count = lax.axis_size(axes)
    return exchange(jnp.broadcast_to(value[None], (count,) + value.shape), axes)


def split3(value):
    high = lax.reduce_precision(value, 8, 7)
    rest = value - high
    middle = lax.reduce_precision(rest, 8, 7)
    low = lax.reduce_precision(rest - middle, 8, 7)
    return jnp.stack([high, middle, low]).astype(BF16)


def join3(rows):
    parts = rows.astype(F32)
    return parts[..., 0, :] + (parts[..., 1, :] + parts[..., 2, :])


def shards(x_emb, y_emb, q_factor, r_factor, g_weights, a_mass, b_mass, expr):
    rows, width = q_factor.shape
    dim = x_emb.shape[1]
    genes = expr.shape[1]
    cell_devices = lax.axis_size(CELLS)
    ranks = lax.axis_size("x")
    cells_total = rows * cell_devices
    share = dim // cell_devices

    norms_one = jnp.sum(jnp.square(x_emb.astype(F32)), axis=1)
    norms_two = jnp.sum(jnp.square(y_emb.astype(F32)), axis=1)
    part_xq = contract_rows(x_emb, q_factor.astype(BF16))
    part_yr = contract_rows(y_emb, r_factor.astype(BF16))
    part_vec = jnp.stack(
        [
            jnp.sum(norms_one[:, None] * q_factor, axis=0),
            jnp.sum(q_factor, axis=0),
            jnp.sum(norms_two[:, None] * r_factor, axis=0),
            jnp.sum(r_factor, axis=0),
        ]
    )
    outgoing = jnp.concatenate(
        [
            part_xq.reshape(cell_devices, share, width),
            part_yr.reshape(cell_devices, share, width),
            jnp.broadcast_to(part_vec[None], (cell_devices, 4, width)),
        ],
        axis=1,
    )
    summed = jnp.sum(exchange(outgoing, CELLS), axis=0)
    mine_xq, mine_yr = summed[:share], summed[share : 2 * share]
    xq_vec, cq_vec, yr_vec, cr_vec = (summed[2 * share + i] for i in range(4))
    mine_dot = jnp.sum(mine_xq * mine_yr, axis=0)
    crosses = to_all(
        jnp.concatenate([mine_xq.astype(BF16), mine_yr.astype(BF16), split3(mine_dot)], axis=0),
        CELLS,
    )
    cross_xq = crosses[:, :share].reshape(dim, width)
    cross_yr = crosses[:, share : 2 * share].reshape(dim, width)
    cross_dot = jnp.sum(join3(crosses[:, 2 * share :]), axis=0)

    grad_q = (
        SCALE
        * (
            norms_one[:, None] * cr_vec[None, :]
            + yr_vec[None, :]
            - 2.0 * jnp.dot(x_emb, cross_yr, preferred_element_type=F32)
        )
        / g_weights[None, :]
    )
    grad_r = (
        SCALE
        * (
            norms_two[:, None] * cq_vec[None, :]
            + xq_vec[None, :]
            - 2.0 * jnp.dot(y_emb, cross_xq, preferred_element_type=F32)
        )
        / g_weights[None, :]
    )
    curvature = SCALE * (xq_vec * cr_vec + cq_vec * yr_vec - 2.0 * cross_dot)
    grad_g = -curvature / jnp.square(g_weights)
    local_peak = jnp.maximum(
        jnp.max(jnp.abs(grad_q), axis=0),
        jnp.maximum(jnp.max(jnp.abs(grad_r), axis=0), jnp.abs(grad_g)),
    )
    peak = jnp.max(to_all(local_peak[None], EVERY))
    eta = GAMMA / (peak + 1e-06)
    kern_q = q_factor * jnp.exp(-eta * grad_q)
    kern_r = r_factor * jnp.exp(-eta * grad_r)
    kern_g = g_weights * jnp.exp(-eta * grad_g)

    kerns = to_all(
        jnp.concatenate([kern_q.astype(BF16), kern_r.astype(BF16), split3(kern_g)], axis=0), "x"
    )
    all_q = kerns[:, :rows]
    all_r = kerns[:, rows : 2 * rows]
    log_g = jnp.log(join3(kerns[:, 2 * rows :]))

    def row_sums(v_q, v_r):
        return (
            jnp.sum(all_q.astype(F32) * v_q[:, None, :], axis=(0, 2)),
            jnp.sum(all_r.astype(F32) * v_r[:, None, :], axis=(0, 2)),
        )

    v_q = jnp.ones((ranks, width), F32)
    v_r = jnp.ones((ranks, width), F32)
    for step in range(PASSES):
        s_q, s_r = row_sums(v_q, v_r)
        u_q = (a_mass / s_q) ** POWER
        u_r = (b_mass / s_r) ** POWER
        part = jnp.concatenate(
            [
                jnp.sum(all_q.astype(F32) * u_q[None, :, None], axis=1),
                jnp.sum(all_r.astype(F32) * u_r[None, :, None], axis=1),
            ],
            axis=0,
        )
        total = jnp.sum(to_all(part, CELLS), axis=0)
        t_q, t_r = total[:ranks], total[ranks:]
        weights = jnp.exp((log_g + jnp.log(v_q * t_q) + jnp.log(v_r * t_r)) / 3.0)
        v_q = weights / t_q
        v_r = weights / t_r

    here = lax.axis_index("x")

    def own(value):
        return lax.dynamic_index_in_dim(value, here, 0, keepdims=False)

    q_new = u_q[:, None] * kern_q * own(v_q)[None, :]
    r_new = u_r[:, None] * kern_r * own(v_r)[None, :]
    s_q = jnp.sum(all_q.astype(F32) * v_q[:, None, :], axis=(0, 2))
    right = (all_r.astype(F32) * v_r[:, None, :] * u_r[None, :, None]).astype(BF16)
    scaled = (all_q.astype(F32) * (v_q / weights)[:, None, :]).astype(BF16)

    part = lax.dot_general(
        right, expr, (((1,), (0,)), ((), ())), preferred_element_type=F32
    ).reshape(2, ranks * width // 2, genes)
    half = jnp.sum(exchange(part, "c"), axis=0)
    others = lax.axis_size(("y", "z"))
    piece = jnp.sum(exchange(half.reshape(others, -1, genes), ("y", "z")), axis=0)
    half = to_all(piece.astype(BF16), ("y", "z")).reshape(-1, genes)
    profiles = lax.all_gather(half, "c", axis=0, tiled=True).reshape(ranks, width, genes)
    mixed = lax.dot_general(
        scaled, profiles, (((0, 2), (0, 1)), ((), ())), preferred_element_type=F32
    )
    predicted = (mixed / s_q[:, None]).astype(BF16)
    return (q_new, r_new, own(weights) / cells_total, predicted)


def solution(mesh):
    named = Mesh(mesh.devices.reshape(4, 8, 2, 4), EVERY)
    block = P(CELLS, "x")
    return jax.shard_map(
        shards,
        mesh=named,
        in_specs=(
            P(CELLS, None),
            P(CELLS, None),
            block,
            block,
            P("x"),
            P(CELLS),
            P(CELLS),
            block,
        ),
        out_specs=(block, block, P("x"), block),
        check_vma=False,
    )
```

```python
import jax
import jax.numpy as jnp
from jax import lax
from jax.sharding import Mesh
from jax.sharding import PartitionSpec as P

PASSES = 10
SCALE = 0.0625
GAMMA = 10.0
POWER = 0.8

CHIPS = ("y", "z")
CELLS = ("y", "z", "c")
EVERY = ("y", "z", "c", "x")
F32 = jnp.float32
BF16 = jnp.bfloat16


def contract_rows(left, right):
    return lax.dot_general(
        left, right, (((0,), (0,)), ((), ())), preferred_element_type=F32
    )


def exchange(chunks, axes):
    return lax.all_to_all(chunks, axes, 0, 0, tiled=False)


def to_all(value, axes):
    count = lax.axis_size(axes)
    return exchange(jnp.broadcast_to(value[None], (count,) + value.shape), axes)


def swap(value):
    return lax.ppermute(value, "c", [(0, 1), (1, 0)])


def pick(value, index):
    return lax.dynamic_index_in_dim(value, index, 0, keepdims=False)


def split3(value):
    high = lax.reduce_precision(value, 8, 7)
    rest = value - high
    middle = lax.reduce_precision(rest, 8, 7)
    low = lax.reduce_precision(rest - middle, 8, 7)
    return jnp.stack([high, middle, low]).astype(BF16)


def join3(rows):
    parts = rows.astype(F32)
    return parts[..., 0, :] + (parts[..., 1, :] + parts[..., 2, :])


def shards(x_emb, y_emb, q_factor, r_factor, g_weights, a_mass, b_mass, expr):
    rows, width = q_factor.shape
    dim = x_emb.shape[1]
    genes = expr.shape[1]
    others = lax.axis_size(CHIPS)
    cell_devices = 2 * others
    ranks = lax.axis_size("x")
    cells_total = rows * cell_devices
    share = dim // cell_devices

    here = lax.axis_index("x")
    core = lax.axis_index("c")
    other_expr = swap(expr)
    masses = jnp.stack([a_mass, b_mass])
    masses = jnp.stack([masses, swap(masses)])
    norms_one = jnp.sum(jnp.square(x_emb.astype(F32)), axis=1)
    norms_two = jnp.sum(jnp.square(y_emb.astype(F32)), axis=1)
    part_xq = contract_rows(x_emb, q_factor.astype(BF16)).reshape(2, others, share, width)
    part_yr = contract_rows(y_emb, r_factor.astype(BF16)).reshape(2, others, share, width)
    part_cross = jnp.concatenate([part_xq, part_yr], axis=2)
    part_vec = jnp.stack(
        [
            jnp.sum(norms_one[:, None] * q_factor, axis=0),
            jnp.sum(q_factor, axis=0),
            jnp.sum(norms_two[:, None] * r_factor, axis=0),
            jnp.sum(r_factor, axis=0),
        ]
    )

    def with_vec(cross):
        return jnp.concatenate(
            [cross, jnp.broadcast_to(part_vec[None], (others, 4, width))], axis=1
        ).reshape(others, (2 * share + 4) // 4, 4, width)

    outgoing = with_vec(pick(part_cross, core)) + swap(with_vec(pick(part_cross, 1 - core)))
    summed = jnp.sum(exchange(outgoing, CHIPS), axis=0).reshape(2 * share + 4, width)
    mine_xq, mine_yr = summed[:share], summed[share : 2 * share]
    xq_vec, cq_vec, yr_vec, cr_vec = (summed[2 * share + i] for i in range(4))
    mine_dot = jnp.sum(mine_xq * mine_yr, axis=0)
    sent = jnp.concatenate(
        [
            mine_xq.astype(BF16),
            mine_yr.astype(BF16),
            split3(mine_dot),
            jnp.zeros((1, width), BF16),
        ],
        axis=0,
    ).reshape(share + 2, 2, width)
    crosses = lax.all_gather(to_all(sent, CHIPS), "c").reshape(2 * others, 2 * share + 4, width)
    cross_xq = crosses[:, :share].reshape(dim, width)
    cross_yr = crosses[:, share : 2 * share].reshape(dim, width)
    cross_dot = jnp.sum(join3(crosses[:, 2 * share : 2 * share + 3]), axis=0)

    grad_q = (
        SCALE
        * (
            norms_one[:, None] * cr_vec[None, :]
            + yr_vec[None, :]
            - 2.0 * jnp.dot(x_emb, cross_yr, preferred_element_type=F32)
        )
        / g_weights[None, :]
    )
    grad_r = (
        SCALE
        * (
            norms_two[:, None] * cq_vec[None, :]
            + xq_vec[None, :]
            - 2.0 * jnp.dot(y_emb, cross_xq, preferred_element_type=F32)
        )
        / g_weights[None, :]
    )
    curvature = SCALE * (xq_vec * cr_vec + cq_vec * yr_vec - 2.0 * cross_dot)
    grad_g = -curvature / jnp.square(g_weights)
    local_peak = jnp.maximum(
        jnp.max(jnp.abs(grad_q), axis=0),
        jnp.maximum(jnp.max(jnp.abs(grad_r), axis=0), jnp.abs(grad_g)),
    )
    peak = jnp.max(to_all(local_peak[None], EVERY))
    eta = GAMMA / (peak + 1e-06)
    kern_q = q_factor * jnp.exp(-eta * grad_q)
    kern_r = r_factor * jnp.exp(-eta * grad_r)
    kern_g = g_weights * jnp.exp(-eta * grad_g)

    mine = to_all(
        jnp.concatenate([kern_q.astype(BF16), kern_r.astype(BF16), split3(kern_g)], axis=0), "x"
    )
    log_g = jnp.log(join3(mine[:, 2 * rows :]))
    mine_q = mine[:, :rows]
    kerns = mine[:, : 2 * rows]
    pair = jnp.stack([kerns, swap(kerns)]).reshape(2, ranks, 2, rows, width)
    flat = jnp.ones((2, ranks, width), F32)

    def one_pass(v):
        s = jnp.sum(pair.astype(F32) * v.transpose(1, 0, 2)[None, :, :, None, :], axis=(1, 4))
        u = (masses / s) ** POWER
        parts = jnp.sum(pair.astype(F32) * u[:, None, :, :, None], axis=3)
        part = (parts[0] + parts[1]).transpose(1, 0, 2).reshape(2 * ranks, width)
        t = jnp.sum(to_all(part, CHIPS), axis=0).reshape(2, ranks, width)
        weights = jnp.exp((log_g + jnp.log(v[0] * t[0]) + jnp.log(v[1] * t[1])) / 3.0)
        return weights[None] / t, weights, u

    v = lax.fori_loop(0, PASSES - 1, lambda step, v: one_pass(v)[0], flat)
    (v_q, v_r), weights, u = one_pass(v)

    q_new = u[0, 0][:, None] * kern_q * pick(v_q, here)[None, :]
    r_new = u[0, 1][:, None] * kern_r * pick(v_r, here)[None, :]
    s_q = jnp.sum(mine_q.astype(F32) * v_q[:, None, :], axis=(0, 2))
    scaled = (mine_q.astype(F32) * (v_q / weights)[:, None, :]).astype(BF16)

    half = ranks // 2
    half_v = lax.dynamic_slice_in_dim(v_r, core * half, half, 0)

    def product(member, cells):
        kern = lax.dynamic_slice_in_dim(pair[member, :, 1], core * half, half, 0)
        right = (kern.astype(F32) * half_v[:, None, :] * u[member, 1][None, :, None]).astype(BF16)
        return lax.dot_general(right, cells, (((1,), (0,)), ((), ())), preferred_element_type=F32)

    part = product(0, expr) + product(1, other_expr)
    piece = jnp.sum(exchange(part.reshape(others, -1, genes), CHIPS), axis=0)
    profiles = lax.all_gather(to_all(piece.astype(BF16), CHIPS), "c").reshape(ranks, width, genes)
    mixed = lax.dot_general(
        scaled, profiles, (((0, 2), (0, 1)), ((), ())), preferred_element_type=F32
    )
    predicted = (mixed / s_q[:, None]).astype(BF16)
    return (q_new, r_new, pick(weights, here) / cells_total, predicted)


def solution(mesh):
    named = Mesh(mesh.devices.reshape(4, 8, 2, 4), EVERY)
    block = P(CELLS, "x")
    return jax.shard_map(
        shards,
        mesh=named,
        in_specs=(
            P(CELLS, None),
            P(CELLS, None),
            block,
            block,
            P("x"),
            P(CELLS),
            P(CELLS),
            block,
        ),
        out_specs=(block, block, P("x"), block),
        check_vma=False,
    )
```

```python
import jax
import jax.numpy as jnp
from jax import lax
from jax.experimental import pallas as pl
from jax.experimental.pallas import tpu as pltpu
from jax.sharding import Mesh
from jax.sharding import PartitionSpec as P

PASSES = 10
SCALE = 0.0625
GAMMA = 10.0
POWER = 0.8

CHIPS = ("y", "z")
CELLS = ("y", "z", "c")
EVERY = ("y", "z", "c", "x")
F32 = jnp.float32
BF16 = jnp.bfloat16


def contract_rows(left, right):
    return lax.dot_general(
        left, right, (((0,), (0,)), ((), ())), preferred_element_type=F32
    )


def exchange(chunks, axes):
    return lax.all_to_all(chunks, axes, 0, 0, tiled=False)


def to_all(value, axes):
    count = lax.axis_size(axes)
    return exchange(jnp.broadcast_to(value[None], (count,) + value.shape), axes)


def swap(value):
    return lax.ppermute(value, "c", [(0, 1), (1, 0)])


def pick(value, index):
    return lax.dynamic_index_in_dim(value, index, 0, keepdims=False)


def split3(value):
    high = lax.reduce_precision(value, 8, 7)
    rest = value - high
    middle = lax.reduce_precision(rest, 8, 7)
    low = lax.reduce_precision(rest - middle, 8, 7)
    return jnp.stack([high, middle, low]).astype(BF16)


def join3(rows):
    parts = rows.astype(F32)
    return parts[..., 0, :] + (parts[..., 1, :] + parts[..., 2, :])


def stack3(value):
    high = value.astype(BF16).astype(F32)
    rest = value - high
    middle = rest.astype(BF16).astype(F32)
    return jnp.concatenate([high, middle, rest - middle], axis=0)


def one_row(stacked, row, period):
    index = lax.broadcasted_iota(jnp.int32, stacked.shape, 0) % period
    return jnp.where(index == row, stacked, 0.0).astype(BF16)


def new_scalings(ranks, got_ref, v_ref, log_ref):
    t = jnp.sum(got_ref[...], axis=0)
    passed = jnp.log(v_ref[...] * t)
    weights = jnp.exp((log_ref[...] + passed[:ranks] + passed[ranks:]) / 3.0)
    return jnp.concatenate([weights, weights], axis=0) / t, weights


def send_columns(ranks, rows, v, mass_ref, own_ref, other_ref, sent_ref, u_ref):
    v_stack = stack3(v)
    sums = []
    for kern_ref in (own_ref, other_ref):
        for side in range(2):
            total = None
            for block in range(ranks):
                part = lax.dot_general(
                    one_row(v_stack, side * ranks + block, 2 * ranks),
                    kern_ref[block, pl.ds(side * rows, rows), :],
                    (((1,), (1,)), ((), ())),
                    preferred_element_type=F32,
                )
                total = part if total is None else total + part
            sums.append(jnp.sum(total, axis=0, keepdims=True))
    s = jnp.concatenate(sums, axis=0)
    u = jnp.exp(POWER * jnp.log(mass_ref[...] / s))
    u_ref[...] = u
    u_stack = stack3(u)
    columns = []
    for side in range(2):
        picked = [one_row(u_stack, 2 * member + side, 4) for member in range(2)]
        for block in range(ranks):
            total = None
            for member, kern_ref in enumerate((own_ref, other_ref)):
                part = lax.dot_general(
                    picked[member],
                    kern_ref[block, pl.ds(side * rows, rows), :],
                    (((1,), (0,)), ((), ())),
                    preferred_element_type=F32,
                )
                total = part if total is None else total + part
            columns.append(jnp.sum(total, axis=0, keepdims=True))
    part = jnp.concatenate(columns, axis=0)
    sent_ref[...] = jnp.broadcast_to(part[None], sent_ref.shape).astype(sent_ref.dtype)


def first_pass(mass_ref, own_ref, other_ref, sent_ref, u_ref):
    ranks = own_ref.shape[0]
    rows = other_ref.shape[1] // 2
    ones = jnp.ones((2 * ranks, own_ref.shape[2]), F32)
    send_columns(ranks, rows, ones, mass_ref, own_ref, other_ref, sent_ref, u_ref)


def next_pass(got_ref, v_ref, log_ref, mass_ref, own_ref, other_ref, sent_ref, u_ref, new_ref):
    ranks = own_ref.shape[0]
    rows = other_ref.shape[1] // 2
    v, _ = new_scalings(ranks, got_ref, v_ref, log_ref)
    new_ref[...] = v
    send_columns(ranks, rows, v, mass_ref, own_ref, other_ref, sent_ref, u_ref)


def on_chip(kernel, shapes, name):
    return pl.pallas_call(
        kernel,
        out_shape=tuple(jax.ShapeDtypeStruct(shape, dtype) for shape, dtype in shapes),
        compiler_params=pltpu.CompilerParams(vmem_limit_bytes=32 << 20),
        name=name,
    )


def shards(x_emb, y_emb, q_factor, r_factor, g_weights, a_mass, b_mass, expr):
    rows, width = q_factor.shape
    dim = x_emb.shape[1]
    genes = expr.shape[1]
    others = lax.axis_size(CHIPS)
    cell_devices = 2 * others
    ranks = lax.axis_size("x")
    cells_total = rows * cell_devices
    share = dim // cell_devices

    here = lax.axis_index("x")
    core = lax.axis_index("c")
    other_expr = swap(expr)
    masses = jnp.stack([a_mass, b_mass])
    masses = jnp.concatenate([masses, swap(masses)])
    norms_one = jnp.sum(jnp.square(x_emb.astype(F32)), axis=1)
    norms_two = jnp.sum(jnp.square(y_emb.astype(F32)), axis=1)
    part_xq = contract_rows(x_emb, q_factor.astype(BF16)).reshape(2, others, share, width)
    part_yr = contract_rows(y_emb, r_factor.astype(BF16)).reshape(2, others, share, width)
    part_cross = jnp.concatenate([part_xq, part_yr], axis=2)
    part_vec = jnp.stack(
        [
            jnp.sum(norms_one[:, None] * q_factor, axis=0),
            jnp.sum(q_factor, axis=0),
            jnp.sum(norms_two[:, None] * r_factor, axis=0),
            jnp.sum(r_factor, axis=0),
        ]
    )

    def with_vec(cross):
        return jnp.concatenate(
            [cross, jnp.broadcast_to(part_vec[None], (others, 4, width))], axis=1
        ).reshape(others, (2 * share + 4) // 4, 4, width)

    outgoing = with_vec(pick(part_cross, core)) + swap(with_vec(pick(part_cross, 1 - core)))
    summed = jnp.sum(exchange(outgoing, CHIPS), axis=0).reshape(2 * share + 4, width)
    mine_xq, mine_yr = summed[:share], summed[share : 2 * share]
    xq_vec, cq_vec, yr_vec, cr_vec = (summed[2 * share + i] for i in range(4))
    mine_dot = jnp.sum(mine_xq * mine_yr, axis=0)
    sent = jnp.concatenate(
        [
            mine_xq.astype(BF16),
            mine_yr.astype(BF16),
            split3(mine_dot),
            jnp.zeros((1, width), BF16),
        ],
        axis=0,
    ).reshape(share + 2, 2, width)
    crosses = lax.all_gather(to_all(sent, CHIPS), "c").reshape(2 * others, 2 * share + 4, width)
    cross_xq = crosses[:, :share].reshape(dim, width)
    cross_yr = crosses[:, share : 2 * share].reshape(dim, width)
    cross_dot = jnp.sum(join3(crosses[:, 2 * share : 2 * share + 3]), axis=0)

    grad_q = (
        SCALE
        * (
            norms_one[:, None] * cr_vec[None, :]
            + yr_vec[None, :]
            - 2.0 * jnp.dot(x_emb, cross_yr, preferred_element_type=F32)
        )
        / g_weights[None, :]
    )
    grad_r = (
        SCALE
        * (
            norms_two[:, None] * cq_vec[None, :]
            + xq_vec[None, :]
            - 2.0 * jnp.dot(y_emb, cross_xq, preferred_element_type=F32)
        )
        / g_weights[None, :]
    )
    curvature = SCALE * (xq_vec * cr_vec + cq_vec * yr_vec - 2.0 * cross_dot)
    grad_g = -curvature / jnp.square(g_weights)
    local_peak = jnp.maximum(
        jnp.max(jnp.abs(grad_q), axis=0),
        jnp.maximum(jnp.max(jnp.abs(grad_r), axis=0), jnp.abs(grad_g)),
    )
    peak = jnp.max(to_all(local_peak[None], EVERY))
    eta = GAMMA / (peak + 1e-06)
    kern_q = q_factor * jnp.exp(-eta * grad_q)
    kern_r = r_factor * jnp.exp(-eta * grad_r)
    kern_g = g_weights * jnp.exp(-eta * grad_g)

    mine = to_all(
        jnp.concatenate([kern_q.astype(BF16), kern_r.astype(BF16), split3(kern_g)], axis=0), "x"
    )
    log_g = jnp.log(join3(mine[:, 2 * rows :]))
    mine_q = mine[:, :rows]
    kerns = mine[:, : 2 * rows]
    theirs = swap(kerns)
    sent_shape = ((others, 2 * ranks, width), F32)
    u_shape = ((4, rows), F32)
    v_shape = ((2 * ranks, width), F32)
    sent, u = on_chip(first_pass, (sent_shape, u_shape), "first_pass")(masses, kerns, theirs)
    v = jnp.ones(v_shape[0], F32)
    for step in range(1, PASSES):
        sent, u, v = on_chip(next_pass, (sent_shape, u_shape, v_shape), "next_pass")(
            exchange(sent, CHIPS), v, log_g, masses, kerns, theirs
        )
    t = jnp.sum(exchange(sent, CHIPS), axis=0)
    passed = jnp.log(v * t)
    weights = jnp.exp((log_g + passed[:ranks] + passed[ranks:]) / 3.0)
    v_q, v_r = weights / t[:ranks], weights / t[ranks:]

    q_new = u[0][:, None] * kern_q * pick(v_q, here)[None, :]
    r_new = u[1][:, None] * kern_r * pick(v_r, here)[None, :]
    s_q = jnp.sum(mine_q.astype(F32) * v_q[:, None, :], axis=(0, 2))
    scaled = (mine_q.astype(F32) * (v_q / weights)[:, None, :]).astype(BF16)

    half = ranks // 2
    half_v = lax.dynamic_slice_in_dim(v_r, core * half, half, 0)

    def product(kern, u_cells, cells):
        kern = lax.dynamic_slice_in_dim(kern[:, rows:], core * half, half, 0)
        right = (kern.astype(F32) * half_v[:, None, :] * u_cells[None, :, None]).astype(BF16)
        return lax.dot_general(right, cells, (((1,), (0,)), ((), ())), preferred_element_type=F32)

    part = product(kerns, u[1], expr) + product(theirs, u[3], other_expr)
    piece = jnp.sum(exchange(part.reshape(others, -1, genes), CHIPS), axis=0)
    profiles = lax.all_gather(to_all(piece.astype(BF16), CHIPS), "c").reshape(ranks, width, genes)
    mixed = lax.dot_general(
        scaled, profiles, (((0, 2), (0, 1)), ((), ())), preferred_element_type=F32
    )
    predicted = (mixed / s_q[:, None]).astype(BF16)
    return (q_new, r_new, pick(weights, here) / cells_total, predicted)


def solution(mesh):
    named = Mesh(mesh.devices.reshape(4, 8, 2, 4), EVERY)
    block = P(CELLS, "x")
    return jax.shard_map(
        shards,
        mesh=named,
        in_specs=(
            P(CELLS, None),
            P(CELLS, None),
            block,
            block,
            P("x"),
            P(CELLS),
            P(CELLS),
            block,
        ),
        out_specs=(block, block, P("x"), block),
        check_vma=False,
    )
```

```python
import jax
import jax.numpy as jnp
from jax import lax
from jax.experimental import pallas as pl
from jax.experimental.pallas import tpu as pltpu
from jax.sharding import Mesh
from jax.sharding import PartitionSpec as P

PASSES = 10
SCALE = 0.0625
GAMMA = 10.0
POWER = 0.8

CHIPS = ("y", "z")
CELLS = ("y", "z", "c")
EVERY = ("y", "z", "c", "x")
F32 = jnp.float32
BF16 = jnp.bfloat16


def contract_rows(left, right):
    return lax.dot_general(
        left, right, (((0,), (0,)), ((), ())), preferred_element_type=F32
    )


def exchange(chunks, axes):
    return lax.all_to_all(chunks, axes, 0, 0, tiled=False)


def to_all(value, axes):
    count = lax.axis_size(axes)
    return exchange(jnp.broadcast_to(value[None], (count,) + value.shape), axes)


def swap(value):
    return lax.ppermute(value, "c", [(0, 1), (1, 0)])


def pick(value, index):
    return lax.dynamic_index_in_dim(value, index, 0, keepdims=False)


def split3(value):
    high = lax.reduce_precision(value, 8, 7)
    rest = value - high
    middle = lax.reduce_precision(rest, 8, 7)
    low = lax.reduce_precision(rest - middle, 8, 7)
    return jnp.stack([high, middle, low]).astype(BF16)


def join3(rows):
    parts = rows.astype(F32)
    return parts[..., 0, :] + (parts[..., 1, :] + parts[..., 2, :])


def stack3(value):
    high = value.astype(BF16).astype(F32)
    rest = value - high
    middle = rest.astype(BF16).astype(F32)
    return jnp.concatenate([high, middle, rest - middle], axis=0).astype(BF16)


def sum_rows(value):
    return value[0:1] + (value[1:2] + value[2:3])


def in_lanes(blocks, first, count):
    return jnp.concatenate([blocks[first + i : first + i + 1] for i in range(count)], axis=1)


def in_rows(row, count):
    width = row.shape[1] // count
    return [row[:, i * width : (i + 1) * width] for i in range(count)]


def start_kernel(x_ref, y_ref, q_ref, r_ref, xq_ref, yr_ref, vec_ref):
    rows = []
    for emb_ref, factor_ref, cross_ref in ((x_ref, q_ref, xq_ref), (y_ref, r_ref, yr_ref)):
        factor = factor_ref[...]
        cross_ref[...] = contract_rows(emb_ref[...], factor.astype(BF16))
        norms = jnp.sum(jnp.square(emb_ref[...].astype(F32)), axis=1, keepdims=True)
        rows.append(jnp.sum(norms * factor, axis=0, keepdims=True))
        rows.append(jnp.sum(factor, axis=0, keepdims=True))
    vec_ref[...] = jnp.concatenate(rows, axis=0)


def chunk_kernel(got_ref, sent_ref, vec_ref):
    summed = jnp.sum(got_ref[...], axis=0)
    xq, yr = summed[0], summed[1]
    vec_ref[...] = summed[2]
    dot = jnp.sum(xq * yr, axis=0, keepdims=True)
    high = dot.astype(BF16).astype(F32)
    rest = dot - high
    middle = rest.astype(BF16).astype(F32)
    nothing = jnp.zeros((5, dot.shape[1]), F32)
    chunk = jnp.concatenate([xq, yr, high, middle, rest - middle, nothing], axis=0)
    sent_ref[...] = jnp.broadcast_to(chunk.astype(BF16)[None], sent_ref.shape)


def new_scalings(ranks, got_ref, v_ref, log_ref):
    t = jnp.sum(got_ref[...].astype(F32), axis=0)
    passed = jnp.log(v_ref[...] * t)
    weights = jnp.exp((log_ref[...] + passed[:ranks] + passed[ranks:]) / 3.0)
    return jnp.concatenate([weights, weights], axis=0) / t, weights


def send_columns(v, mass_ref, own_ref, other_ref, sent_ref, u_ref):
    ranks = own_ref.shape[0]
    rows = other_ref.shape[1] // 2

    def kern(member, side):
        kern_ref = (own_ref, other_ref)[member]
        blocks = [kern_ref[block, pl.ds(side * rows, rows), :] for block in range(ranks)]
        return jnp.concatenate(blocks, axis=1)

    v_rows = [stack3(in_lanes(v, side * ranks, ranks)) for side in range(2)]
    sums = []
    for member in range(2):
        for side in range(2):
            part = lax.dot_general(
                v_rows[side], kern(member, side), (((1,), (1,)), ((), ())),
                preferred_element_type=F32,
            )
            sums.append(sum_rows(part))
    u = jnp.exp(POWER * jnp.log(mass_ref[...] / jnp.concatenate(sums, axis=0)))
    u_ref[...] = u
    columns = []
    for side in range(2):
        total = None
        for member in range(2):
            row = 2 * member + side
            part = jnp.dot(
                stack3(u[row : row + 1]), kern(member, side), preferred_element_type=F32
            )
            total = part if total is None else total + part
        columns += in_rows(sum_rows(total), ranks)
    part = jnp.concatenate(columns, axis=0).astype(sent_ref.dtype)
    sent_ref[...] = jnp.broadcast_to(part[None], sent_ref.shape)


def first_pass(mass_ref, own_ref, other_ref, sent_ref, u_ref):
    ones = jnp.ones((2 * own_ref.shape[0], own_ref.shape[2]), F32)
    send_columns(ones, mass_ref, own_ref, other_ref, sent_ref, u_ref)


def next_pass(got_ref, v_ref, log_ref, mass_ref, own_ref, other_ref, sent_ref, u_ref, new_ref):
    v, _ = new_scalings(own_ref.shape[0], got_ref, v_ref, log_ref)
    new_ref[...] = v
    send_columns(v, mass_ref, own_ref, other_ref, sent_ref, u_ref)


def profile_kernel(
    core_ref, got_ref, v_ref, log_ref, u_ref, own_ref, other_ref, expr_ref, more_ref,
    part_ref, new_ref, weights_ref,
):
    ranks, _, width = own_ref.shape
    rows = other_ref.shape[1] // 2
    v, weights = new_scalings(ranks, got_ref, v_ref, log_ref)
    new_ref[...] = v
    weights_ref[...] = weights
    u_columns = jnp.concatenate([u_ref[...], u_ref[...]], axis=0).T
    half = ranks // 2
    for i in range(half):
        block = core_ref[0] * half + i
        scale = new_ref[pl.ds(ranks + block, 1), :]
        total = None
        for member, (kern_ref, cells_ref) in enumerate(((own_ref, expr_ref), (other_ref, more_ref))):
            kern = kern_ref[block, pl.ds(rows, rows), :].astype(F32)
            column = u_columns[:, 2 * member + 1 : 2 * member + 2]
            part = contract_rows((kern * scale * column).astype(BF16), cells_ref[...])
            total = part if total is None else total + part
        part_ref[pl.ds(i * width, width), :] = total


def on_chip(kernel, shapes, name, scalars=0, inputs=0):
    specs = {}
    if scalars:
        specs["in_specs"] = [pl.BlockSpec(memory_space=pltpu.SMEM)] * scalars + [
            pl.BlockSpec(memory_space=pltpu.VMEM)
        ] * inputs
    return pl.pallas_call(
        kernel,
        out_shape=tuple(jax.ShapeDtypeStruct(shape, dtype) for shape, dtype in shapes),
        **specs,
        compiler_params=pltpu.CompilerParams(vmem_limit_bytes=32 << 20),
        name=name,
    )


def shards(x_emb, y_emb, q_factor, r_factor, g_weights, a_mass, b_mass, expr):
    rows, width = q_factor.shape
    dim = x_emb.shape[1]
    genes = expr.shape[1]
    others = lax.axis_size(CHIPS)
    cell_devices = 2 * others
    ranks = lax.axis_size("x")
    cells_total = rows * cell_devices
    share = dim // cell_devices

    here = lax.axis_index("x")
    core = lax.axis_index("c")
    other_expr = swap(expr)
    masses = jnp.stack([a_mass, b_mass])
    masses = jnp.concatenate([masses, swap(masses)])
    norms_one = jnp.sum(jnp.square(x_emb.astype(F32)), axis=1)
    norms_two = jnp.sum(jnp.square(y_emb.astype(F32)), axis=1)
    part_xq, part_yr, part_vec = on_chip(
        start_kernel, (((dim, width), F32), ((dim, width), F32), ((4, width), F32)), "start"
    )(x_emb, y_emb, q_factor, r_factor)
    part_cross = jnp.concatenate(
        [part.reshape(2, others, share, width) for part in (part_xq, part_yr)], axis=2
    )

    def with_vec(cross):
        return jnp.concatenate(
            [cross, jnp.broadcast_to(part_vec[None], (others, 4, width))], axis=1
        ).reshape(others, (2 * share + 4) // 4, 4, width)

    outgoing = with_vec(pick(part_cross, core)) + swap(with_vec(pick(part_cross, 1 - core)))
    chunk_rows = 2 * share + 8
    sent, vec = on_chip(
        chunk_kernel, (((others, chunk_rows, width), BF16), ((4, width), F32)), "chunk"
    )(exchange(outgoing, CHIPS))
    xq_vec, cq_vec, yr_vec, cr_vec = (vec[i] for i in range(4))
    crosses = lax.all_gather(exchange(sent, CHIPS), "c").reshape(2 * others, chunk_rows, width)
    cross_xq = crosses[:, :share].reshape(dim, width)
    cross_yr = crosses[:, share : 2 * share].reshape(dim, width)
    cross_dot = jnp.sum(join3(crosses[:, 2 * share : 2 * share + 3]), axis=0)

    grad_q = (
        SCALE
        * (
            norms_one[:, None] * cr_vec[None, :]
            + yr_vec[None, :]
            - 2.0 * jnp.dot(x_emb, cross_yr, preferred_element_type=F32)
        )
        / g_weights[None, :]
    )
    grad_r = (
        SCALE
        * (
            norms_two[:, None] * cq_vec[None, :]
            + xq_vec[None, :]
            - 2.0 * jnp.dot(y_emb, cross_xq, preferred_element_type=F32)
        )
        / g_weights[None, :]
    )
    curvature = SCALE * (xq_vec * cr_vec + cq_vec * yr_vec - 2.0 * cross_dot)
    grad_g = -curvature / jnp.square(g_weights)
    local_peak = jnp.maximum(
        jnp.max(jnp.abs(grad_q), axis=0),
        jnp.maximum(jnp.max(jnp.abs(grad_r), axis=0), jnp.abs(grad_g)),
    )
    peak = jnp.max(to_all(local_peak[None], EVERY))
    eta = GAMMA / (peak + 1e-06)
    kern_q = q_factor * jnp.exp(-eta * grad_q)
    kern_r = r_factor * jnp.exp(-eta * grad_r)
    kern_g = g_weights * jnp.exp(-eta * grad_g)

    mine = to_all(
        jnp.concatenate([kern_q.astype(BF16), kern_r.astype(BF16), split3(kern_g)], axis=0), "x"
    )
    log_g = jnp.log(join3(mine[:, 2 * rows :]))
    mine_q = mine[:, :rows]
    kerns = mine[:, : 2 * rows]
    theirs = swap(kerns)
    sent_shape = ((others, 2 * ranks, width), BF16)
    u_shape = ((4, rows), F32)
    v_shape = ((2 * ranks, width), F32)
    sent, u = on_chip(first_pass, (sent_shape, u_shape), "first_pass")(masses, kerns, theirs)
    v = jnp.ones(v_shape[0], F32)
    for step in range(1, PASSES):
        sent, u, v = on_chip(next_pass, (sent_shape, u_shape, v_shape), "next_pass")(
            exchange(sent, CHIPS), v, log_g, masses, kerns, theirs
        )
    part, v, weights = on_chip(
        profile_kernel,
        (((ranks * width // 2, genes), F32), v_shape, ((ranks, width), F32)),
        "profile",
        scalars=1,
        inputs=8,
    )(
        core.astype(jnp.int32)[None], exchange(sent, CHIPS), v, log_g, u, kerns, theirs,
        expr, other_expr,
    )
    v_q, v_r = v[:ranks], v[ranks:]
    q_new = u[0][:, None] * kern_q * pick(v_q, here)[None, :]
    r_new = u[1][:, None] * kern_r * pick(v_r, here)[None, :]
    s_q = jnp.sum(mine_q.astype(F32) * v_q[:, None, :], axis=(0, 2))
    scaled = (mine_q.astype(F32) * (v_q / weights)[:, None, :]).astype(BF16)

    piece = jnp.sum(exchange(part.reshape(others, -1, genes), CHIPS), axis=0)
    profiles = lax.all_gather(to_all(piece.astype(BF16), CHIPS), "c").reshape(ranks, width, genes)
    mixed = lax.dot_general(
        scaled, profiles, (((0, 2), (0, 1)), ((), ())), preferred_element_type=F32
    )
    predicted = (mixed / s_q[:, None]).astype(BF16)
    return (q_new, r_new, pick(weights, here) / cells_total, predicted)


def solution(mesh):
    named = Mesh(mesh.devices.reshape(4, 8, 2, 4), EVERY)
    block = P(CELLS, "x")
    return jax.shard_map(
        shards,
        mesh=named,
        in_specs=(
            P(CELLS, None),
            P(CELLS, None),
            block,
            block,
            P("x"),
            P(CELLS),
            P(CELLS),
            block,
        ),
        out_specs=(block, block, P("x"), block),
        check_vma=False,
    )
```

```python
import jax
import jax.numpy as jnp
from jax import lax
from jax.experimental import pallas as pl
from jax.experimental.pallas import tpu as pltpu
from jax.sharding import Mesh
from jax.sharding import PartitionSpec as P

PASSES = 10
SCALE = 0.0625
GAMMA = 10.0
POWER = 0.8

CHIPS = ("y", "z")
CELLS = ("y", "z", "c")
EVERY = ("y", "z", "c", "x")
F32 = jnp.float32
BF16 = jnp.bfloat16


def contract_rows(left, right):
    return lax.dot_general(
        left, right, (((0,), (0,)), ((), ())), preferred_element_type=F32
    )


def exchange(chunks, axes):
    return lax.all_to_all(chunks, axes, 0, 0, tiled=False)


def to_all(value, axes):
    count = lax.axis_size(axes)
    return exchange(jnp.broadcast_to(value[None], (count,) + value.shape), axes)


def swap(value):
    return lax.ppermute(value, "c", [(0, 1), (1, 0)])


def pick(value, index):
    return lax.dynamic_index_in_dim(value, index, 0, keepdims=False)


def split3(value):
    high = lax.reduce_precision(value, 8, 7)
    rest = value - high
    middle = lax.reduce_precision(rest, 8, 7)
    low = lax.reduce_precision(rest - middle, 8, 7)
    return jnp.stack([high, middle, low]).astype(BF16)


def join3(rows):
    parts = rows.astype(F32)
    return parts[..., 0, :] + (parts[..., 1, :] + parts[..., 2, :])


def stack3(value):
    high = value.astype(BF16).astype(F32)
    rest = value - high
    middle = rest.astype(BF16).astype(F32)
    return jnp.concatenate([high, middle, rest - middle], axis=0).astype(BF16)


def sum_rows(value):
    return value[0:1] + (value[1:2] + value[2:3])


def in_lanes(blocks, first, count):
    return jnp.concatenate([blocks[first + i : first + i + 1] for i in range(count)], axis=1)


def in_rows(row, count):
    width = row.shape[1] // count
    return [row[:, i * width : (i + 1) * width] for i in range(count)]


def start_kernel(x_ref, y_ref, q_ref, r_ref, xq_ref, yr_ref, vec_ref):
    rows = []
    for emb_ref, factor_ref, cross_ref in ((x_ref, q_ref, xq_ref), (y_ref, r_ref, yr_ref)):
        factor = factor_ref[...]
        cross_ref[...] = contract_rows(emb_ref[...], factor.astype(BF16))
        norms = jnp.sum(jnp.square(emb_ref[...].astype(F32)), axis=1, keepdims=True)
        rows.append(jnp.sum(norms * factor, axis=0, keepdims=True))
        rows.append(jnp.sum(factor, axis=0, keepdims=True))
    vec_ref[...] = jnp.concatenate(rows, axis=0)


def chunk_kernel(got_ref, g_ref, sent_ref):
    summed = jnp.sum(got_ref[...], axis=0)
    xq, yr = summed[0], summed[1]
    dot = jnp.sum(xq * yr, axis=0, keepdims=True)
    nothing = jnp.zeros((2, dot.shape[1]), F32)
    chunk = jnp.concatenate([xq, yr, summed[2], dot, g_ref[...], nothing], axis=0)
    sent_ref[...] = jnp.broadcast_to(chunk[None], sent_ref.shape)


def spread_kernel(got_ref, sent_ref, vec_ref):
    every = jnp.concatenate([got_ref[i] for i in range(got_ref.shape[0])], axis=1)
    dot = every[12:13]
    high = dot.astype(BF16).astype(F32)
    rest = dot - high
    middle = rest.astype(BF16).astype(F32)
    nothing = jnp.zeros((5, dot.shape[1]), F32)
    chunk = jnp.concatenate([every[:8], high, middle, rest - middle, nothing], axis=0)
    sent_ref[...] = jnp.broadcast_to(chunk.astype(BF16)[None], sent_ref.shape)
    vec_ref[...] = every[8:16]


def grad_kernel(
    core_ref, x_ref, y_ref, mine_ref, other_ref, vec_ref, grad_q_ref, grad_r_ref, grad_g_ref, peak_ref
):
    half = x_ref.shape[1] // 2
    chunks = mine_ref.shape[0]
    core = core_ref[0]
    g = vec_ref[5:6]
    scale = SCALE / g
    place = lax.broadcasted_iota(jnp.int32, (half, chunks), 1)
    wanted = lax.broadcasted_iota(jnp.int32, (half, chunks), 0)
    wanted = (wanted // 4) * 16 + wanted % 4
    place8 = lax.broadcasted_iota(jnp.int32, (8, chunks), 1) % 16
    is_dot = jnp.where((place8 >= 8) & (place8 < 11), 1.0, 0.0).astype(BF16)
    spread = jnp.dot(is_dot, mine_ref[...], preferred_element_type=F32) + jnp.dot(
        is_dot, other_ref[...], preferred_element_type=F32
    )
    xq, cq, yr, cr = (vec_ref[i : i + 1] for i in range(4))
    curvature = SCALE * (xq * cr + cq * yr - 2.0 * spread[0:1])
    grad_g = -curvature / jnp.square(g)
    grad_g_ref[...] = grad_g
    top = jnp.abs(grad_g)
    for emb_ref, offset, count, total, out_ref in (
        (x_ref, 4, cr, yr, grad_q_ref),
        (y_ref, 0, cq, xq, grad_r_ref),
    ):
        select = jnp.where(place == wanted + offset, 1.0, 0.0).astype(BF16)
        product = None
        for position, cross_ref in ((core, mine_ref), (1 - core, other_ref)):
            rows = jnp.dot(select, cross_ref[...], preferred_element_type=F32).astype(BF16)
            emb = emb_ref[:, pl.ds(pl.multiple_of(position * half, half), half)]
            part = jnp.dot(emb, rows, preferred_element_type=F32)
            product = part if product is None else product + part
        norms = jnp.sum(jnp.square(emb_ref[...].astype(F32)), axis=1, keepdims=True)
        grad = scale * (norms * count + total - 2.0 * product)
        out_ref[...] = grad
        top = jnp.maximum(top, jnp.max(jnp.abs(grad), axis=0, keepdims=True))
    blocks = in_rows(top, top.shape[1] // peak_ref.shape[2])
    peak = blocks[0]
    for block in blocks[1:]:
        peak = jnp.maximum(peak, block)
    peak_ref[...] = jnp.broadcast_to(peak[None], peak_ref.shape)


def kern_kernel(
    here_ref, peak_ref, grad_q_ref, grad_r_ref, grad_g_ref, vec_ref, all_ref, q_ref, r_ref,
    kern_ref, own_q_ref, own_r_ref, log_ref,
):
    ranks = all_ref.shape[0]
    rows, width = q_ref.shape
    peak = jnp.max(jnp.max(peak_ref[...], axis=0), axis=1, keepdims=True)
    eta = GAMMA / (peak + 1e-06)
    kern_g = vec_ref[5:6] * jnp.exp(-eta * grad_g_ref[...])
    log_ref[...] = jnp.concatenate(in_rows(jnp.log(kern_g), ranks), axis=0)
    mine = pl.ds(pl.multiple_of(here_ref[0] * width, width), width)
    for side, (grad_ref, factor_ref, own_ref) in enumerate(
        ((grad_q_ref, q_ref, own_q_ref), (grad_r_ref, r_ref, own_r_ref))
    ):
        own_ref[...] = factor_ref[...] * jnp.exp(-eta * grad_ref[:, mine])
        for block in range(ranks):
            lanes = pl.ds(block * width, width)
            kern = all_ref[block, side].astype(F32) * jnp.exp(-eta * grad_ref[:, lanes])
            kern_ref[pl.ds(side * rows, rows), lanes] = kern.astype(BF16)


def new_scalings(ranks, got_ref, v_ref, log_ref):
    t = jnp.sum(got_ref[...].astype(F32), axis=0)
    passed = jnp.log(v_ref[...] * t)
    weights = jnp.exp((log_ref[...] + passed[:ranks] + passed[ranks:]) / 3.0)
    return jnp.concatenate([weights, weights], axis=0) / t, weights


def send_columns(v, mass_ref, own_ref, other_ref, sent_ref, u_ref):
    ranks = v.shape[0] // 2
    rows = own_ref.shape[0] // 2

    def kern(member, side):
        return (own_ref, other_ref)[member][pl.ds(side * rows, rows), :]

    v_rows = [stack3(in_lanes(v, side * ranks, ranks)) for side in range(2)]
    sums = []
    for member in range(2):
        for side in range(2):
            part = lax.dot_general(
                v_rows[side], kern(member, side), (((1,), (1,)), ((), ())),
                preferred_element_type=F32,
            )
            sums.append(sum_rows(part))
    u = jnp.exp(POWER * jnp.log(mass_ref[...] / jnp.concatenate(sums, axis=0)))
    u_ref[...] = u
    columns = []
    for side in range(2):
        total = None
        for member in range(2):
            row = 2 * member + side
            part = jnp.dot(
                stack3(u[row : row + 1]), kern(member, side), preferred_element_type=F32
            )
            total = part if total is None else total + part
        columns += in_rows(sum_rows(total), ranks)
    part = jnp.concatenate(columns, axis=0).astype(sent_ref.dtype)
    sent_ref[...] = jnp.broadcast_to(part[None], sent_ref.shape)


def first_pass(mass_ref, own_ref, other_ref, sent_ref, u_ref):
    ones = jnp.ones(sent_ref.shape[1:], F32)
    send_columns(ones, mass_ref, own_ref, other_ref, sent_ref, u_ref)


def next_pass(got_ref, v_ref, log_ref, mass_ref, own_ref, other_ref, sent_ref, u_ref, new_ref):
    v, _ = new_scalings(log_ref.shape[0], got_ref, v_ref, log_ref)
    new_ref[...] = v
    send_columns(v, mass_ref, own_ref, other_ref, sent_ref, u_ref)


def profile_kernel(
    core_ref, got_ref, v_ref, log_ref, u_ref, own_ref, other_ref, expr_ref, more_ref,
    part_ref, new_ref, weights_ref,
):
    ranks = log_ref.shape[0]
    rows = own_ref.shape[0] // 2
    half = own_ref.shape[1] // 2
    v, weights = new_scalings(ranks, got_ref, v_ref, log_ref)
    new_ref[...] = v
    weights_ref[...] = weights
    u_columns = jnp.concatenate([u_ref[...], u_ref[...]], axis=0).T
    core = core_ref[0]
    blocks = [new_ref[pl.ds(ranks + core * (ranks // 2) + i, 1), :] for i in range(ranks // 2)]
    scale = jnp.concatenate(blocks, axis=1)
    lanes = pl.ds(pl.multiple_of(core * half, half), half)
    total = None
    for member, (kern_ref, cells_ref) in enumerate(((own_ref, expr_ref), (other_ref, more_ref))):
        kern = kern_ref[pl.ds(rows, rows), lanes].astype(F32)
        column = u_columns[:, 2 * member + 1 : 2 * member + 2]
        part = contract_rows((kern * scale * column).astype(BF16), cells_ref[...])
        total = part if total is None else total + part
    part_ref[...] = total


def on_chip(kernel, shapes, name, scalars=0, inputs=0):
    specs = {}
    if scalars:
        specs["in_specs"] = [pl.BlockSpec(memory_space=pltpu.SMEM)] * scalars + [
            pl.BlockSpec(memory_space=pltpu.VMEM)
        ] * inputs
    return pl.pallas_call(
        kernel,
        out_shape=tuple(jax.ShapeDtypeStruct(shape, dtype) for shape, dtype in shapes),
        **specs,
        compiler_params=pltpu.CompilerParams(vmem_limit_bytes=32 << 20),
        name=name,
    )


def shards(x_emb, y_emb, q_factor, r_factor, g_weights, a_mass, b_mass, expr):
    rows, width = q_factor.shape
    dim = x_emb.shape[1]
    genes = expr.shape[1]
    others = lax.axis_size(CHIPS)
    cell_devices = 2 * others
    ranks = lax.axis_size("x")
    cells_total = rows * cell_devices
    share = dim // cell_devices

    here = lax.axis_index("x")
    core = lax.axis_index("c")
    other_expr = swap(expr)
    masses = jnp.stack([a_mass, b_mass])
    masses = jnp.concatenate([masses, swap(masses)])
    core_index = core.astype(jnp.int32)[None]
    every = lax.all_gather(jnp.stack([q_factor, r_factor]).astype(BF16), "x")
    part_xq, part_yr, part_vec = on_chip(
        start_kernel, (((dim, width), F32), ((dim, width), F32), ((4, width), F32)), "start"
    )(x_emb, y_emb, q_factor, r_factor)
    part_cross = jnp.concatenate(
        [part.reshape(2, others, share, width) for part in (part_xq, part_yr)], axis=2
    )

    def with_vec(cross):
        return jnp.concatenate(
            [cross, jnp.broadcast_to(part_vec[None], (others, 4, width))], axis=1
        ).reshape(others, (2 * share + 4) // 4, 4, width)

    outgoing = with_vec(pick(part_cross, core)) + swap(with_vec(pick(part_cross, 1 - core)))
    columns = ranks * width
    tall = ((rows, columns), F32)
    sent = on_chip(chunk_kernel, (((ranks, 16, width), F32),), "chunk")(
        exchange(outgoing, CHIPS), g_weights[None]
    )[0]
    sent, vec = on_chip(
        spread_kernel, (((others, 16, columns), BF16), ((8, columns), F32)), "spread"
    )(exchange(sent, "x"))
    crosses = exchange(sent, CHIPS).reshape(others * 16, columns)
    grad_q, grad_r, grad_g, peak = on_chip(
        grad_kernel,
        (tall, tall, ((1, columns), F32), ((cell_devices, 1, width), F32)),
        "grad",
        scalars=1,
        inputs=5,
    )(core_index, x_emb, y_emb, crosses, swap(crosses), vec)
    kerns, kern_q, kern_r, log_g = on_chip(
        kern_kernel,
        (((2 * rows, columns), BF16), ((rows, width), F32), ((rows, width), F32), ((ranks, width), F32)),
        "kern",
        scalars=1,
        inputs=8,
    )(
        here.astype(jnp.int32)[None], exchange(peak, CELLS), grad_q, grad_r, grad_g, vec,
        every, q_factor, r_factor,
    )
    theirs = swap(kerns)
    sent_shape = ((others, 2 * ranks, width), BF16)
    u_shape = ((4, rows), F32)
    v_shape = ((2 * ranks, width), F32)
    sent, u = on_chip(first_pass, (sent_shape, u_shape), "first_pass")(masses, kerns, theirs)
    v = jnp.ones(v_shape[0], F32)
    for step in range(1, PASSES):
        sent, u, v = on_chip(next_pass, (sent_shape, u_shape, v_shape), "next_pass")(
            exchange(sent, CHIPS), v, log_g, masses, kerns, theirs
        )
    part, v, weights = on_chip(
        profile_kernel,
        (((ranks * width // 2, genes), F32), v_shape, ((ranks, width), F32)),
        "profile",
        scalars=1,
        inputs=8,
    )(
        core_index, exchange(sent, CHIPS), v, log_g, u, kerns, theirs,
        expr, other_expr,
    )
    v_q, v_r = v[:ranks], v[ranks:]
    q_new = u[0][:, None] * kern_q * pick(v_q, here)[None, :]
    r_new = u[1][:, None] * kern_r * pick(v_r, here)[None, :]
    mine_q = kerns[:rows].astype(F32)
    s_q = jnp.sum(mine_q * v_q.reshape(1, columns), axis=1)
    scaled = (mine_q * (v_q / weights).reshape(1, columns)).astype(BF16)

    piece = jnp.sum(exchange(part.reshape(others, -1, genes), CHIPS), axis=0)
    profiles = lax.all_gather(to_all(piece.astype(BF16), CHIPS), "c").reshape(columns, genes)
    mixed = jnp.dot(scaled, profiles, preferred_element_type=F32)
    predicted = (mixed / s_q[:, None]).astype(BF16)
    return (q_new, r_new, pick(weights, here) / cells_total, predicted)


def solution(mesh):
    named = Mesh(mesh.devices.reshape(4, 8, 2, 4), EVERY)
    block = P(CELLS, "x")
    return jax.shard_map(
        shards,
        mesh=named,
        in_specs=(
            P(CELLS, None),
            P(CELLS, None),
            block,
            block,
            P("x"),
            P(CELLS),
            P(CELLS),
            block,
        ),
        out_specs=(block, block, P("x"), block),
        check_vma=False,
    )
```

```python
import jax
import jax.numpy as jnp
from jax import lax
from jax.experimental import pallas as pl
from jax.experimental.pallas import tpu as pltpu
from jax.sharding import Mesh
from jax.sharding import PartitionSpec as P

PASSES = 10
SCALE = 0.0625
GAMMA = 10.0
POWER = 0.8
LIMIT = 12 << 20

CHIPS = ("y", "z")
CELLS = ("y", "z", "c")
EVERY = ("y", "z", "c", "x")
F32 = jnp.float32
BF16 = jnp.bfloat16


def contract_rows(left, right):
    return lax.dot_general(
        left, right, (((0,), (0,)), ((), ())), preferred_element_type=F32
    )


def exchange(chunks, axes):
    return lax.all_to_all(chunks, axes, 0, 0, tiled=False)


def to_all(value, axes):
    count = lax.axis_size(axes)
    return exchange(jnp.broadcast_to(value[None], (count,) + value.shape), axes)


def swap(value):
    return lax.ppermute(value, "c", [(0, 1), (1, 0)])


def pick(value, index):
    return lax.dynamic_index_in_dim(value, index, 0, keepdims=False)


def split3(value):
    high = lax.reduce_precision(value, 8, 7)
    rest = value - high
    middle = lax.reduce_precision(rest, 8, 7)
    low = lax.reduce_precision(rest - middle, 8, 7)
    return jnp.stack([high, middle, low]).astype(BF16)


def join3(rows):
    parts = rows.astype(F32)
    return parts[..., 0, :] + (parts[..., 1, :] + parts[..., 2, :])


def stack3(value):
    high = value.astype(BF16).astype(F32)
    rest = value - high
    middle = rest.astype(BF16).astype(F32)
    return jnp.concatenate([high, middle, rest - middle], axis=0).astype(BF16)


def sum_rows(value):
    return value[0:1] + (value[1:2] + value[2:3])


def in_lanes(blocks, first, count):
    return jnp.concatenate([blocks[first + i : first + i + 1] for i in range(count)], axis=1)


def in_rows(row, count):
    width = row.shape[1] // count
    return [row[:, i * width : (i + 1) * width] for i in range(count)]


def start_kernel(
    x_hbm, y_hbm, q_hbm, r_hbm, xq_ref, yr_ref, vec_ref, cast_ref, x_ref, y_ref, q_ref, r_ref, sems
):
    pieces = sems.shape[1]
    copies = []
    for i, (source, target) in enumerate(
        ((x_hbm, x_ref), (q_hbm, q_ref), (y_hbm, y_ref), (r_hbm, r_ref))
    ):
        size = source.shape[0] // pieces
        for k in range(pieces):
            part = pl.ds(k * size, size)
            copies.append(pltpu.make_async_copy(source.at[part], target.at[part], sems.at[i, k]))
    for copy in copies:
        copy.start()
    rows = []
    for side, (emb_ref, factor_ref, cross_ref) in enumerate(
        ((x_ref, q_ref, xq_ref), (y_ref, r_ref, yr_ref))
    ):
        for copy in copies[2 * side * pieces : 2 * (side + 1) * pieces]:
            copy.wait()
        factor = factor_ref[...]
        rounded = factor.astype(BF16)
        cast_ref[side] = rounded
        cross_ref[...] = contract_rows(emb_ref[...], rounded)
        norms = jnp.sum(jnp.square(emb_ref[...].astype(F32)), axis=1, keepdims=True)
        rows.append(jnp.sum(norms * factor, axis=0, keepdims=True))
        rows.append(jnp.sum(factor, axis=0, keepdims=True))
    vec_ref[...] = jnp.concatenate(rows, axis=0)


def chunk_kernel(got_ref, g_ref, sent_ref):
    summed = jnp.sum(got_ref[...], axis=0)
    xq, yr = summed[0], summed[1]
    dot = jnp.sum(xq * yr, axis=0, keepdims=True)
    nothing = jnp.zeros((2, dot.shape[1]), F32)
    chunk = jnp.concatenate([xq, yr, summed[2], dot, g_ref[...], nothing], axis=0)
    sent_ref[...] = jnp.broadcast_to(chunk[None], sent_ref.shape)


def spread_kernel(got_ref, sent_ref, vec_ref):
    every = jnp.concatenate([got_ref[i] for i in range(got_ref.shape[0])], axis=1)
    dot = every[12:13]
    high = dot.astype(BF16).astype(F32)
    rest = dot - high
    middle = rest.astype(BF16).astype(F32)
    nothing = jnp.zeros((5, dot.shape[1]), F32)
    chunk = jnp.concatenate([every[:8], high, middle, rest - middle, nothing], axis=0)
    sent_ref[...] = jnp.broadcast_to(chunk.astype(BF16)[None], sent_ref.shape)
    vec_ref[...] = every[8:16]


def grad_kernel(
    core_ref, x_ref, y_ref, mine_ref, other_ref, vec_ref, grad_q_ref, grad_r_ref, grad_g_ref, peak_ref
):
    half = x_ref.shape[1] // 2
    chunks = mine_ref.shape[0]
    core = core_ref[0]
    g = vec_ref[5:6]
    scale = SCALE / g
    place = lax.broadcasted_iota(jnp.int32, (half, chunks), 1)
    wanted = lax.broadcasted_iota(jnp.int32, (half, chunks), 0)
    wanted = (wanted // 4) * 16 + wanted % 4
    place8 = lax.broadcasted_iota(jnp.int32, (8, chunks), 1) % 16
    is_dot = jnp.where((place8 >= 8) & (place8 < 11), 1.0, 0.0).astype(BF16)
    spread = jnp.dot(is_dot, mine_ref[...], preferred_element_type=F32) + jnp.dot(
        is_dot, other_ref[...], preferred_element_type=F32
    )
    xq, cq, yr, cr = (vec_ref[i : i + 1] for i in range(4))
    curvature = SCALE * (xq * cr + cq * yr - 2.0 * spread[0:1])
    grad_g = -curvature / jnp.square(g)
    grad_g_ref[...] = grad_g
    top = jnp.abs(grad_g)
    for emb_ref, offset, count, total, out_ref in (
        (x_ref, 4, cr, yr, grad_q_ref),
        (y_ref, 0, cq, xq, grad_r_ref),
    ):
        select = jnp.where(place == wanted + offset, 1.0, 0.0).astype(BF16)
        product = None
        for position, cross_ref in ((core, mine_ref), (1 - core, other_ref)):
            rows = jnp.dot(select, cross_ref[...], preferred_element_type=F32).astype(BF16)
            emb = emb_ref[:, pl.ds(pl.multiple_of(position * half, half), half)]
            part = jnp.dot(emb, rows, preferred_element_type=F32)
            product = part if product is None else product + part
        norms = jnp.sum(jnp.square(emb_ref[...].astype(F32)), axis=1, keepdims=True)
        grad = scale * (norms * count + total - 2.0 * product)
        out_ref[...] = grad
        top = jnp.maximum(top, jnp.max(jnp.abs(grad), axis=0, keepdims=True))
    blocks = in_rows(top, top.shape[1] // peak_ref.shape[2])
    peak = blocks[0]
    for block in blocks[1:]:
        peak = jnp.maximum(peak, block)
    peak_ref[...] = jnp.broadcast_to(peak[None], peak_ref.shape)


def kern_kernel(
    here_ref, peak_ref, grad_q_ref, grad_r_ref, grad_g_ref, vec_ref, q_ref, r_ref, *refs
):
    from_others, (kern_ref, own_q_ref, own_r_ref, log_ref) = refs[:-4], refs[-4:]
    ranks = len(from_others) + 1
    rows, width = q_ref.shape
    peak = jnp.max(jnp.max(peak_ref[...], axis=0), axis=1, keepdims=True)
    eta = GAMMA / (peak + 1e-06)
    kern_g = vec_ref[5:6] * jnp.exp(-eta * grad_g_ref[...])
    log_ref[...] = jnp.concatenate(in_rows(jnp.log(kern_g), ranks), axis=0)
    for shift in range(ranks):
        block = lax.rem(here_ref[0] + ranks - shift, ranks)
        lanes = pl.ds(pl.multiple_of(block * width, width), width)
        for side, (grad_ref, factor_ref, own_ref) in enumerate(
            ((grad_q_ref, q_ref, own_q_ref), (grad_r_ref, r_ref, own_r_ref))
        ):
            factor = from_others[shift - 1][side].astype(F32) if shift else factor_ref[...]
            kern = factor * jnp.exp(-eta * grad_ref[:, lanes])
            if shift == 0:
                own_ref[...] = kern
            kern_ref[pl.ds(side * rows, rows), lanes] = kern.astype(BF16)


def new_scalings(ranks, got_ref, v_ref, log_ref):
    t = jnp.sum(got_ref[...].astype(F32), axis=0)
    passed = jnp.log(v_ref[...] * t)
    weights = jnp.exp((log_ref[...] + passed[:ranks] + passed[ranks:]) / 3.0)
    return jnp.concatenate([weights, weights], axis=0) / t, weights


def send_columns(v, mass_ref, own_ref, other_ref, sent_ref, u_ref):
    ranks = v.shape[0] // 2
    rows = own_ref.shape[0] // 2

    def kern(member, side):
        return (own_ref, other_ref)[member][pl.ds(side * rows, rows), :]

    v_rows = [stack3(in_lanes(v, side * ranks, ranks)) for side in range(2)]
    sums = []
    for member in range(2):
        for side in range(2):
            part = lax.dot_general(
                v_rows[side], kern(member, side), (((1,), (1,)), ((), ())),
                preferred_element_type=F32,
            )
            sums.append(sum_rows(part))
    u = jnp.exp(POWER * jnp.log(mass_ref[...] / jnp.concatenate(sums, axis=0)))
    u_ref[...] = u
    columns = []
    for side in range(2):
        total = None
        for member in range(2):
            row = 2 * member + side
            part = jnp.dot(
                stack3(u[row : row + 1]), kern(member, side), preferred_element_type=F32
            )
            total = part if total is None else total + part
        columns += in_rows(sum_rows(total), ranks)
    part = jnp.concatenate(columns, axis=0).astype(sent_ref.dtype)
    sent_ref[...] = jnp.broadcast_to(part[None], sent_ref.shape)


def first_pass(mass_ref, own_ref, other_ref, sent_ref, u_ref):
    ones = jnp.ones(sent_ref.shape[1:], F32)
    send_columns(ones, mass_ref, own_ref, other_ref, sent_ref, u_ref)


def next_pass(got_ref, v_ref, log_ref, mass_ref, own_ref, other_ref, sent_ref, u_ref, new_ref):
    v, _ = new_scalings(log_ref.shape[0], got_ref, v_ref, log_ref)
    new_ref[...] = v
    send_columns(v, mass_ref, own_ref, other_ref, sent_ref, u_ref)


def profile_kernel(
    core_ref, got_ref, v_ref, log_ref, u_ref, own_ref, other_ref, expr_ref, more_ref,
    part_ref, new_ref, weights_ref,
):
    ranks = log_ref.shape[0]
    rows = own_ref.shape[0] // 2
    half = own_ref.shape[1] // 2
    v, weights = new_scalings(ranks, got_ref, v_ref, log_ref)
    new_ref[...] = v
    weights_ref[...] = weights
    u_columns = jnp.concatenate([u_ref[...], u_ref[...]], axis=0).T
    core = core_ref[0]
    blocks = [new_ref[pl.ds(ranks + core * (ranks // 2) + i, 1), :] for i in range(ranks // 2)]
    scale = jnp.concatenate(blocks, axis=1)
    lanes = pl.ds(pl.multiple_of(core * half, half), half)
    total = None
    for member, (kern_ref, cells_ref) in enumerate(((own_ref, expr_ref), (other_ref, more_ref))):
        kern = kern_ref[pl.ds(rows, rows), lanes].astype(F32)
        column = u_columns[:, 2 * member + 1 : 2 * member + 2]
        part = contract_rows((kern * scale * column).astype(BF16), cells_ref[...])
        total = part if total is None else total + part
    part_ref[...] = total


def on_chip(kernel, shapes, name, scalars=0, inputs=0, off_chip=0, scratch=(), limit=LIMIT):
    specs = {}
    if scalars:
        specs["in_specs"] = [pl.BlockSpec(memory_space=pltpu.SMEM)] * scalars + [
            pl.BlockSpec(memory_space=pltpu.VMEM)
        ] * inputs
    if off_chip:
        specs["in_specs"] = [pl.BlockSpec(memory_space=pltpu.HBM)] * off_chip
    return pl.pallas_call(
        kernel,
        out_shape=tuple(jax.ShapeDtypeStruct(shape, dtype) for shape, dtype in shapes),
        scratch_shapes=scratch,
        **specs,
        compiler_params=pltpu.CompilerParams(vmem_limit_bytes=limit),
        name=name,
    )


def shards(x_emb, y_emb, q_factor, r_factor, g_weights, a_mass, b_mass, expr):
    rows, width = q_factor.shape
    dim = x_emb.shape[1]
    genes = expr.shape[1]
    others = lax.axis_size(CHIPS)
    cell_devices = 2 * others
    ranks = lax.axis_size("x")
    cells_total = rows * cell_devices
    share = dim // cell_devices

    here = lax.axis_index("x")
    core = lax.axis_index("c")
    other_expr = swap(expr)
    masses = jnp.stack([a_mass, b_mass])
    masses = jnp.concatenate([masses, swap(masses)])
    core_index = core.astype(jnp.int32)[None]
    part_xq, part_yr, part_vec, rounded = on_chip(
        start_kernel,
        (
            ((dim, width), F32),
            ((dim, width), F32),
            ((4, width), F32),
            ((2, rows, width), BF16),
        ),
        "start",
        off_chip=4,
        limit=60 << 20,
        scratch=[
            pltpu.VMEM(x_emb.shape, BF16),
            pltpu.VMEM(y_emb.shape, BF16),
            pltpu.VMEM(q_factor.shape, F32),
            pltpu.VMEM(r_factor.shape, F32),
            pltpu.SemaphoreType.DMA((4, 2)),
        ],
    )(x_emb, y_emb, q_factor, r_factor)
    from_others = [
        lax.ppermute(rounded, "x", [(i, (i + shift) % ranks) for i in range(ranks)])
        for shift in range(1, ranks)
    ]
    part_cross = jnp.concatenate(
        [part.reshape(2, others, share, width) for part in (part_xq, part_yr)], axis=2
    )

    def with_vec(cross):
        return jnp.concatenate(
            [cross, jnp.broadcast_to(part_vec[None], (others, 4, width))], axis=1
        ).reshape(others, (2 * share + 4) // 4, 4, width)

    outgoing = with_vec(pick(part_cross, core)) + swap(with_vec(pick(part_cross, 1 - core)))
    columns = ranks * width
    tall = ((rows, columns), F32)
    sent = on_chip(chunk_kernel, (((ranks, 16, width), F32),), "chunk")(
        exchange(outgoing, CHIPS), g_weights[None]
    )[0]
    sent, vec = on_chip(
        spread_kernel, (((others, 16, columns), BF16), ((8, columns), F32)), "spread"
    )(exchange(sent, "x"))
    crosses = exchange(sent, CHIPS).reshape(others * 16, columns)
    grad_q, grad_r, grad_g, peak = on_chip(
        grad_kernel,
        (tall, tall, ((1, columns), F32), ((cell_devices, 1, width), F32)),
        "grad",
        scalars=1,
        inputs=5,
    )(core_index, x_emb, y_emb, crosses, swap(crosses), vec)
    kerns, kern_q, kern_r, log_g = on_chip(
        kern_kernel,
        (((2 * rows, columns), BF16), ((rows, width), F32), ((rows, width), F32), ((ranks, width), F32)),
        "kern",
        scalars=1,
        inputs=7 + ranks - 1,
    )(
        here.astype(jnp.int32)[None], exchange(peak, CELLS), grad_q, grad_r, grad_g, vec,
        q_factor, r_factor, *from_others,
    )
    theirs = swap(kerns)
    sent_shape = ((others, 2 * ranks, width), BF16)
    u_shape = ((4, rows), F32)
    v_shape = ((2 * ranks, width), F32)
    sent, u = on_chip(first_pass, (sent_shape, u_shape), "first_pass")(masses, kerns, theirs)
    v = jnp.ones(v_shape[0], F32)
    for step in range(1, PASSES):
        sent, u, v = on_chip(next_pass, (sent_shape, u_shape, v_shape), "next_pass")(
            exchange(sent, CHIPS), v, log_g, masses, kerns, theirs
        )
    part, v, weights = on_chip(
        profile_kernel,
        (((ranks * width // 2, genes), F32), v_shape, ((ranks, width), F32)),
        "profile",
        scalars=1,
        inputs=8,
    )(
        core_index, exchange(sent, CHIPS), v, log_g, u, kerns, theirs,
        expr, other_expr,
    )
    v_q, v_r = v[:ranks], v[ranks:]
    q_new = u[0][:, None] * kern_q * pick(v_q, here)[None, :]
    r_new = u[1][:, None] * kern_r * pick(v_r, here)[None, :]
    mine_q = kerns[:rows].astype(F32)
    s_q = jnp.sum(mine_q * v_q.reshape(1, columns), axis=1)
    scaled = (mine_q * (v_q / weights).reshape(1, columns)).astype(BF16)

    piece = jnp.sum(exchange(part.reshape(others, -1, genes), CHIPS), axis=0)
    profiles = lax.all_gather(to_all(piece.astype(BF16), CHIPS), "c").reshape(columns, genes)
    mixed = jnp.dot(scaled, profiles, preferred_element_type=F32)
    predicted = (mixed / s_q[:, None]).astype(BF16)
    return (q_new, r_new, pick(weights, here) / cells_total, predicted)


def solution(mesh):
    named = Mesh(mesh.devices.reshape(4, 8, 2, 4), EVERY)
    block = P(CELLS, "x")
    return jax.shard_map(
        shards,
        mesh=named,
        in_specs=(
            P(CELLS, None),
            P(CELLS, None),
            block,
            block,
            P("x"),
            P(CELLS),
            P(CELLS),
            block,
        ),
        out_specs=(block, block, P("x"), block),
        check_vma=False,
    )
```

```python
import jax
import jax.numpy as jnp
from jax import lax
from jax.experimental import pallas as pl
from jax.experimental.pallas import tpu as pltpu
from jax.sharding import Mesh
from jax.sharding import PartitionSpec as P

PASSES = 10
SCALE = 0.0625
GAMMA = 10.0
POWER = 0.8
LIMIT = 12 << 20

CHIPS = ("y", "z")
CELLS = ("y", "z", "c")
EVERY = ("y", "z", "c", "x")
F32 = jnp.float32
BF16 = jnp.bfloat16


def contract_rows(left, right):
    return lax.dot_general(
        left, right, (((0,), (0,)), ((), ())), preferred_element_type=F32
    )


def exchange(chunks, axes):
    return lax.all_to_all(chunks, axes, 0, 0, tiled=False)


def to_all(value, axes):
    count = lax.axis_size(axes)
    return exchange(jnp.broadcast_to(value[None], (count,) + value.shape), axes)


def swap(value):
    return lax.ppermute(value, "c", [(0, 1), (1, 0)])


def pick(value, index):
    return lax.dynamic_index_in_dim(value, index, 0, keepdims=False)


def split3(value):
    high = lax.reduce_precision(value, 8, 7)
    rest = value - high
    middle = lax.reduce_precision(rest, 8, 7)
    low = lax.reduce_precision(rest - middle, 8, 7)
    return jnp.stack([high, middle, low]).astype(BF16)


def join3(rows):
    parts = rows.astype(F32)
    return parts[..., 0, :] + (parts[..., 1, :] + parts[..., 2, :])


def stack3(value):
    high = value.astype(BF16).astype(F32)
    rest = value - high
    middle = rest.astype(BF16).astype(F32)
    return jnp.concatenate([high, middle, rest - middle], axis=0).astype(BF16)


def sum_rows(value):
    return value[0:1] + (value[1:2] + value[2:3])


def in_lanes(blocks, first, count):
    return jnp.concatenate([blocks[first + i : first + i + 1] for i in range(count)], axis=1)


def in_rows(row, count):
    width = row.shape[1] // count
    return [row[:, i * width : (i + 1) * width] for i in range(count)]


def start_kernel(
    x_hbm, y_hbm, q_hbm, r_hbm, xq_ref, yr_ref, vec_ref, cast_ref, x_ref, y_ref, q_ref, r_ref, sems
):
    pieces = sems.shape[1]
    copies = []
    for i, (source, target) in enumerate(
        ((x_hbm, x_ref), (q_hbm, q_ref), (y_hbm, y_ref), (r_hbm, r_ref))
    ):
        size = source.shape[0] // pieces
        for k in range(pieces):
            part = pl.ds(k * size, size)
            copies.append(pltpu.make_async_copy(source.at[part], target.at[part], sems.at[i, k]))
    for copy in copies:
        copy.start()
    rows = []
    for side, (emb_ref, factor_ref, cross_ref) in enumerate(
        ((x_ref, q_ref, xq_ref), (y_ref, r_ref, yr_ref))
    ):
        for copy in copies[2 * side * pieces : 2 * (side + 1) * pieces]:
            copy.wait()
        factor = factor_ref[...]
        rounded = factor.astype(BF16)
        cast_ref[side] = rounded
        cross_ref[...] = contract_rows(emb_ref[...], rounded)
        norms = jnp.sum(jnp.square(emb_ref[...].astype(F32)), axis=1, keepdims=True)
        rows.append(jnp.sum(norms * factor, axis=0, keepdims=True))
        rows.append(jnp.sum(factor, axis=0, keepdims=True))
    vec_ref[...] = jnp.concatenate(rows, axis=0)


def chunk_kernel(got_ref, g_ref, sent_ref):
    summed = jnp.sum(got_ref[...], axis=0)
    xq, yr = summed[0], summed[1]
    dot = jnp.sum(xq * yr, axis=0, keepdims=True)
    nothing = jnp.zeros((2, dot.shape[1]), F32)
    chunk = jnp.concatenate([xq, yr, summed[2], dot, g_ref[...], nothing], axis=0)
    sent_ref[...] = jnp.broadcast_to(chunk[None], sent_ref.shape)


def spread_kernel(got_ref, sent_ref, vec_ref):
    every = jnp.concatenate([got_ref[i] for i in range(got_ref.shape[0])], axis=1)
    dot = every[12:13]
    high = dot.astype(BF16).astype(F32)
    rest = dot - high
    middle = rest.astype(BF16).astype(F32)
    nothing = jnp.zeros((5, dot.shape[1]), F32)
    chunk = jnp.concatenate([every[:8], high, middle, rest - middle, nothing], axis=0)
    sent_ref[...] = jnp.broadcast_to(chunk.astype(BF16)[None], sent_ref.shape)
    vec_ref[...] = every[8:16]


def grad_kernel(
    core_ref, here_ref, x_ref, y_ref, mine_ref, other_ref, vec_ref, mass_ref, mass2_ref, *refs
):
    factors = refs[:-8]
    grad_q_ref, grad_r_ref, grad_g_ref, peak_ref, all_ref, own_q_ref, own_r_ref, masses_ref = refs[-8:]
    masses_ref[...] = jnp.concatenate([mass_ref[...], mass2_ref[...]], axis=0)
    ranks = len(factors)
    rows, width = factors[0].shape[1:]

    def lanes_of(block):
        return pl.ds(pl.multiple_of(block * width, width), width)

    for shift, factor_ref in enumerate(factors):
        lanes = lanes_of(lax.rem(here_ref[0] + ranks - shift, ranks))
        for side in range(2):
            all_ref[pl.ds(side * rows, rows), lanes] = factor_ref[side]
    half = x_ref.shape[1] // 2
    chunks = mine_ref.shape[0]
    core = core_ref[0]
    g = vec_ref[5:6]
    scale = SCALE / g
    place = lax.broadcasted_iota(jnp.int32, (half, chunks), 1)
    wanted = lax.broadcasted_iota(jnp.int32, (half, chunks), 0)
    wanted = (wanted // 4) * 16 + wanted % 4
    place8 = lax.broadcasted_iota(jnp.int32, (8, chunks), 1) % 16
    is_dot = jnp.where((place8 >= 8) & (place8 < 11), 1.0, 0.0).astype(BF16)
    spread = jnp.dot(is_dot, mine_ref[...], preferred_element_type=F32) + jnp.dot(
        is_dot, other_ref[...], preferred_element_type=F32
    )
    xq, cq, yr, cr = (vec_ref[i : i + 1] for i in range(4))
    curvature = SCALE * (xq * cr + cq * yr - 2.0 * spread[0:1])
    grad_g = -curvature / jnp.square(g)
    grad_g_ref[...] = grad_g
    top = jnp.abs(grad_g)
    for emb_ref, offset, count, total, out_ref, own_ref in (
        (x_ref, 4, cr, yr, grad_q_ref, own_q_ref),
        (y_ref, 0, cq, xq, grad_r_ref, own_r_ref),
    ):
        select = jnp.where(place == wanted + offset, 1.0, 0.0).astype(BF16)
        product = None
        for position, cross_ref in ((core, mine_ref), (1 - core, other_ref)):
            rows = jnp.dot(select, cross_ref[...], preferred_element_type=F32).astype(BF16)
            emb = emb_ref[:, pl.ds(pl.multiple_of(position * half, half), half)]
            part = jnp.dot(emb, rows, preferred_element_type=F32)
            product = part if product is None else product + part
        norms = jnp.sum(jnp.square(emb_ref[...].astype(F32)), axis=1, keepdims=True)
        grad = scale * (norms * count + total - 2.0 * product)
        out_ref[...] = grad
        own_ref[...] = out_ref[:, lanes_of(here_ref[0])]
        top = jnp.maximum(top, jnp.max(jnp.abs(grad), axis=0, keepdims=True))
    blocks = in_rows(top, top.shape[1] // peak_ref.shape[2])
    peak = blocks[0]
    for block in blocks[1:]:
        peak = jnp.maximum(peak, block)
    peak_ref[...] = jnp.broadcast_to(peak[None], peak_ref.shape)


def kern_kernel(
    peak_ref, grad_q_ref, grad_r_ref, grad_g_ref, vec_ref, all_ref, kern_ref, log_ref, eta_ref
):
    rows = grad_q_ref.shape[0]
    peak = jnp.max(jnp.max(peak_ref[...], axis=0), axis=1, keepdims=True)
    eta = GAMMA / (peak + 1e-06)
    eta_ref[...] = jnp.broadcast_to(eta, eta_ref.shape)
    kern_g = vec_ref[5:6] * jnp.exp(-eta * grad_g_ref[...])
    log_ref[...] = jnp.concatenate(in_rows(jnp.log(kern_g), log_ref.shape[0]), axis=0)
    for side, grad_ref in enumerate((grad_q_ref, grad_r_ref)):
        part = pl.ds(side * rows, rows)
        kern = all_ref[part, :].astype(F32) * jnp.exp(-eta * grad_ref[...])
        kern_ref[part, :] = kern.astype(BF16)


def new_scalings(ranks, got_ref, v_ref, log_ref):
    t = jnp.sum(got_ref[...].astype(F32), axis=0)
    passed = jnp.log(v_ref[...] * t)
    weights = jnp.exp((log_ref[...] + passed[:ranks] + passed[ranks:]) / 3.0)
    return jnp.concatenate([weights, weights], axis=0) / t, weights


def send_columns(v, mass_ref, own_ref, other_ref, sent_ref, u_ref):
    ranks = v.shape[0] // 2
    rows = own_ref.shape[0] // 2

    def kern(member, side):
        return (own_ref, other_ref)[member][pl.ds(side * rows, rows), :]

    v_rows = [stack3(in_lanes(v, side * ranks, ranks)) for side in range(2)]
    sums = []
    for member in range(2):
        for side in range(2):
            part = lax.dot_general(
                v_rows[side], kern(member, side), (((1,), (1,)), ((), ())),
                preferred_element_type=F32,
            )
            sums.append(sum_rows(part))
    u = jnp.exp(POWER * jnp.log(mass_ref[...] / jnp.concatenate(sums, axis=0)))
    u_ref[...] = u
    columns = []
    for side in range(2):
        total = None
        for member in range(2):
            row = 2 * member + side
            part = jnp.dot(
                stack3(u[row : row + 1]), kern(member, side), preferred_element_type=F32
            )
            total = part if total is None else total + part
        columns += in_rows(sum_rows(total), ranks)
    part = jnp.concatenate(columns, axis=0).astype(sent_ref.dtype)
    sent_ref[...] = jnp.broadcast_to(part[None], sent_ref.shape)


def first_pass(mass_ref, own_ref, other_ref, sent_ref, u_ref):
    ones = jnp.ones(sent_ref.shape[1:], F32)
    send_columns(ones, mass_ref, own_ref, other_ref, sent_ref, u_ref)


def next_pass(got_ref, v_ref, log_ref, mass_ref, own_ref, other_ref, sent_ref, u_ref, new_ref):
    v, _ = new_scalings(log_ref.shape[0], got_ref, v_ref, log_ref)
    new_ref[...] = v
    send_columns(v, mass_ref, own_ref, other_ref, sent_ref, u_ref)


def profile_kernel(
    core_ref, got_ref, v_ref, log_ref, u_ref, own_ref, other_ref, expr_ref, more_ref,
    part_ref, new_ref, weights_ref,
):
    ranks = log_ref.shape[0]
    rows = own_ref.shape[0] // 2
    half = own_ref.shape[1] // 2
    v, weights = new_scalings(ranks, got_ref, v_ref, log_ref)
    new_ref[...] = v
    weights_ref[...] = weights
    u_columns = jnp.concatenate([u_ref[...], u_ref[...]], axis=0).T
    core = core_ref[0]
    blocks = [new_ref[pl.ds(ranks + core * (ranks // 2) + i, 1), :] for i in range(ranks // 2)]
    scale = jnp.concatenate(blocks, axis=1)
    lanes = pl.ds(pl.multiple_of(core * half, half), half)
    total = None
    for member, (kern_ref, cells_ref) in enumerate(((own_ref, expr_ref), (other_ref, more_ref))):
        kern = kern_ref[pl.ds(rows, rows), lanes].astype(F32)
        column = u_columns[:, 2 * member + 1 : 2 * member + 2]
        part = contract_rows((kern * scale * column).astype(BF16), cells_ref[...])
        total = part if total is None else total + part
    part_ref[...] = total


def on_chip(kernel, shapes, name, scalars=0, inputs=0, off_chip=0, scratch=(), limit=LIMIT):
    specs = {}
    if scalars:
        specs["in_specs"] = [pl.BlockSpec(memory_space=pltpu.SMEM)] * scalars + [
            pl.BlockSpec(memory_space=pltpu.VMEM)
        ] * inputs
    if off_chip:
        specs["in_specs"] = [pl.BlockSpec(memory_space=pltpu.HBM)] * off_chip
    return pl.pallas_call(
        kernel,
        out_shape=tuple(jax.ShapeDtypeStruct(shape, dtype) for shape, dtype in shapes),
        scratch_shapes=scratch,
        **specs,
        compiler_params=pltpu.CompilerParams(vmem_limit_bytes=limit),
        name=name,
    )


def shards(x_emb, y_emb, q_factor, r_factor, g_weights, a_mass, b_mass, expr):
    rows, width = q_factor.shape
    dim = x_emb.shape[1]
    genes = expr.shape[1]
    others = lax.axis_size(CHIPS)
    cell_devices = 2 * others
    ranks = lax.axis_size("x")
    cells_total = rows * cell_devices
    share = dim // cell_devices

    here = lax.axis_index("x")
    core = lax.axis_index("c")
    other_expr = swap(expr)
    core_index = core.astype(jnp.int32)[None]
    part_xq, part_yr, part_vec, rounded = on_chip(
        start_kernel,
        (
            ((dim, width), F32),
            ((dim, width), F32),
            ((4, width), F32),
            ((2, rows, width), BF16),
        ),
        "start",
        off_chip=4,
        limit=60 << 20,
        scratch=[
            pltpu.VMEM(x_emb.shape, BF16),
            pltpu.VMEM(y_emb.shape, BF16),
            pltpu.VMEM(q_factor.shape, F32),
            pltpu.VMEM(r_factor.shape, F32),
            pltpu.SemaphoreType.DMA((4, 2)),
        ],
    )(x_emb, y_emb, q_factor, r_factor)
    from_others = [
        lax.ppermute(rounded, "x", [(i, (i + shift) % ranks) for i in range(ranks)])
        for shift in range(1, ranks)
    ]
    part_cross = jnp.concatenate(
        [part.reshape(2, others, share, width) for part in (part_xq, part_yr)], axis=2
    )

    def with_vec(cross):
        return jnp.concatenate(
            [cross, jnp.broadcast_to(part_vec[None], (others, 4, width))], axis=1
        ).reshape(others, (2 * share + 4) // 4, 4, width)

    outgoing = with_vec(pick(part_cross, core)) + swap(with_vec(pick(part_cross, 1 - core)))
    columns = ranks * width
    tall = ((rows, columns), F32)
    sent = on_chip(chunk_kernel, (((ranks, 16, width), F32),), "chunk")(
        exchange(outgoing, CHIPS), g_weights[None]
    )[0]
    sent, vec = on_chip(
        spread_kernel, (((others, 16, columns), BF16), ((8, columns), F32)), "spread"
    )(exchange(sent, "x"))
    masses = jnp.stack([a_mass, b_mass])
    crosses, from_others, their_masses = lax.optimization_barrier(
        (exchange(sent, CHIPS), from_others, swap(masses))
    )
    crosses = crosses.reshape(others * 16, columns)
    own_grad = ((rows, width), F32)
    grad_q, grad_r, grad_g, peak, factors, own_grad_q, own_grad_r, masses = on_chip(
        grad_kernel,
        (
            tall, tall, ((1, columns), F32), ((cell_devices, 1, width), F32),
            ((2 * rows, columns), BF16), own_grad, own_grad, ((4, rows), F32),
        ),
        "grad",
        scalars=2,
        inputs=7 + ranks,
    )(
        core_index, here.astype(jnp.int32)[None], x_emb, y_emb, crosses, swap(crosses), vec,
        masses, their_masses, rounded, *from_others,
    )
    kerns, log_g, eta = on_chip(
        kern_kernel,
        (((2 * rows, columns), BF16), ((ranks, width), F32), ((1, width), F32)),
        "kern",
    )(exchange(peak, CELLS), grad_q, grad_r, grad_g, vec, factors)
    theirs = swap(kerns)
    sent_shape = ((others, 2 * ranks, width), BF16)
    u_shape = ((4, rows), F32)
    v_shape = ((2 * ranks, width), F32)
    sent, u = on_chip(first_pass, (sent_shape, u_shape), "first_pass")(masses, kerns, theirs)
    v = jnp.ones(v_shape[0], F32)
    for step in range(1, PASSES):
        sent, u, v = on_chip(next_pass, (sent_shape, u_shape, v_shape), "next_pass")(
            exchange(sent, CHIPS), v, log_g, masses, kerns, theirs
        )
    part, v, weights = on_chip(
        profile_kernel,
        (((ranks * width // 2, genes), F32), v_shape, ((ranks, width), F32)),
        "profile",
        scalars=1,
        inputs=8,
    )(
        core_index, exchange(sent, CHIPS), v, log_g, u, kerns, theirs,
        expr, other_expr,
    )
    v_q, v_r = v[:ranks], v[ranks:]
    kern_q = q_factor * jnp.exp(-eta * own_grad_q)
    kern_r = r_factor * jnp.exp(-eta * own_grad_r)
    q_new = u[0][:, None] * kern_q * pick(v_q, here)[None, :]
    r_new = u[1][:, None] * kern_r * pick(v_r, here)[None, :]
    mine_q = kerns[:rows].astype(F32)
    s_q = jnp.sum(mine_q * v_q.reshape(1, columns), axis=1)
    scaled = (mine_q * (v_q / weights).reshape(1, columns)).astype(BF16)

    piece = jnp.sum(exchange(part.reshape(others, -1, genes), CHIPS), axis=0)
    mine = to_all(piece.astype(BF16), CHIPS).reshape(columns // 2, genes)
    half = columns // 2
    mixed = jnp.dot(
        lax.dynamic_slice_in_dim(scaled, core * half, half, 1), mine, preferred_element_type=F32
    ) + jnp.dot(
        lax.dynamic_slice_in_dim(scaled, (1 - core) * half, half, 1),
        swap(mine),
        preferred_element_type=F32,
    )
    predicted = (mixed / s_q[:, None]).astype(BF16)
    return (q_new, r_new, pick(weights, here) / cells_total, predicted)


def solution(mesh):
    named = Mesh(mesh.devices.reshape(4, 8, 2, 4), EVERY)
    block = P(CELLS, "x")
    return jax.shard_map(
        shards,
        mesh=named,
        in_specs=(
            P(CELLS, None),
            P(CELLS, None),
            block,
            block,
            P("x"),
            P(CELLS),
            P(CELLS),
            block,
        ),
        out_specs=(block, block, P("x"), block),
        check_vma=False,
    )
```

```python
import jax
import jax.numpy as jnp
from jax import lax
from jax.experimental import pallas as pl
from jax.experimental.pallas import tpu as pltpu
from jax.sharding import Mesh
from jax.sharding import PartitionSpec as P

PASSES = 10
SCALE = 0.0625
GAMMA = 10.0
POWER = 0.8
LIMIT = 12 << 20

CHIPS = ("y", "z")
CELLS = ("y", "z", "c")
EVERY = ("y", "z", "c", "x")
F32 = jnp.float32
BF16 = jnp.bfloat16


def contract_rows(left, right):
    return lax.dot_general(
        left, right, (((0,), (0,)), ((), ())), preferred_element_type=F32
    )


def exchange(chunks, axes):
    return lax.all_to_all(chunks, axes, 0, 0, tiled=False)


def to_all(value, axes):
    count = lax.axis_size(axes)
    return exchange(jnp.broadcast_to(value[None], (count,) + value.shape), axes)


def swap(value):
    return lax.ppermute(value, "c", [(0, 1), (1, 0)])


def pick(value, index):
    return lax.dynamic_index_in_dim(value, index, 0, keepdims=False)


def split3(value):
    high = lax.reduce_precision(value, 8, 7)
    rest = value - high
    middle = lax.reduce_precision(rest, 8, 7)
    low = lax.reduce_precision(rest - middle, 8, 7)
    return jnp.stack([high, middle, low]).astype(BF16)


def join3(rows):
    parts = rows.astype(F32)
    return parts[..., 0, :] + (parts[..., 1, :] + parts[..., 2, :])


def stack3(value):
    high = value.astype(BF16).astype(F32)
    rest = value - high
    middle = rest.astype(BF16).astype(F32)
    return jnp.concatenate([high, middle, rest - middle], axis=0).astype(BF16)


def sum_rows(value):
    return value[0:1] + (value[1:2] + value[2:3])


def in_lanes(blocks, first, count):
    return jnp.concatenate([blocks[first + i : first + i + 1] for i in range(count)], axis=1)


def in_rows(row, count):
    width = row.shape[1] // count
    return [row[:, i * width : (i + 1) * width] for i in range(count)]


def start_kernel(
    core_ref, x_hbm, y_hbm, q_hbm, r_hbm, keep_ref, give_ref, cast_ref,
    x_ref, y_ref, q_ref, r_ref, sems,
):
    pieces = sems.shape[1]
    copies = []
    for i, (source, target) in enumerate(
        ((x_hbm, x_ref), (q_hbm, q_ref), (y_hbm, y_ref), (r_hbm, r_ref))
    ):
        size = source.shape[0] // pieces
        for k in range(pieces):
            part = pl.ds(k * size, size)
            copies.append(pltpu.make_async_copy(source.at[part], target.at[part], sems.at[i, k]))
    for copy in copies:
        copy.start()
    chunks, _, share, width = keep_ref.shape
    half = x_ref.shape[1] // 2
    rows = []
    for side, (emb_ref, factor_ref) in enumerate(((x_ref, q_ref), (y_ref, r_ref))):
        for copy in copies[2 * side * pieces : 2 * (side + 1) * pieces]:
            copy.wait()
        factor = factor_ref[...]
        rounded = factor.astype(BF16)
        cast_ref[side] = rounded
        for position, out_ref in ((core_ref[0], keep_ref), (1 - core_ref[0], give_ref)):
            emb = emb_ref[:, pl.ds(pl.multiple_of(position * half, half), half)]
            cross = contract_rows(emb, rounded)
            for chunk in range(chunks):
                out_ref[chunk, side] = cross[chunk * share : (chunk + 1) * share]
        norms = jnp.sum(jnp.square(emb_ref[...].astype(F32)), axis=1, keepdims=True)
        rows.append(jnp.sum(norms * factor, axis=0, keepdims=True))
        rows.append(jnp.sum(factor, axis=0, keepdims=True))
    vec = jnp.concatenate(rows, axis=0)
    for out_ref in (keep_ref, give_ref):
        out_ref[:, 2] = jnp.broadcast_to(vec[None], (chunks, 4, width))


def chunk_kernel(got_ref, g_ref, sent_ref):
    summed = jnp.sum(got_ref[...], axis=0)
    xq, yr = summed[0], summed[1]
    dot = jnp.sum(xq * yr, axis=0, keepdims=True)
    nothing = jnp.zeros((2, dot.shape[1]), F32)
    chunk = jnp.concatenate([xq, yr, summed[2], dot, g_ref[...], nothing], axis=0)
    sent_ref[...] = jnp.broadcast_to(chunk[None], sent_ref.shape)


def spread_kernel(got_ref, sent_ref, vec_ref):
    every = jnp.concatenate([got_ref[i] for i in range(got_ref.shape[0])], axis=1)
    dot = every[12:13]
    high = dot.astype(BF16).astype(F32)
    rest = dot - high
    middle = rest.astype(BF16).astype(F32)
    nothing = jnp.zeros((5, dot.shape[1]), F32)
    chunk = jnp.concatenate([every[:8], high, middle, rest - middle, nothing], axis=0)
    sent_ref[...] = jnp.broadcast_to(chunk.astype(BF16)[None], sent_ref.shape)
    vec_ref[...] = every[8:16]


def grad_kernel(
    core_ref, here_ref, x_ref, y_ref, mine_ref, other_ref, vec_ref, mass_ref, mass2_ref, *refs
):
    factors = refs[:-6]
    grad_q_ref, grad_r_ref, grad_g_ref, peak_ref, all_ref, masses_ref = refs[-6:]
    masses_ref[...] = jnp.concatenate([mass_ref[...], mass2_ref[...]], axis=0)
    ranks = len(factors)
    rows, width = factors[0].shape[1:]

    def lanes_of(block):
        return pl.ds(pl.multiple_of(block * width, width), width)

    for shift, factor_ref in enumerate(factors):
        lanes = lanes_of(lax.rem(here_ref[0] + ranks - shift, ranks))
        for side in range(2):
            all_ref[pl.ds(side * rows, rows), lanes] = factor_ref[side]
    half = x_ref.shape[1] // 2
    chunks = mine_ref.shape[0]
    core = core_ref[0]
    g = vec_ref[5:6]
    scale = SCALE / g
    place = lax.broadcasted_iota(jnp.int32, (half, chunks), 1)
    wanted = lax.broadcasted_iota(jnp.int32, (half, chunks), 0)
    wanted = (wanted // 4) * 16 + wanted % 4
    place8 = lax.broadcasted_iota(jnp.int32, (8, chunks), 1) % 16
    is_dot = jnp.where((place8 >= 8) & (place8 < 11), 1.0, 0.0).astype(BF16)
    spread = jnp.dot(is_dot, mine_ref[...], preferred_element_type=F32) + jnp.dot(
        is_dot, other_ref[...], preferred_element_type=F32
    )
    xq, cq, yr, cr = (vec_ref[i : i + 1] for i in range(4))
    curvature = SCALE * (xq * cr + cq * yr - 2.0 * spread[0:1])
    grad_g = -curvature / jnp.square(g)
    grad_g_ref[...] = grad_g
    top = jnp.abs(grad_g)
    for emb_ref, offset, count, total, out_ref in (
        (x_ref, 4, cr, yr, grad_q_ref),
        (y_ref, 0, cq, xq, grad_r_ref),
    ):
        select = jnp.where(place == wanted + offset, 1.0, 0.0).astype(BF16)
        product = None
        for position, cross_ref in ((core, mine_ref), (1 - core, other_ref)):
            rows = jnp.dot(select, cross_ref[...], preferred_element_type=F32).astype(BF16)
            emb = emb_ref[:, pl.ds(pl.multiple_of(position * half, half), half)]
            part = jnp.dot(emb, rows, preferred_element_type=F32)
            product = part if product is None else product + part
        norms = jnp.sum(jnp.square(emb_ref[...].astype(F32)), axis=1, keepdims=True)
        grad = scale * (norms * count + total - 2.0 * product)
        out_ref[...] = grad
        top = jnp.maximum(top, jnp.max(jnp.abs(grad), axis=0, keepdims=True))
    blocks = in_rows(top, top.shape[1] // peak_ref.shape[2])
    peak = blocks[0]
    for block in blocks[1:]:
        peak = jnp.maximum(peak, block)
    peak_ref[...] = jnp.broadcast_to(peak[None], peak_ref.shape)


def kern_kernel(
    here_ref, peak_ref, grad_q_ref, grad_r_ref, grad_g_ref, vec_ref, all_ref,
    kern_ref, log_ref, eta_ref, own_q_ref, own_r_ref,
):
    rows = grad_q_ref.shape[0]
    width = own_q_ref.shape[1]
    mine = pl.ds(pl.multiple_of(here_ref[0] * width, width), width)
    own_q_ref[...] = grad_q_ref[:, mine]
    own_r_ref[...] = grad_r_ref[:, mine]
    peak = jnp.max(jnp.max(peak_ref[...], axis=0), axis=1, keepdims=True)
    eta = GAMMA / (peak + 1e-06)
    eta_ref[...] = jnp.broadcast_to(eta, eta_ref.shape)
    kern_g = vec_ref[5:6] * jnp.exp(-eta * grad_g_ref[...])
    log_ref[...] = jnp.concatenate(in_rows(jnp.log(kern_g), log_ref.shape[0]), axis=0)
    for side, grad_ref in enumerate((grad_q_ref, grad_r_ref)):
        part = pl.ds(side * rows, rows)
        kern = all_ref[part, :].astype(F32) * jnp.exp(-eta * grad_ref[...])
        kern_ref[part, :] = kern.astype(BF16)


def new_scalings(ranks, got_ref, v_ref, log_ref):
    t = jnp.sum(got_ref[...].astype(F32), axis=0)
    passed = jnp.log(v_ref[...] * t)
    weights = jnp.exp((log_ref[...] + passed[:ranks] + passed[ranks:]) / 3.0)
    return jnp.concatenate([weights, weights], axis=0) / t, weights


def send_columns(v, mass_ref, own_ref, other_ref, sent_ref, u_ref):
    ranks = v.shape[0] // 2
    rows = own_ref.shape[0] // 2

    def kern(member, side):
        return (own_ref, other_ref)[member][pl.ds(side * rows, rows), :]

    v_rows = [stack3(in_lanes(v, side * ranks, ranks)) for side in range(2)]
    sums = []
    for member in range(2):
        for side in range(2):
            part = lax.dot_general(
                v_rows[side], kern(member, side), (((1,), (1,)), ((), ())),
                preferred_element_type=F32,
            )
            sums.append(sum_rows(part))
    u = jnp.exp(POWER * jnp.log(mass_ref[...] / jnp.concatenate(sums, axis=0)))
    u_ref[...] = u
    columns = []
    for side in range(2):
        total = None
        for member in range(2):
            row = 2 * member + side
            part = jnp.dot(
                stack3(u[row : row + 1]), kern(member, side), preferred_element_type=F32
            )
            total = part if total is None else total + part
        columns += in_rows(sum_rows(total), ranks)
    part = jnp.concatenate(columns, axis=0).astype(sent_ref.dtype)
    sent_ref[...] = jnp.broadcast_to(part[None], sent_ref.shape)


def first_pass(mass_ref, own_ref, other_ref, sent_ref, u_ref):
    ones = jnp.ones(sent_ref.shape[1:], F32)
    send_columns(ones, mass_ref, own_ref, other_ref, sent_ref, u_ref)


def next_pass(got_ref, v_ref, log_ref, mass_ref, own_ref, other_ref, sent_ref, u_ref, new_ref):
    v, _ = new_scalings(log_ref.shape[0], got_ref, v_ref, log_ref)
    new_ref[...] = v
    send_columns(v, mass_ref, own_ref, other_ref, sent_ref, u_ref)


def profile_kernel(
    core_ref, got_ref, v_ref, log_ref, u_ref, own_ref, other_ref, expr_ref, more_ref,
    part_ref, new_ref, weights_ref,
):
    ranks = log_ref.shape[0]
    rows = own_ref.shape[0] // 2
    half = own_ref.shape[1] // 2
    v, weights = new_scalings(ranks, got_ref, v_ref, log_ref)
    new_ref[...] = v
    weights_ref[...] = weights
    u_columns = jnp.concatenate([u_ref[...], u_ref[...]], axis=0).T
    core = core_ref[0]
    blocks = [new_ref[pl.ds(ranks + core * (ranks // 2) + i, 1), :] for i in range(ranks // 2)]
    scale = jnp.concatenate(blocks, axis=1)
    lanes = pl.ds(pl.multiple_of(core * half, half), half)
    total = None
    for member, (kern_ref, cells_ref) in enumerate(((own_ref, expr_ref), (other_ref, more_ref))):
        kern = kern_ref[pl.ds(rows, rows), lanes].astype(F32)
        column = u_columns[:, 2 * member + 1 : 2 * member + 2]
        part = contract_rows((kern * scale * column).astype(BF16), cells_ref[...])
        total = part if total is None else total + part
    part_ref[...] = total


def on_chip(kernel, shapes, name, scalars=0, inputs=0, off_chip=0, scratch=(), limit=LIMIT):
    specs = {}
    if scalars:
        specs["in_specs"] = (
            [pl.BlockSpec(memory_space=pltpu.SMEM)] * scalars
            + [pl.BlockSpec(memory_space=pltpu.VMEM)] * inputs
            + [pl.BlockSpec(memory_space=pltpu.HBM)] * off_chip
        )
    return pl.pallas_call(
        kernel,
        out_shape=tuple(jax.ShapeDtypeStruct(shape, dtype) for shape, dtype in shapes),
        scratch_shapes=scratch,
        **specs,
        compiler_params=pltpu.CompilerParams(vmem_limit_bytes=limit),
        name=name,
    )


def shards(x_emb, y_emb, q_factor, r_factor, g_weights, a_mass, b_mass, expr):
    rows, width = q_factor.shape
    dim = x_emb.shape[1]
    genes = expr.shape[1]
    others = lax.axis_size(CHIPS)
    cell_devices = 2 * others
    ranks = lax.axis_size("x")
    cells_total = rows * cell_devices
    share = dim // cell_devices

    here = lax.axis_index("x")
    core = lax.axis_index("c")
    other_expr = swap(expr)
    core_index = core.astype(jnp.int32)[None]
    chunk_shape = ((others, 3, share, width), F32)
    keep, give, rounded = on_chip(
        start_kernel,
        (chunk_shape, chunk_shape, ((2, rows, width), BF16)),
        "start",
        scalars=1,
        off_chip=4,
        limit=60 << 20,
        scratch=[
            pltpu.VMEM(x_emb.shape, BF16),
            pltpu.VMEM(y_emb.shape, BF16),
            pltpu.VMEM(q_factor.shape, F32),
            pltpu.VMEM(r_factor.shape, F32),
            pltpu.SemaphoreType.DMA((4, 2)),
        ],
    )(core_index, x_emb, y_emb, q_factor, r_factor)

    def from_shift(shift):
        return lax.ppermute(rounded, "x", [(i, (i + shift) % ranks) for i in range(ranks)])

    outgoing = keep + swap(give)
    columns = ranks * width
    tall = ((rows, columns), F32)
    got, second = lax.optimization_barrier((exchange(outgoing, CHIPS), from_shift(2)))
    sent = on_chip(chunk_kernel, (((ranks, 16, width), F32),), "chunk")(got, g_weights[None])[0]
    got, first = lax.optimization_barrier((exchange(sent, "x"), from_shift(1)))
    sent, vec = on_chip(
        spread_kernel, (((others, 16, columns), BF16), ((8, columns), F32)), "spread"
    )(got)
    masses = jnp.stack([a_mass, b_mass])
    crosses, third, their_masses = lax.optimization_barrier(
        (exchange(sent, CHIPS), from_shift(3), swap(masses))
    )
    crosses = crosses.reshape(others * 16, columns)
    own_grad = ((rows, width), F32)
    grad_q, grad_r, grad_g, peak, factors, masses = on_chip(
        grad_kernel,
        (
            tall, tall, ((1, columns), F32), ((cell_devices, 1, width), F32),
            ((2 * rows, columns), BF16), ((4, rows), F32),
        ),
        "grad",
        scalars=2,
        inputs=7 + ranks,
    )(
        core_index, here.astype(jnp.int32)[None], x_emb, y_emb, crosses, swap(crosses), vec,
        masses, their_masses, rounded, first, second, third,
    )
    kerns, log_g, eta, own_grad_q, own_grad_r = on_chip(
        kern_kernel,
        (((2 * rows, columns), BF16), ((ranks, width), F32), ((1, width), F32), own_grad, own_grad),
        "kern",
        scalars=1,
        inputs=6,
    )(
        here.astype(jnp.int32)[None], exchange(peak, CELLS), grad_q, grad_r, grad_g, vec, factors
    )
    theirs = swap(kerns)
    sent_shape = ((others, 2 * ranks, width), BF16)
    u_shape = ((4, rows), F32)
    v_shape = ((2 * ranks, width), F32)
    sent, u = on_chip(first_pass, (sent_shape, u_shape), "first_pass")(masses, kerns, theirs)
    v = jnp.ones(v_shape[0], F32)
    for step in range(1, PASSES):
        sent, u, v = on_chip(next_pass, (sent_shape, u_shape, v_shape), "next_pass")(
            exchange(sent, CHIPS), v, log_g, masses, kerns, theirs
        )
    part, v, weights = on_chip(
        profile_kernel,
        (((ranks * width // 2, genes), F32), v_shape, ((ranks, width), F32)),
        "profile",
        scalars=1,
        inputs=8,
    )(
        core_index, exchange(sent, CHIPS), v, log_g, u, kerns, theirs,
        expr, other_expr,
    )
    v_q, v_r = v[:ranks], v[ranks:]
    kern_q = q_factor * jnp.exp(-eta * own_grad_q)
    kern_r = r_factor * jnp.exp(-eta * own_grad_r)
    q_new = u[0][:, None] * kern_q * pick(v_q, here)[None, :]
    r_new = u[1][:, None] * kern_r * pick(v_r, here)[None, :]
    mine_q = kerns[:rows].astype(F32)
    s_q = jnp.sum(mine_q * v_q.reshape(1, columns), axis=1)
    scaled = (mine_q * (v_q / weights).reshape(1, columns)).astype(BF16)

    piece = jnp.sum(exchange(part.reshape(others, -1, genes), CHIPS), axis=0)
    mine = to_all(piece.astype(BF16), CHIPS).reshape(columns // 2, genes)
    half = columns // 2
    mixed = jnp.dot(
        lax.dynamic_slice_in_dim(scaled, core * half, half, 1), mine, preferred_element_type=F32
    ) + jnp.dot(
        lax.dynamic_slice_in_dim(scaled, (1 - core) * half, half, 1),
        swap(mine),
        preferred_element_type=F32,
    )
    predicted = (mixed / s_q[:, None]).astype(BF16)
    return (q_new, r_new, pick(weights, here) / cells_total, predicted)


def solution(mesh):
    named = Mesh(mesh.devices.reshape(4, 8, 2, 4), EVERY)
    block = P(CELLS, "x")
    return jax.shard_map(
        shards,
        mesh=named,
        in_specs=(
            P(CELLS, None),
            P(CELLS, None),
            block,
            block,
            P("x"),
            P(CELLS),
            P(CELLS),
            block,
        ),
        out_specs=(block, block, P("x"), block),
        check_vma=False,
    )
```

```python
import jax
import jax.numpy as jnp
from jax import lax
from jax.experimental import pallas as pl
from jax.experimental.pallas import tpu as pltpu
from jax.sharding import Mesh
from jax.sharding import PartitionSpec as P

PASSES = 10
SCALE = 0.0625
GAMMA = 10.0
POWER = 0.8
LIMIT = 12 << 20

CHIPS = ("y", "z")
CELLS = ("y", "z", "c")
EVERY = ("y", "z", "c", "x")
F32 = jnp.float32
BF16 = jnp.bfloat16


def contract_rows(left, right):
    return lax.dot_general(
        left, right, (((0,), (0,)), ((), ())), preferred_element_type=F32
    )


def exchange(chunks, axes):
    return lax.all_to_all(chunks, axes, 0, 0, tiled=False)


def to_all(value, axes):
    count = lax.axis_size(axes)
    return exchange(jnp.broadcast_to(value[None], (count,) + value.shape), axes)


def swap(value):
    return lax.ppermute(value, "c", [(0, 1), (1, 0)])


def pick(value, index):
    return lax.dynamic_index_in_dim(value, index, 0, keepdims=False)


def split3(value):
    high = lax.reduce_precision(value, 8, 7)
    rest = value - high
    middle = lax.reduce_precision(rest, 8, 7)
    low = lax.reduce_precision(rest - middle, 8, 7)
    return jnp.stack([high, middle, low]).astype(BF16)


def join3(rows):
    parts = rows.astype(F32)
    return parts[..., 0, :] + (parts[..., 1, :] + parts[..., 2, :])


def stack3(value):
    high = value.astype(BF16).astype(F32)
    rest = value - high
    middle = rest.astype(BF16).astype(F32)
    return jnp.concatenate([high, middle, rest - middle], axis=0).astype(BF16)


def sum_rows(value):
    return value[0:1] + (value[1:2] + value[2:3])


def in_lanes(blocks, first, count):
    return jnp.concatenate([blocks[first + i : first + i + 1] for i in range(count)], axis=1)


def in_rows(row, count):
    width = row.shape[1] // count
    return [row[:, i * width : (i + 1) * width] for i in range(count)]


def start_kernel(
    core_ref, x_hbm, y_hbm, q_hbm, r_hbm, keep_ref, give_ref, cast_ref,
    x_ref, y_ref, q_ref, r_ref, sems,
):
    pieces = sems.shape[1]
    copies = []
    for i, (source, target) in enumerate(
        ((x_hbm, x_ref), (q_hbm, q_ref), (y_hbm, y_ref), (r_hbm, r_ref))
    ):
        size = source.shape[0] // pieces
        for k in range(pieces):
            part = pl.ds(k * size, size)
            copies.append(pltpu.make_async_copy(source.at[part], target.at[part], sems.at[i, k]))
    for copy in copies:
        copy.start()
    chunks, _, share, width = keep_ref.shape
    half = x_ref.shape[1] // 2
    rows = []
    for side, (emb_ref, factor_ref) in enumerate(((x_ref, q_ref), (y_ref, r_ref))):
        for copy in copies[2 * side * pieces : 2 * (side + 1) * pieces]:
            copy.wait()
        factor = factor_ref[...]
        rounded = factor.astype(BF16)
        cast_ref[side] = rounded
        for position, out_ref in ((core_ref[0], keep_ref), (1 - core_ref[0], give_ref)):
            emb = emb_ref[:, pl.ds(pl.multiple_of(position * half, half), half)]
            cross = contract_rows(emb, rounded)
            for chunk in range(chunks):
                out_ref[chunk, side] = cross[chunk * share : (chunk + 1) * share]
        norms = jnp.sum(jnp.square(emb_ref[...].astype(F32)), axis=1, keepdims=True)
        rows.append(jnp.sum(norms * factor, axis=0, keepdims=True))
        rows.append(jnp.sum(factor, axis=0, keepdims=True))
    vec = jnp.concatenate(rows, axis=0)
    for out_ref in (keep_ref, give_ref):
        out_ref[:, 2] = jnp.broadcast_to(vec[None], (chunks, 4, width))


def chunk_kernel(got_ref, g_ref, sent_ref):
    summed = jnp.sum(got_ref[...], axis=0)
    xq, yr = summed[0], summed[1]
    dot = jnp.sum(xq * yr, axis=0, keepdims=True)
    nothing = jnp.zeros((2, dot.shape[1]), F32)
    chunk = jnp.concatenate([xq, yr, summed[2], dot, g_ref[...], nothing], axis=0)
    sent_ref[...] = jnp.broadcast_to(chunk[None], sent_ref.shape)


def spread_kernel(got_ref, sent_ref, vec_ref):
    every = jnp.concatenate([got_ref[i] for i in range(got_ref.shape[0])], axis=1)
    dot = every[12:13]
    high = dot.astype(BF16).astype(F32)
    rest = dot - high
    middle = rest.astype(BF16).astype(F32)
    nothing = jnp.zeros((5, dot.shape[1]), F32)
    chunk = jnp.concatenate([every[:8], high, middle, rest - middle, nothing], axis=0)
    sent_ref[...] = jnp.broadcast_to(chunk.astype(BF16)[None], sent_ref.shape)
    vec_ref[...] = every[8:16]


def grad_kernel(
    core_ref, here_ref, x_ref, y_ref, mine_ref, other_ref, vec_ref, mass_ref, mass2_ref, *refs
):
    factors = refs[:-6]
    grad_q_ref, grad_r_ref, grad_g_ref, peak_ref, all_ref, masses_ref = refs[-6:]
    masses_ref[...] = jnp.concatenate([mass_ref[...], mass2_ref[...]], axis=0)
    ranks = len(factors)
    rows, width = factors[0].shape[1:]

    def lanes_of(block):
        return pl.ds(pl.multiple_of(block * width, width), width)

    for shift, factor_ref in enumerate(factors):
        lanes = lanes_of(lax.rem(here_ref[0] + ranks - shift, ranks))
        for side in range(2):
            all_ref[pl.ds(side * rows, rows), lanes] = factor_ref[side]
    half = x_ref.shape[1] // 2
    chunks = mine_ref.shape[0]
    core = core_ref[0]
    g = vec_ref[5:6]
    scale = SCALE / g
    place = lax.broadcasted_iota(jnp.int32, (half, chunks), 1)
    wanted = lax.broadcasted_iota(jnp.int32, (half, chunks), 0)
    wanted = (wanted // 4) * 16 + wanted % 4
    place8 = lax.broadcasted_iota(jnp.int32, (8, chunks), 1) % 16
    is_dot = jnp.where((place8 >= 8) & (place8 < 11), 1.0, 0.0).astype(BF16)
    spread = jnp.dot(is_dot, mine_ref[...], preferred_element_type=F32) + jnp.dot(
        is_dot, other_ref[...], preferred_element_type=F32
    )
    xq, cq, yr, cr = (vec_ref[i : i + 1] for i in range(4))
    curvature = SCALE * (xq * cr + cq * yr - 2.0 * spread[0:1])
    grad_g = -curvature / jnp.square(g)
    grad_g_ref[...] = grad_g
    top = jnp.abs(grad_g)
    for emb_ref, offset, count, total, out_ref in (
        (x_ref, 4, cr, yr, grad_q_ref),
        (y_ref, 0, cq, xq, grad_r_ref),
    ):
        select = jnp.where(place == wanted + offset, 1.0, 0.0).astype(BF16)
        product = None
        for position, cross_ref in ((core, mine_ref), (1 - core, other_ref)):
            rows = jnp.dot(select, cross_ref[...], preferred_element_type=F32).astype(BF16)
            emb = emb_ref[:, pl.ds(pl.multiple_of(position * half, half), half)]
            part = jnp.dot(emb, rows, preferred_element_type=F32)
            product = part if product is None else product + part
        norms = jnp.sum(jnp.square(emb_ref[...].astype(F32)), axis=1, keepdims=True)
        grad = scale * (norms * count + total - 2.0 * product)
        out_ref[...] = grad
        top = jnp.maximum(top, jnp.max(jnp.abs(grad), axis=0, keepdims=True))
    blocks = in_rows(top, top.shape[1] // peak_ref.shape[2])
    peak = blocks[0]
    for block in blocks[1:]:
        peak = jnp.maximum(peak, block)
    peak_ref[...] = jnp.broadcast_to(peak[None], peak_ref.shape)


def kern_kernel(
    here_ref, peak_ref, grad_q_ref, grad_r_ref, grad_g_ref, vec_ref, all_ref,
    kern_ref, log_ref, eta_ref, own_q_ref, own_r_ref,
):
    rows = grad_q_ref.shape[0]
    width = own_q_ref.shape[1]
    mine = pl.ds(pl.multiple_of(here_ref[0] * width, width), width)
    own_q_ref[...] = grad_q_ref[:, mine]
    own_r_ref[...] = grad_r_ref[:, mine]
    peak = jnp.max(jnp.max(peak_ref[...], axis=0), axis=1, keepdims=True)
    eta = GAMMA / (peak + 1e-06)
    eta_ref[...] = jnp.broadcast_to(eta, eta_ref.shape)
    kern_g = vec_ref[5:6] * jnp.exp(-eta * grad_g_ref[...])
    log_ref[...] = jnp.concatenate(in_rows(jnp.log(kern_g), log_ref.shape[0]), axis=0)
    for side, grad_ref in enumerate((grad_q_ref, grad_r_ref)):
        part = pl.ds(side * rows, rows)
        kern = all_ref[part, :].astype(F32) * jnp.exp(-eta * grad_ref[...])
        kern_ref[part, :] = kern.astype(BF16)


def new_scalings(ranks, got_ref, v_ref, log_ref):
    t = jnp.sum(got_ref[...].astype(F32), axis=0)
    passed = jnp.log(v_ref[...] * t)
    weights = jnp.exp((log_ref[...] + passed[:ranks] + passed[ranks:]) / 3.0)
    return jnp.concatenate([weights, weights], axis=0) / t, weights


def send_columns(v, mass_ref, own_ref, other_ref, sent_ref, u_ref):
    ranks = v.shape[0] // 2
    rows = own_ref.shape[0] // 2

    def kern(member, side):
        return (own_ref, other_ref)[member][pl.ds(side * rows, rows), :]

    v_rows = [stack3(in_lanes(v, side * ranks, ranks)) for side in range(2)]
    sums = []
    for member in range(2):
        for side in range(2):
            part = lax.dot_general(
                v_rows[side], kern(member, side), (((1,), (1,)), ((), ())),
                preferred_element_type=F32,
            )
            sums.append(sum_rows(part))
    u = jnp.exp(POWER * jnp.log(mass_ref[...] / jnp.concatenate(sums, axis=0)))
    u_ref[...] = u
    columns = []
    for side in range(2):
        total = None
        for member in range(2):
            row = 2 * member + side
            part = jnp.dot(
                stack3(u[row : row + 1]), kern(member, side), preferred_element_type=F32
            )
            total = part if total is None else total + part
        columns += in_rows(sum_rows(total), ranks)
    part = jnp.concatenate(columns, axis=0).astype(sent_ref.dtype)
    sent_ref[...] = jnp.broadcast_to(part[None], sent_ref.shape)


def first_pass(mass_ref, own_ref, other_ref, sent_ref, u_ref):
    ones = jnp.ones(sent_ref.shape[1:], F32)
    send_columns(ones, mass_ref, own_ref, other_ref, sent_ref, u_ref)


def next_pass(got_ref, v_ref, log_ref, mass_ref, own_ref, other_ref, sent_ref, u_ref, new_ref):
    v, _ = new_scalings(log_ref.shape[0], got_ref, v_ref, log_ref)
    new_ref[...] = v
    send_columns(v, mass_ref, own_ref, other_ref, sent_ref, u_ref)


def profile_kernel(
    core_ref, got_ref, v_ref, log_ref, u_ref, own_ref, other_ref, expr_ref, more_ref,
    part_ref, new_ref, weights_ref,
):
    ranks = log_ref.shape[0]
    rows = own_ref.shape[0] // 2
    half = own_ref.shape[1] // 2
    v, weights = new_scalings(ranks, got_ref, v_ref, log_ref)
    new_ref[...] = v
    weights_ref[...] = weights
    u_columns = jnp.concatenate([u_ref[...], u_ref[...]], axis=0).T
    core = core_ref[0]
    blocks = [new_ref[pl.ds(ranks + core * (ranks // 2) + i, 1), :] for i in range(ranks // 2)]
    scale = jnp.concatenate(blocks, axis=1)
    lanes = pl.ds(pl.multiple_of(core * half, half), half)
    total = None
    for member, (kern_ref, cells_ref) in enumerate(((own_ref, expr_ref), (other_ref, more_ref))):
        kern = kern_ref[pl.ds(rows, rows), lanes].astype(F32)
        column = u_columns[:, 2 * member + 1 : 2 * member + 2]
        part = contract_rows((kern * scale * column).astype(BF16), cells_ref[...])
        total = part if total is None else total + part
    part_ref[...] = total


def on_chip(kernel, shapes, name, scalars=0, inputs=0, off_chip=0, scratch=(), limit=LIMIT):
    specs = {}
    if scalars:
        specs["in_specs"] = (
            [pl.BlockSpec(memory_space=pltpu.SMEM)] * scalars
            + [pl.BlockSpec(memory_space=pltpu.VMEM)] * inputs
            + [pl.BlockSpec(memory_space=pltpu.HBM)] * off_chip
        )
    return pl.pallas_call(
        kernel,
        out_shape=tuple(jax.ShapeDtypeStruct(shape, dtype) for shape, dtype in shapes),
        scratch_shapes=scratch,
        **specs,
        compiler_params=pltpu.CompilerParams(vmem_limit_bytes=limit),
        name=name,
    )


def shards(x_emb, y_emb, q_factor, r_factor, g_weights, a_mass, b_mass, expr):
    rows, width = q_factor.shape
    dim = x_emb.shape[1]
    genes = expr.shape[1]
    others = lax.axis_size(CHIPS)
    cell_devices = 2 * others
    ranks = lax.axis_size("x")
    cells_total = rows * cell_devices
    share = dim // cell_devices

    here = lax.axis_index("x")
    core = lax.axis_index("c")
    core_index = core.astype(jnp.int32)[None]
    chunk_shape = ((others, 3, share, width), F32)
    keep, give, rounded = on_chip(
        start_kernel,
        (chunk_shape, chunk_shape, ((2, rows, width), BF16)),
        "start",
        scalars=1,
        off_chip=4,
        limit=60 << 20,
        scratch=[
            pltpu.VMEM(x_emb.shape, BF16),
            pltpu.VMEM(y_emb.shape, BF16),
            pltpu.VMEM(q_factor.shape, F32),
            pltpu.VMEM(r_factor.shape, F32),
            pltpu.SemaphoreType.DMA((4, 2)),
        ],
    )(core_index, x_emb, y_emb, q_factor, r_factor)

    def from_shift(shift):
        return lax.ppermute(rounded, "x", [(i, (i + shift) % ranks) for i in range(ranks)])

    outgoing = keep + swap(give)
    columns = ranks * width
    tall = ((rows, columns), F32)
    sent = on_chip(chunk_kernel, (((ranks, 16, width), F32),), "chunk")(
        exchange(outgoing, CHIPS), g_weights[None]
    )[0]
    masses = jnp.stack([a_mass, b_mass])
    got, first, second, third, their_masses = lax.optimization_barrier(
        (exchange(sent, "x"), from_shift(1), from_shift(2), from_shift(3), swap(masses))
    )
    sent, vec = on_chip(
        spread_kernel, (((others, 16, columns), BF16), ((8, columns), F32)), "spread"
    )(got)
    crosses, other_expr = lax.optimization_barrier((exchange(sent, CHIPS), swap(expr)))
    crosses = crosses.reshape(others * 16, columns)
    own_grad = ((rows, width), F32)
    grad_q, grad_r, grad_g, peak, factors, masses = on_chip(
        grad_kernel,
        (
            tall, tall, ((1, columns), F32), ((cell_devices, 1, width), F32),
            ((2 * rows, columns), BF16), ((4, rows), F32),
        ),
        "grad",
        scalars=2,
        inputs=7 + ranks,
    )(
        core_index, here.astype(jnp.int32)[None], x_emb, y_emb, crosses, swap(crosses), vec,
        masses, their_masses, rounded, first, second, third,
    )
    kerns, log_g, eta, own_grad_q, own_grad_r = on_chip(
        kern_kernel,
        (((2 * rows, columns), BF16), ((ranks, width), F32), ((1, width), F32), own_grad, own_grad),
        "kern",
        scalars=1,
        inputs=6,
    )(
        here.astype(jnp.int32)[None], exchange(peak, CELLS), grad_q, grad_r, grad_g, vec, factors
    )
    theirs = swap(kerns)
    sent_shape = ((others, 2 * ranks, width), BF16)
    u_shape = ((4, rows), F32)
    v_shape = ((2 * ranks, width), F32)
    sent, u = on_chip(first_pass, (sent_shape, u_shape), "first_pass")(masses, kerns, theirs)
    v = jnp.ones(v_shape[0], F32)
    for step in range(1, PASSES):
        sent, u, v = on_chip(next_pass, (sent_shape, u_shape, v_shape), "next_pass")(
            exchange(sent, CHIPS), v, log_g, masses, kerns, theirs
        )
    part, v, weights = on_chip(
        profile_kernel,
        (((ranks * width // 2, genes), F32), v_shape, ((ranks, width), F32)),
        "profile",
        scalars=1,
        inputs=8,
    )(
        core_index, exchange(sent, CHIPS), v, log_g, u, kerns, theirs,
        expr, other_expr,
    )
    v_q, v_r = v[:ranks], v[ranks:]
    kern_q = q_factor * jnp.exp(-eta * own_grad_q)
    kern_r = r_factor * jnp.exp(-eta * own_grad_r)
    q_new = u[0][:, None] * kern_q * pick(v_q, here)[None, :]
    r_new = u[1][:, None] * kern_r * pick(v_r, here)[None, :]
    mine_q = kerns[:rows].astype(F32)
    s_q = jnp.sum(mine_q * v_q.reshape(1, columns), axis=1)
    scaled = (mine_q * (v_q / weights).reshape(1, columns)).astype(BF16)

    piece = jnp.sum(exchange(part.reshape(others, -1, genes), CHIPS), axis=0)
    mine = to_all(piece.astype(BF16), CHIPS).reshape(columns // 2, genes)
    half = columns // 2
    mixed = jnp.dot(
        lax.dynamic_slice_in_dim(scaled, core * half, half, 1), mine, preferred_element_type=F32
    ) + jnp.dot(
        lax.dynamic_slice_in_dim(scaled, (1 - core) * half, half, 1),
        swap(mine),
        preferred_element_type=F32,
    )
    predicted = (mixed / s_q[:, None]).astype(BF16)
    return (q_new, r_new, pick(weights, here) / cells_total, predicted)


def solution(mesh):
    named = Mesh(mesh.devices.reshape(4, 8, 2, 4), EVERY)
    block = P(CELLS, "x")
    return jax.shard_map(
        shards,
        mesh=named,
        in_specs=(
            P(CELLS, None),
            P(CELLS, None),
            block,
            block,
            P("x"),
            P(CELLS),
            P(CELLS),
            block,
        ),
        out_specs=(block, block, P("x"), block),
        check_vma=False,
    )
```

```python
import jax
import jax.numpy as jnp
from jax import lax
from jax.experimental import pallas as pl
from jax.experimental.pallas import tpu as pltpu
from jax.sharding import Mesh
from jax.sharding import PartitionSpec as P

PASSES = 10
SCALE = 0.0625
GAMMA = 10.0
POWER = 0.8
LIMIT = 12 << 20

CHIPS = ("y", "z")
CELLS = ("y", "z", "c")
EVERY = ("y", "z", "c", "x")
F32 = jnp.float32
BF16 = jnp.bfloat16


def contract_rows(left, right):
    return lax.dot_general(
        left, right, (((0,), (0,)), ((), ())), preferred_element_type=F32
    )


def exchange(chunks, axes):
    return lax.all_to_all(chunks, axes, 0, 0, tiled=False)


def to_all(value, axes):
    count = lax.axis_size(axes)
    return exchange(jnp.broadcast_to(value[None], (count,) + value.shape), axes)


def swap(value):
    return lax.ppermute(value, "c", [(0, 1), (1, 0)])


def pick(value, index):
    return lax.dynamic_index_in_dim(value, index, 0, keepdims=False)


def split3(value):
    high = lax.reduce_precision(value, 8, 7)
    rest = value - high
    middle = lax.reduce_precision(rest, 8, 7)
    low = lax.reduce_precision(rest - middle, 8, 7)
    return jnp.stack([high, middle, low]).astype(BF16)


def join3(rows):
    parts = rows.astype(F32)
    return parts[..., 0, :] + (parts[..., 1, :] + parts[..., 2, :])


def stack3(value):
    high = value.astype(BF16).astype(F32)
    rest = value - high
    middle = rest.astype(BF16).astype(F32)
    return jnp.concatenate([high, middle, rest - middle], axis=0).astype(BF16)


def sum_rows(value):
    return value[0:1] + (value[1:2] + value[2:3])


def in_lanes(blocks, first, count):
    return jnp.concatenate([blocks[first + i : first + i + 1] for i in range(count)], axis=1)


def in_rows(row, count):
    width = row.shape[1] // count
    return [row[:, i * width : (i + 1) * width] for i in range(count)]


def start_kernel(
    core_ref, x_hbm, y_hbm, q_hbm, r_hbm, keep_ref, give_ref, cast_ref,
    x_ref, y_ref, q_ref, r_ref, sems,
):
    pieces = sems.shape[1]
    copies = []
    for i, (source, target) in enumerate(
        ((x_hbm, x_ref), (q_hbm, q_ref), (y_hbm, y_ref), (r_hbm, r_ref))
    ):
        size = source.shape[0] // pieces
        for k in range(pieces):
            part = pl.ds(k * size, size)
            copies.append(pltpu.make_async_copy(source.at[part], target.at[part], sems.at[i, k]))
    for copy in copies:
        copy.start()
    chunks, _, share, width = keep_ref.shape
    half = x_ref.shape[1] // 2
    rows = []
    for side, (emb_ref, factor_ref) in enumerate(((x_ref, q_ref), (y_ref, r_ref))):
        for copy in copies[2 * side * pieces : 2 * (side + 1) * pieces]:
            copy.wait()
        factor = factor_ref[...]
        rounded = factor.astype(BF16)
        cast_ref[side] = rounded
        for position, out_ref in ((core_ref[0], keep_ref), (1 - core_ref[0], give_ref)):
            emb = emb_ref[:, pl.ds(pl.multiple_of(position * half, half), half)]
            cross = contract_rows(emb, rounded)
            for chunk in range(chunks):
                out_ref[chunk, side] = cross[chunk * share : (chunk + 1) * share]
        norms = jnp.sum(jnp.square(emb_ref[...].astype(F32)), axis=1, keepdims=True)
        rows.append(jnp.sum(norms * factor, axis=0, keepdims=True))
        rows.append(jnp.sum(factor, axis=0, keepdims=True))
    vec = jnp.concatenate(rows, axis=0)
    for out_ref in (keep_ref, give_ref):
        out_ref[:, 2] = jnp.broadcast_to(vec[None], (chunks, 4, width))


def chunk_kernel(got_ref, g_ref, sent_ref):
    summed = jnp.sum(got_ref[...], axis=0)
    xq, yr = summed[0], summed[1]
    dot = jnp.sum(xq * yr, axis=0, keepdims=True)
    nothing = jnp.zeros((2, dot.shape[1]), F32)
    chunk = jnp.concatenate([xq, yr, summed[2], dot, g_ref[...], nothing], axis=0)
    sent_ref[...] = jnp.broadcast_to(chunk[None], sent_ref.shape)


def spread_kernel(got_ref, sent_ref, vec_ref):
    every = jnp.concatenate([got_ref[i] for i in range(got_ref.shape[0])], axis=1)
    dot = every[12:13]
    high = dot.astype(BF16).astype(F32)
    rest = dot - high
    middle = rest.astype(BF16).astype(F32)
    nothing = jnp.zeros((5, dot.shape[1]), F32)
    chunk = jnp.concatenate([every[:8], high, middle, rest - middle, nothing], axis=0)
    sent_ref[...] = jnp.broadcast_to(chunk.astype(BF16)[None], sent_ref.shape)
    vec_ref[...] = every[8:16]


def grad_kernel(
    core_ref, here_ref, x_ref, y_ref, mine_ref, other_ref, vec_ref, mass_ref, mass2_ref, *refs
):
    factors = refs[:-6]
    grad_q_ref, grad_r_ref, grad_g_ref, peak_ref, all_ref, masses_ref = refs[-6:]
    masses_ref[...] = jnp.concatenate([mass_ref[...], mass2_ref[...]], axis=0)
    ranks = len(factors)
    rows, width = factors[0].shape[1:]

    def lanes_of(block):
        return pl.ds(pl.multiple_of(block * width, width), width)

    for shift, factor_ref in enumerate(factors):
        lanes = lanes_of(lax.rem(here_ref[0] + ranks - shift, ranks))
        for side in range(2):
            all_ref[pl.ds(side * rows, rows), lanes] = factor_ref[side]
    half = x_ref.shape[1] // 2
    chunks = mine_ref.shape[0]
    core = core_ref[0]
    g = vec_ref[5:6]
    scale = SCALE / g
    place = lax.broadcasted_iota(jnp.int32, (half, chunks), 1)
    wanted = lax.broadcasted_iota(jnp.int32, (half, chunks), 0)
    wanted = (wanted // 4) * 16 + wanted % 4
    place8 = lax.broadcasted_iota(jnp.int32, (8, chunks), 1) % 16
    is_dot = jnp.where((place8 >= 8) & (place8 < 11), 1.0, 0.0).astype(BF16)
    spread = jnp.dot(is_dot, mine_ref[...], preferred_element_type=F32) + jnp.dot(
        is_dot, other_ref[...], preferred_element_type=F32
    )
    xq, cq, yr, cr = (vec_ref[i : i + 1] for i in range(4))
    curvature = SCALE * (xq * cr + cq * yr - 2.0 * spread[0:1])
    grad_g = -curvature / jnp.square(g)
    grad_g_ref[...] = grad_g
    top = jnp.abs(grad_g)
    for emb_ref, offset, count, total, out_ref in (
        (x_ref, 4, cr, yr, grad_q_ref),
        (y_ref, 0, cq, xq, grad_r_ref),
    ):
        select = jnp.where(place == wanted + offset, 1.0, 0.0).astype(BF16)
        product = None
        for position, cross_ref in ((core, mine_ref), (1 - core, other_ref)):
            rows = jnp.dot(select, cross_ref[...], preferred_element_type=F32).astype(BF16)
            emb = emb_ref[:, pl.ds(pl.multiple_of(position * half, half), half)]
            part = jnp.dot(emb, rows, preferred_element_type=F32)
            product = part if product is None else product + part
        norms = jnp.sum(jnp.square(emb_ref[...].astype(F32)), axis=1, keepdims=True)
        grad = scale * (norms * count + total - 2.0 * product)
        out_ref[...] = grad
        top = jnp.maximum(top, jnp.max(jnp.abs(grad), axis=0, keepdims=True))
    blocks = in_rows(top, top.shape[1] // peak_ref.shape[2])
    peak = blocks[0]
    for block in blocks[1:]:
        peak = jnp.maximum(peak, block)
    peak_ref[...] = jnp.broadcast_to(peak[None], peak_ref.shape)


def kern_kernel(
    here_ref, peak_ref, grad_q_ref, grad_r_ref, grad_g_ref, vec_ref, all_ref,
    kern_ref, log_ref, eta_ref, own_q_ref, own_r_ref,
):
    rows = grad_q_ref.shape[0]
    width = own_q_ref.shape[1]
    mine = pl.ds(pl.multiple_of(here_ref[0] * width, width), width)
    own_q_ref[...] = grad_q_ref[:, mine]
    own_r_ref[...] = grad_r_ref[:, mine]
    peak = jnp.max(jnp.max(peak_ref[...], axis=0), axis=1, keepdims=True)
    eta = GAMMA / (peak + 1e-06)
    eta_ref[...] = jnp.broadcast_to(eta, eta_ref.shape)
    kern_g = vec_ref[5:6] * jnp.exp(-eta * grad_g_ref[...])
    log_ref[...] = jnp.concatenate(in_rows(jnp.log(kern_g), log_ref.shape[0]), axis=0)
    for side, grad_ref in enumerate((grad_q_ref, grad_r_ref)):
        part = pl.ds(side * rows, rows)
        kern = all_ref[part, :].astype(F32) * jnp.exp(-eta * grad_ref[...])
        kern_ref[part, :] = kern.astype(BF16)


def new_scalings(ranks, got_ref, v_ref, log_ref):
    t = jnp.sum(got_ref[...].astype(F32), axis=0)
    passed = jnp.log(v_ref[...] * t)
    weights = jnp.exp((log_ref[...] + passed[:ranks] + passed[ranks:]) / 3.0)
    return jnp.concatenate([weights, weights], axis=0) / t, weights


def send_columns(v, mass_ref, own_ref, other_ref, sent_ref, u_ref=None):
    ranks = v.shape[0] // 2
    rows = own_ref.shape[0] // 2

    def kern(member, side):
        return (own_ref, other_ref)[member][pl.ds(side * rows, rows), :]

    v_rows = [stack3(in_lanes(v, side * ranks, ranks)) for side in range(2)]
    sums = []
    for member in range(2):
        for side in range(2):
            part = lax.dot_general(
                v_rows[side], kern(member, side), (((1,), (1,)), ((), ())),
                preferred_element_type=F32,
            )
            sums.append(sum_rows(part))
    u = jnp.exp(POWER * jnp.log(mass_ref[...] / jnp.concatenate(sums, axis=0)))
    if u_ref is not None:
        u_ref[...] = u
    columns = []
    for side in range(2):
        total = None
        for member in range(2):
            row = 2 * member + side
            part = jnp.dot(
                stack3(u[row : row + 1]), kern(member, side), preferred_element_type=F32
            )
            total = part if total is None else total + part
        columns += in_rows(sum_rows(total), ranks)
    part = jnp.concatenate(columns, axis=0).astype(sent_ref.dtype)
    sent_ref[...] = jnp.broadcast_to(part[None], sent_ref.shape)


def first_pass(mass_ref, own_ref, other_ref, sent_ref):
    ones = jnp.ones(sent_ref.shape[1:], F32)
    send_columns(ones, mass_ref, own_ref, other_ref, sent_ref)


def next_pass(
    got_ref, v_ref, log_ref, mass_ref, own_ref, other_ref, sent_ref, new_ref, u_ref=None
):
    v, _ = new_scalings(log_ref.shape[0], got_ref, v_ref, log_ref)
    new_ref[...] = v
    send_columns(v, mass_ref, own_ref, other_ref, sent_ref, u_ref)


def profile_kernel(
    core_ref, got_ref, v_ref, log_ref, u_ref, own_ref, other_ref, expr_ref, more_ref,
    part_ref, new_ref, weights_ref,
):
    ranks = log_ref.shape[0]
    rows = own_ref.shape[0] // 2
    half = own_ref.shape[1] // 2
    v, weights = new_scalings(ranks, got_ref, v_ref, log_ref)
    new_ref[...] = v
    weights_ref[...] = weights
    u_columns = jnp.concatenate([u_ref[...], u_ref[...]], axis=0).T
    core = core_ref[0]
    blocks = [new_ref[pl.ds(ranks + core * (ranks // 2) + i, 1), :] for i in range(ranks // 2)]
    scale = jnp.concatenate(blocks, axis=1)
    lanes = pl.ds(pl.multiple_of(core * half, half), half)
    total = None
    for member, (kern_ref, cells_ref) in enumerate(((own_ref, expr_ref), (other_ref, more_ref))):
        kern = kern_ref[pl.ds(rows, rows), lanes].astype(F32)
        column = u_columns[:, 2 * member + 1 : 2 * member + 2]
        part = contract_rows((kern * scale * column).astype(BF16), cells_ref[...])
        total = part if total is None else total + part
    part_ref[...] = total


def on_chip(kernel, shapes, name, scalars=0, inputs=0, off_chip=0, scratch=(), limit=LIMIT):
    specs = {}
    if scalars:
        specs["in_specs"] = (
            [pl.BlockSpec(memory_space=pltpu.SMEM)] * scalars
            + [pl.BlockSpec(memory_space=pltpu.VMEM)] * inputs
            + [pl.BlockSpec(memory_space=pltpu.HBM)] * off_chip
        )
    return pl.pallas_call(
        kernel,
        out_shape=tuple(jax.ShapeDtypeStruct(shape, dtype) for shape, dtype in shapes),
        scratch_shapes=scratch,
        **specs,
        compiler_params=pltpu.CompilerParams(vmem_limit_bytes=limit),
        name=name,
    )


def shards(x_emb, y_emb, q_factor, r_factor, g_weights, a_mass, b_mass, expr):
    rows, width = q_factor.shape
    dim = x_emb.shape[1]
    genes = expr.shape[1]
    others = lax.axis_size(CHIPS)
    cell_devices = 2 * others
    ranks = lax.axis_size("x")
    cells_total = rows * cell_devices
    share = dim // cell_devices

    here = lax.axis_index("x")
    core = lax.axis_index("c")
    core_index = core.astype(jnp.int32)[None]
    chunk_shape = ((others, 3, share, width), F32)
    keep, give, rounded = on_chip(
        start_kernel,
        (chunk_shape, chunk_shape, ((2, rows, width), BF16)),
        "start",
        scalars=1,
        off_chip=4,
        limit=60 << 20,
        scratch=[
            pltpu.VMEM(x_emb.shape, BF16),
            pltpu.VMEM(y_emb.shape, BF16),
            pltpu.VMEM(q_factor.shape, F32),
            pltpu.VMEM(r_factor.shape, F32),
            pltpu.SemaphoreType.DMA((4, 2)),
        ],
    )(core_index, x_emb, y_emb, q_factor, r_factor)

    def from_shift(shift):
        return lax.ppermute(rounded, "x", [(i, (i + shift) % ranks) for i in range(ranks)])

    outgoing = keep + swap(give)
    columns = ranks * width
    tall = ((rows, columns), F32)
    sent = on_chip(chunk_kernel, (((ranks, 16, width), F32),), "chunk")(
        exchange(outgoing, CHIPS), g_weights[None]
    )[0]
    masses = jnp.stack([a_mass, b_mass])
    got, first, second, third, their_masses = lax.optimization_barrier(
        (exchange(sent, "x"), from_shift(1), from_shift(2), from_shift(3), swap(masses))
    )
    sent, vec = on_chip(
        spread_kernel, (((others, 16, columns), BF16), ((8, columns), F32)), "spread"
    )(got)
    crosses, other_expr = lax.optimization_barrier((exchange(sent, CHIPS), swap(expr)))
    crosses = crosses.reshape(others * 16, columns)
    own_grad = ((rows, width), F32)
    grad_q, grad_r, grad_g, peak, factors, masses = on_chip(
        grad_kernel,
        (
            tall, tall, ((1, columns), F32), ((cell_devices, 1, width), F32),
            ((2 * rows, columns), BF16), ((4, rows), F32),
        ),
        "grad",
        scalars=2,
        inputs=7 + ranks,
    )(
        core_index, here.astype(jnp.int32)[None], x_emb, y_emb, crosses, swap(crosses), vec,
        masses, their_masses, rounded, first, second, third,
    )
    kerns, log_g, eta, own_grad_q, own_grad_r = on_chip(
        kern_kernel,
        (((2 * rows, columns), BF16), ((ranks, width), F32), ((1, width), F32), own_grad, own_grad),
        "kern",
        scalars=1,
        inputs=6,
    )(
        here.astype(jnp.int32)[None], exchange(peak, CELLS), grad_q, grad_r, grad_g, vec, factors
    )
    theirs = swap(kerns)
    sent_shape = ((others, 2 * ranks, width), BF16)
    u_shape = ((4, rows), F32)
    v_shape = ((2 * ranks, width), F32)
    sent = on_chip(first_pass, (sent_shape,), "first_pass")(masses, kerns, theirs)[0]
    v = jnp.ones(v_shape[0], F32)
    for step in range(1, PASSES):
        last = (u_shape,) if step == PASSES - 1 else ()
        sent, v, *u = on_chip(next_pass, (sent_shape, v_shape) + last, "next_pass")(
            exchange(sent, CHIPS), v, log_g, masses, kerns, theirs
        )
    (u,) = u
    part, v, weights = on_chip(
        profile_kernel,
        (((ranks * width // 2, genes), F32), v_shape, ((ranks, width), F32)),
        "profile",
        scalars=1,
        inputs=8,
    )(
        core_index, exchange(sent, CHIPS), v, log_g, u, kerns, theirs,
        expr, other_expr,
    )
    v_q, v_r = v[:ranks], v[ranks:]
    kern_q = q_factor * jnp.exp(-eta * own_grad_q)
    kern_r = r_factor * jnp.exp(-eta * own_grad_r)
    q_new = u[0][:, None] * kern_q * pick(v_q, here)[None, :]
    r_new = u[1][:, None] * kern_r * pick(v_r, here)[None, :]
    mine_q = kerns[:rows].astype(F32)
    s_q = jnp.sum(mine_q * v_q.reshape(1, columns), axis=1)
    scaled = (mine_q * (v_q / weights).reshape(1, columns)).astype(BF16)

    piece = jnp.sum(exchange(part.reshape(others, -1, genes), CHIPS), axis=0)
    mine = to_all(piece.astype(BF16), CHIPS).reshape(columns // 2, genes)
    half = columns // 2
    mixed = jnp.dot(
        lax.dynamic_slice_in_dim(scaled, core * half, half, 1), mine, preferred_element_type=F32
    ) + jnp.dot(
        lax.dynamic_slice_in_dim(scaled, (1 - core) * half, half, 1),
        swap(mine),
        preferred_element_type=F32,
    )
    predicted = (mixed / s_q[:, None]).astype(BF16)
    return (q_new, r_new, pick(weights, here) / cells_total, predicted)


def solution(mesh):
    named = Mesh(mesh.devices.reshape(4, 8, 2, 4), EVERY)
    block = P(CELLS, "x")
    return jax.shard_map(
        shards,
        mesh=named,
        in_specs=(
            P(CELLS, None),
            P(CELLS, None),
            block,
            block,
            P("x"),
            P(CELLS),
            P(CELLS),
            block,
        ),
        out_specs=(block, block, P("x"), block),
        check_vma=False,
    )
```

```python
import jax
import jax.numpy as jnp
from jax import lax
from jax.experimental import pallas as pl
from jax.experimental.pallas import tpu as pltpu
from jax.sharding import Mesh
from jax.sharding import PartitionSpec as P

PASSES = 10
SCALE = 0.0625
GAMMA = 10.0
POWER = 0.8
LIMIT = 12 << 20

CHIPS = ("y", "z")
CELLS = ("y", "z", "c")
EVERY = ("y", "z", "c", "x")
F32 = jnp.float32
BF16 = jnp.bfloat16


def contract_rows(left, right):
    return lax.dot_general(
        left, right, (((0,), (0,)), ((), ())), preferred_element_type=F32
    )


def exchange(chunks, axes):
    return lax.all_to_all(chunks, axes, 0, 0, tiled=False)


def to_all(value, axes):
    count = lax.axis_size(axes)
    return exchange(jnp.broadcast_to(value[None], (count,) + value.shape), axes)


def swap(value):
    return lax.ppermute(value, "c", [(0, 1), (1, 0)])


def pick(value, index):
    return lax.dynamic_index_in_dim(value, index, 0, keepdims=False)


def split3(value):
    high = lax.reduce_precision(value, 8, 7)
    rest = value - high
    middle = lax.reduce_precision(rest, 8, 7)
    low = lax.reduce_precision(rest - middle, 8, 7)
    return jnp.stack([high, middle, low]).astype(BF16)


def join3(rows):
    parts = rows.astype(F32)
    return parts[..., 0, :] + (parts[..., 1, :] + parts[..., 2, :])


def stack3(value):
    high = value.astype(BF16).astype(F32)
    rest = value - high
    middle = rest.astype(BF16).astype(F32)
    return jnp.concatenate([high, middle, rest - middle], axis=0).astype(BF16)


def sum_rows(value):
    return value[0:1] + (value[1:2] + value[2:3])


def in_lanes(blocks, first, count):
    return jnp.concatenate([blocks[first + i : first + i + 1] for i in range(count)], axis=1)


def in_rows(row, count):
    width = row.shape[1] // count
    return [row[:, i * width : (i + 1) * width] for i in range(count)]


def start_kernel(
    core_ref, x_hbm, y_hbm, q_hbm, r_hbm, keep_ref, give_ref, cast_ref,
    x_ref, y_ref, q_ref, r_ref, sems,
):
    pieces = sems.shape[1]
    copies = []
    for i, (source, target) in enumerate(
        ((x_hbm, x_ref), (q_hbm, q_ref), (y_hbm, y_ref), (r_hbm, r_ref))
    ):
        size = source.shape[0] // pieces
        for k in range(pieces):
            part = pl.ds(k * size, size)
            copies.append(pltpu.make_async_copy(source.at[part], target.at[part], sems.at[i, k]))
    for copy in copies:
        copy.start()
    chunks, _, share, width = keep_ref.shape
    half = x_ref.shape[1] // 2
    rows = []
    for side, (emb_ref, factor_ref) in enumerate(((x_ref, q_ref), (y_ref, r_ref))):
        for copy in copies[2 * side * pieces : 2 * (side + 1) * pieces]:
            copy.wait()
        factor = factor_ref[...]
        rounded = factor.astype(BF16)
        cast_ref[side] = rounded
        for position, out_ref in ((core_ref[0], keep_ref), (1 - core_ref[0], give_ref)):
            emb = emb_ref[:, pl.ds(pl.multiple_of(position * half, half), half)]
            cross = contract_rows(emb, rounded)
            for chunk in range(chunks):
                out_ref[chunk, side] = cross[chunk * share : (chunk + 1) * share]
        norms = jnp.sum(jnp.square(emb_ref[...].astype(F32)), axis=1, keepdims=True)
        rows.append(jnp.sum(norms * factor, axis=0, keepdims=True))
        rows.append(jnp.sum(factor, axis=0, keepdims=True))
    vec = jnp.concatenate(rows, axis=0)
    for out_ref in (keep_ref, give_ref):
        out_ref[:, 2] = jnp.broadcast_to(vec[None], (chunks, 4, width))


def chunk_kernel(got_ref, g_ref, sent_ref):
    summed = jnp.sum(got_ref[...], axis=0)
    xq, yr = summed[0], summed[1]
    dot = jnp.sum(xq * yr, axis=0, keepdims=True)
    nothing = jnp.zeros((2, dot.shape[1]), F32)
    chunk = jnp.concatenate([xq, yr, summed[2], dot, g_ref[...], nothing], axis=0)
    sent_ref[...] = jnp.broadcast_to(chunk[None], sent_ref.shape)


def spread_kernel(got_ref, sent_ref, vec_ref, dot_ref):
    ranks = got_ref.shape[0]
    every = jnp.concatenate([got_ref[i] for i in range(ranks)], axis=1)
    sent_ref[...] = jnp.broadcast_to(every[:8].astype(BF16)[None], sent_ref.shape)
    vec_ref[...] = every[8:16]
    dot_ref[...] = jnp.concatenate([got_ref[i, 12:13] for i in range(ranks)], axis=0)


def grad_kernel(
    core_ref, here_ref, x_ref, y_ref, mine_ref, other_ref, vec_ref, dot_ref, mass_ref, mass2_ref,
    *refs
):
    factors = refs[:-5]
    grad_q_ref, grad_r_ref, peak_ref, all_ref, masses_ref = refs[-5:]
    masses_ref[...] = jnp.concatenate([mass_ref[...], mass2_ref[...]], axis=0)
    ranks = len(factors)
    rows, width = factors[0].shape[1:]

    def lanes_of(block):
        return pl.ds(pl.multiple_of(block * width, width), width)

    for shift, factor_ref in enumerate(factors):
        lanes = lanes_of(lax.rem(here_ref[0] + ranks - shift, ranks))
        for side in range(2):
            all_ref[pl.ds(side * rows, rows), lanes] = factor_ref[side]
    half = x_ref.shape[1] // 2
    chunks = mine_ref.shape[0]
    core = core_ref[0]
    g = vec_ref[5:6]
    scale = SCALE / g
    place = lax.broadcasted_iota(jnp.int32, (half, chunks), 1)
    wanted = lax.broadcasted_iota(jnp.int32, (half, chunks), 0)
    wanted = (wanted // 4) * 8 + wanted % 4
    xq, cq, yr, cr = (vec_ref[i : i + 1] for i in range(4))
    top = None
    for emb_ref, offset, count, total, out_ref in (
        (x_ref, 4, cr, yr, grad_q_ref),
        (y_ref, 0, cq, xq, grad_r_ref),
    ):
        select = jnp.where(place == wanted + offset, 1.0, 0.0).astype(BF16)
        product = None
        for position, cross_ref in ((core, mine_ref), (1 - core, other_ref)):
            rows = jnp.dot(select, cross_ref[...], preferred_element_type=F32).astype(BF16)
            emb = emb_ref[:, pl.ds(pl.multiple_of(position * half, half), half)]
            part = jnp.dot(emb, rows, preferred_element_type=F32)
            product = part if product is None else product + part
        norms = jnp.sum(jnp.square(emb_ref[...].astype(F32)), axis=1, keepdims=True)
        grad = scale * (norms * count + total - 2.0 * product)
        out_ref[...] = grad
        here = jnp.max(jnp.abs(grad), axis=0, keepdims=True)
        top = here if top is None else jnp.maximum(top, here)
    blocks = in_rows(top, dot_ref.shape[0])
    peak = blocks[0]
    for block in blocks[1:]:
        peak = jnp.maximum(peak, block)
    count = peak_ref.shape[0]
    peak_ref[:, 0] = jnp.broadcast_to(peak[None], (count,) + peak.shape)
    for i in range(dot_ref.shape[0]):
        row = dot_ref[i : i + 1]
        peak_ref[:, 1 + i] = jnp.broadcast_to(row[None], (count,) + row.shape)


def kern_kernel(
    here_ref, peak_ref, grad_q_ref, grad_r_ref, vec_ref, all_ref,
    kern_ref, log_ref, eta_ref, own_q_ref, own_r_ref,
):
    rows = grad_q_ref.shape[0]
    width = own_q_ref.shape[1]
    mine = pl.ds(pl.multiple_of(here_ref[0] * width, width), width)
    own_q_ref[...] = grad_q_ref[:, mine]
    own_r_ref[...] = grad_r_ref[:, mine]
    xq, cq, yr, cr = (vec_ref[i : i + 1] for i in range(4))
    g = vec_ref[5:6]
    dots = [jnp.sum(peak_ref[:, 1 + i], axis=0) for i in range(log_ref.shape[0])]
    dot = jnp.concatenate(dots, axis=1)
    grad_g = -(SCALE * (xq * cr + cq * yr - 2.0 * dot)) / jnp.square(g)
    peak = jnp.maximum(
        jnp.max(jnp.max(peak_ref[:, 0], axis=0), axis=1, keepdims=True),
        jnp.max(jnp.abs(grad_g), axis=1, keepdims=True),
    )
    eta = GAMMA / (peak + 1e-06)
    eta_ref[...] = jnp.broadcast_to(eta, eta_ref.shape)
    kern_g = g * jnp.exp(-eta * grad_g)
    log_ref[...] = jnp.concatenate(in_rows(jnp.log(kern_g), log_ref.shape[0]), axis=0)
    for side, grad_ref in enumerate((grad_q_ref, grad_r_ref)):
        part = pl.ds(side * rows, rows)
        kern = all_ref[part, :].astype(F32) * jnp.exp(-eta * grad_ref[...])
        kern_ref[part, :] = kern.astype(BF16)


def new_scalings(ranks, got_ref, v_ref, log_ref):
    t = jnp.sum(got_ref[...].astype(F32), axis=0)
    passed = jnp.log(v_ref[...] * t)
    weights = jnp.exp((log_ref[...] + passed[:ranks] + passed[ranks:]) / 3.0)
    return jnp.concatenate([weights, weights], axis=0) / t, weights


def send_columns(v, mass_ref, own_ref, other_ref, sent_ref, u_ref=None):
    ranks = v.shape[0] // 2
    rows = own_ref.shape[0] // 2

    def kern(member, side):
        return (own_ref, other_ref)[member][pl.ds(side * rows, rows), :]

    v_rows = [stack3(in_lanes(v, side * ranks, ranks)) for side in range(2)]
    sums = []
    for member in range(2):
        for side in range(2):
            part = lax.dot_general(
                v_rows[side], kern(member, side), (((1,), (1,)), ((), ())),
                preferred_element_type=F32,
            )
            sums.append(sum_rows(part))
    u = jnp.exp(POWER * jnp.log(mass_ref[...] / jnp.concatenate(sums, axis=0)))
    if u_ref is not None:
        u_ref[...] = u
    columns = []
    for side in range(2):
        total = None
        for member in range(2):
            row = 2 * member + side
            part = jnp.dot(
                stack3(u[row : row + 1]), kern(member, side), preferred_element_type=F32
            )
            total = part if total is None else total + part
        columns += in_rows(sum_rows(total), ranks)
    part = jnp.concatenate(columns, axis=0).astype(sent_ref.dtype)
    sent_ref[...] = jnp.broadcast_to(part[None], sent_ref.shape)


def first_pass(mass_ref, own_ref, other_ref, sent_ref):
    ones = jnp.ones(sent_ref.shape[1:], F32)
    send_columns(ones, mass_ref, own_ref, other_ref, sent_ref)


def next_pass(
    got_ref, v_ref, log_ref, mass_ref, own_ref, other_ref, sent_ref, new_ref, u_ref=None
):
    v, _ = new_scalings(log_ref.shape[0], got_ref, v_ref, log_ref)
    new_ref[...] = v
    send_columns(v, mass_ref, own_ref, other_ref, sent_ref, u_ref)


def profile_kernel(
    core_ref, got_ref, v_ref, log_ref, u_ref, own_ref, other_ref, expr_ref, more_ref,
    part_ref, new_ref, weights_ref,
):
    ranks = log_ref.shape[0]
    rows = own_ref.shape[0] // 2
    half = own_ref.shape[1] // 2
    v, weights = new_scalings(ranks, got_ref, v_ref, log_ref)
    new_ref[...] = v
    weights_ref[...] = weights
    u_columns = jnp.concatenate([u_ref[...], u_ref[...]], axis=0).T
    core = core_ref[0]
    blocks = [new_ref[pl.ds(ranks + core * (ranks // 2) + i, 1), :] for i in range(ranks // 2)]
    scale = jnp.concatenate(blocks, axis=1)
    lanes = pl.ds(pl.multiple_of(core * half, half), half)
    total = None
    for member, (kern_ref, cells_ref) in enumerate(((own_ref, expr_ref), (other_ref, more_ref))):
        kern = kern_ref[pl.ds(rows, rows), lanes].astype(F32)
        column = u_columns[:, 2 * member + 1 : 2 * member + 2]
        part = contract_rows((kern * scale * column).astype(BF16), cells_ref[...])
        total = part if total is None else total + part
    part_ref[...] = total


def on_chip(kernel, shapes, name, scalars=0, inputs=0, off_chip=0, scratch=(), limit=LIMIT):
    specs = {}
    if scalars:
        specs["in_specs"] = (
            [pl.BlockSpec(memory_space=pltpu.SMEM)] * scalars
            + [pl.BlockSpec(memory_space=pltpu.VMEM)] * inputs
            + [pl.BlockSpec(memory_space=pltpu.HBM)] * off_chip
        )
    return pl.pallas_call(
        kernel,
        out_shape=tuple(jax.ShapeDtypeStruct(shape, dtype) for shape, dtype in shapes),
        scratch_shapes=scratch,
        **specs,
        compiler_params=pltpu.CompilerParams(vmem_limit_bytes=limit),
        name=name,
    )


def shards(x_emb, y_emb, q_factor, r_factor, g_weights, a_mass, b_mass, expr):
    rows, width = q_factor.shape
    dim = x_emb.shape[1]
    genes = expr.shape[1]
    others = lax.axis_size(CHIPS)
    cell_devices = 2 * others
    ranks = lax.axis_size("x")
    cells_total = rows * cell_devices
    share = dim // cell_devices

    here = lax.axis_index("x")
    core = lax.axis_index("c")
    core_index = core.astype(jnp.int32)[None]
    chunk_shape = ((others, 3, share, width), F32)
    keep, give, rounded = on_chip(
        start_kernel,
        (chunk_shape, chunk_shape, ((2, rows, width), BF16)),
        "start",
        scalars=1,
        off_chip=4,
        limit=60 << 20,
        scratch=[
            pltpu.VMEM(x_emb.shape, BF16),
            pltpu.VMEM(y_emb.shape, BF16),
            pltpu.VMEM(q_factor.shape, F32),
            pltpu.VMEM(r_factor.shape, F32),
            pltpu.SemaphoreType.DMA((4, 2)),
        ],
    )(core_index, x_emb, y_emb, q_factor, r_factor)

    def from_shift(shift):
        return lax.ppermute(rounded, "x", [(i, (i + shift) % ranks) for i in range(ranks)])

    outgoing = keep + swap(give)
    columns = ranks * width
    tall = ((rows, columns), F32)
    sent = on_chip(chunk_kernel, (((ranks, 16, width), F32),), "chunk")(
        exchange(outgoing, CHIPS), g_weights[None]
    )[0]
    masses = jnp.stack([a_mass, b_mass])
    got, first, second, third, their_masses = lax.optimization_barrier(
        (exchange(sent, "x"), from_shift(1), from_shift(2), from_shift(3), swap(masses))
    )
    sent, vec, dot = on_chip(
        spread_kernel,
        (((others, 8, columns), BF16), ((8, columns), F32), ((ranks, width), F32)),
        "spread",
    )(got)
    crosses, other_expr = lax.optimization_barrier((exchange(sent, CHIPS), swap(expr)))
    crosses = crosses.reshape(others * 8, columns)
    own_grad = ((rows, width), F32)
    grad_q, grad_r, peak, factors, masses = on_chip(
        grad_kernel,
        (
            tall, tall, ((cell_devices, 1 + ranks, 1, width), F32),
            ((2 * rows, columns), BF16), ((4, rows), F32),
        ),
        "grad",
        scalars=2,
        inputs=8 + ranks,
    )(
        core_index, here.astype(jnp.int32)[None], x_emb, y_emb, crosses, swap(crosses), vec,
        dot, masses, their_masses, rounded, first, second, third,
    )
    kerns, log_g, eta, own_grad_q, own_grad_r = on_chip(
        kern_kernel,
        (((2 * rows, columns), BF16), ((ranks, width), F32), ((1, width), F32), own_grad, own_grad),
        "kern",
        scalars=1,
        inputs=5,
    )(
        here.astype(jnp.int32)[None], exchange(peak, CELLS), grad_q, grad_r, vec, factors
    )
    theirs = swap(kerns)
    sent_shape = ((others, 2 * ranks, width), BF16)
    u_shape = ((4, rows), F32)
    v_shape = ((2 * ranks, width), F32)
    sent = on_chip(first_pass, (sent_shape,), "first_pass")(masses, kerns, theirs)[0]
    v = jnp.ones(v_shape[0], F32)
    for step in range(1, PASSES):
        last = (u_shape,) if step == PASSES - 1 else ()
        sent, v, *u = on_chip(next_pass, (sent_shape, v_shape) + last, "next_pass")(
            exchange(sent, CHIPS), v, log_g, masses, kerns, theirs
        )
    (u,) = u
    part, v, weights = on_chip(
        profile_kernel,
        (((ranks * width // 2, genes), F32), v_shape, ((ranks, width), F32)),
        "profile",
        scalars=1,
        inputs=8,
    )(
        core_index, exchange(sent, CHIPS), v, log_g, u, kerns, theirs,
        expr, other_expr,
    )
    v_q, v_r = v[:ranks], v[ranks:]
    kern_q = q_factor * jnp.exp(-eta * own_grad_q)
    kern_r = r_factor * jnp.exp(-eta * own_grad_r)
    q_new = u[0][:, None] * kern_q * pick(v_q, here)[None, :]
    r_new = u[1][:, None] * kern_r * pick(v_r, here)[None, :]
    mine_q = kerns[:rows].astype(F32)
    s_q = jnp.sum(mine_q * v_q.reshape(1, columns), axis=1)
    scaled = (mine_q * (v_q / weights).reshape(1, columns)).astype(BF16)

    piece = jnp.sum(exchange(part.reshape(others, -1, genes), CHIPS), axis=0)
    mine = to_all(piece.astype(BF16), CHIPS).reshape(columns // 2, genes)
    half = columns // 2
    mixed = jnp.dot(
        lax.dynamic_slice_in_dim(scaled, core * half, half, 1), mine, preferred_element_type=F32
    ) + jnp.dot(
        lax.dynamic_slice_in_dim(scaled, (1 - core) * half, half, 1),
        swap(mine),
        preferred_element_type=F32,
    )
    predicted = (mixed / s_q[:, None]).astype(BF16)
    return (q_new, r_new, pick(weights, here) / cells_total, predicted)


def solution(mesh):
    named = Mesh(mesh.devices.reshape(4, 8, 2, 4), EVERY)
    block = P(CELLS, "x")
    return jax.shard_map(
        shards,
        mesh=named,
        in_specs=(
            P(CELLS, None),
            P(CELLS, None),
            block,
            block,
            P("x"),
            P(CELLS),
            P(CELLS),
            block,
        ),
        out_specs=(block, block, P("x"), block),
        check_vma=False,
    )
```

```python
import jax
import jax.numpy as jnp
from jax import lax
from jax.experimental import pallas as pl
from jax.experimental.pallas import tpu as pltpu
from jax.sharding import Mesh
from jax.sharding import PartitionSpec as P

PASSES = 10
SCALE = 0.0625
GAMMA = 10.0
POWER = 0.8
LIMIT = 12 << 20

CHIPS = ("y", "z")
CELLS = ("y", "z", "c")
EVERY = ("y", "z", "c", "x")
F32 = jnp.float32
BF16 = jnp.bfloat16


def contract_rows(left, right):
    return lax.dot_general(
        left, right, (((0,), (0,)), ((), ())), preferred_element_type=F32
    )


def exchange(chunks, axes):
    return lax.all_to_all(chunks, axes, 0, 0, tiled=False)


def to_all(value, axes):
    count = lax.axis_size(axes)
    return exchange(jnp.broadcast_to(value[None], (count,) + value.shape), axes)


def swap(value):
    return lax.ppermute(value, "c", [(0, 1), (1, 0)])


def pick(value, index):
    return lax.dynamic_index_in_dim(value, index, 0, keepdims=False)


def split3(value):
    high = lax.reduce_precision(value, 8, 7)
    rest = value - high
    middle = lax.reduce_precision(rest, 8, 7)
    low = lax.reduce_precision(rest - middle, 8, 7)
    return jnp.stack([high, middle, low]).astype(BF16)


def join3(rows):
    parts = rows.astype(F32)
    return parts[..., 0, :] + (parts[..., 1, :] + parts[..., 2, :])


def stack3(value):
    high = value.astype(BF16).astype(F32)
    rest = value - high
    middle = rest.astype(BF16).astype(F32)
    return jnp.concatenate([high, middle, rest - middle], axis=0).astype(BF16)


def sum_rows(value):
    return value[0:1] + (value[1:2] + value[2:3])


def in_lanes(blocks, first, count):
    return jnp.concatenate([blocks[first + i : first + i + 1] for i in range(count)], axis=1)


def in_rows(row, count):
    width = row.shape[1] // count
    return [row[:, i * width : (i + 1) * width] for i in range(count)]


def start_kernel(
    core_ref, x_hbm, y_hbm, q_hbm, r_hbm, keep_ref, give_ref, cast_ref,
    x_ref, y_ref, q_ref, r_ref, sems,
):
    pieces = sems.shape[1]
    copies = []
    for i, (source, target) in enumerate(
        ((x_hbm, x_ref), (q_hbm, q_ref), (y_hbm, y_ref), (r_hbm, r_ref))
    ):
        size = source.shape[0] // pieces
        for k in range(pieces):
            part = pl.ds(k * size, size)
            copies.append(pltpu.make_async_copy(source.at[part], target.at[part], sems.at[i, k]))
    for copy in copies:
        copy.start()
    chunks, _, share, width = keep_ref.shape
    half = x_ref.shape[1] // 2
    rows = []
    for side, (emb_ref, factor_ref) in enumerate(((x_ref, q_ref), (y_ref, r_ref))):
        for copy in copies[2 * side * pieces : 2 * (side + 1) * pieces]:
            copy.wait()
        factor = factor_ref[...]
        rounded = factor.astype(BF16)
        cast_ref[side] = rounded
        for position, out_ref in ((core_ref[0], keep_ref), (1 - core_ref[0], give_ref)):
            emb = emb_ref[:, pl.ds(pl.multiple_of(position * half, half), half)]
            cross = contract_rows(emb, rounded)
            for chunk in range(chunks):
                out_ref[chunk, side] = cross[chunk * share : (chunk + 1) * share]
        norms = jnp.sum(jnp.square(emb_ref[...].astype(F32)), axis=1, keepdims=True)
        rows.append(jnp.sum(norms * factor, axis=0, keepdims=True))
        rows.append(jnp.sum(factor, axis=0, keepdims=True))
    vec = jnp.concatenate(rows, axis=0)
    for out_ref in (keep_ref, give_ref):
        out_ref[:, 2] = jnp.broadcast_to(vec[None], (chunks, 4, width))


def chunk_kernel(got_ref, g_ref, sent_ref):
    summed = jnp.sum(got_ref[...], axis=0)
    xq, yr = summed[0], summed[1]
    dot = jnp.sum(xq * yr, axis=0, keepdims=True)
    nothing = jnp.zeros((2, dot.shape[1]), F32)
    chunk = jnp.concatenate([xq, yr, summed[2], dot, g_ref[...], nothing], axis=0)
    sent_ref[...] = jnp.broadcast_to(chunk[None], sent_ref.shape)


def spread_kernel(got_ref, sent_ref, vec_ref, dot_ref):
    ranks = got_ref.shape[0]
    every = jnp.concatenate([got_ref[i] for i in range(ranks)], axis=1)
    sent_ref[...] = jnp.broadcast_to(every[:8].astype(BF16)[None], sent_ref.shape)
    vec_ref[...] = every[8:16]
    dot_ref[...] = jnp.concatenate([got_ref[i, 12:13] for i in range(ranks)], axis=0)


def grad_kernel(
    core_ref, here_ref, x_ref, y_ref, mine_ref, other_ref, vec_ref, dot_ref, mass_ref, mass2_ref,
    *refs
):
    factors = refs[:-5]
    grad_q_ref, grad_r_ref, peak_ref, all_ref, masses_ref = refs[-5:]
    masses_ref[...] = jnp.concatenate([mass_ref[...], mass2_ref[...]], axis=0)
    ranks = len(factors)
    rows, width = factors[0].shape[1:]

    def lanes_of(block):
        return pl.ds(pl.multiple_of(block * width, width), width)

    for shift, factor_ref in enumerate(factors):
        lanes = lanes_of(lax.rem(here_ref[0] + ranks - shift, ranks))
        for side in range(2):
            all_ref[pl.ds(side * rows, rows), lanes] = factor_ref[side]
    half = x_ref.shape[1] // 2
    chunks = mine_ref.shape[0]
    core = core_ref[0]
    g = vec_ref[5:6]
    scale = SCALE / g
    place = lax.broadcasted_iota(jnp.int32, (half, chunks), 1)
    wanted = lax.broadcasted_iota(jnp.int32, (half, chunks), 0)
    wanted = (wanted // 4) * 8 + wanted % 4
    xq, cq, yr, cr = (vec_ref[i : i + 1] for i in range(4))
    top = None
    for emb_ref, offset, count, total, out_ref in (
        (x_ref, 4, cr, yr, grad_q_ref),
        (y_ref, 0, cq, xq, grad_r_ref),
    ):
        select = jnp.where(place == wanted + offset, 1.0, 0.0).astype(BF16)
        product = None
        for position, cross_ref in ((core, mine_ref), (1 - core, other_ref)):
            rows = jnp.dot(select, cross_ref[...], preferred_element_type=F32).astype(BF16)
            emb = emb_ref[:, pl.ds(pl.multiple_of(position * half, half), half)]
            part = jnp.dot(emb, rows, preferred_element_type=F32)
            product = part if product is None else product + part
        norms = jnp.sum(jnp.square(emb_ref[...].astype(F32)), axis=1, keepdims=True)
        grad = scale * (norms * count + total - 2.0 * product)
        out_ref[...] = grad
        here = jnp.max(jnp.abs(grad), axis=0, keepdims=True)
        top = here if top is None else jnp.maximum(top, here)
    blocks = in_rows(top, dot_ref.shape[0])
    peak = blocks[0]
    for block in blocks[1:]:
        peak = jnp.maximum(peak, block)
    count = peak_ref.shape[0]
    peak_ref[:, 0] = jnp.broadcast_to(peak[None], (count,) + peak.shape)
    for i in range(dot_ref.shape[0]):
        row = dot_ref[i : i + 1]
        peak_ref[:, 1 + i] = jnp.broadcast_to(row[None], (count,) + row.shape)


def kern_kernel(
    here_ref, peak_ref, grad_q_ref, grad_r_ref, vec_ref, all_ref,
    kern_ref, log_ref, eta_ref, own_q_ref, own_r_ref,
):
    rows = grad_q_ref.shape[0]
    width = own_q_ref.shape[1]
    mine = pl.ds(pl.multiple_of(here_ref[0] * width, width), width)
    own_q_ref[...] = grad_q_ref[:, mine]
    own_r_ref[...] = grad_r_ref[:, mine]
    xq, cq, yr, cr = (vec_ref[i : i + 1] for i in range(4))
    g = vec_ref[5:6]
    dots = [jnp.sum(peak_ref[:, 1 + i], axis=0) for i in range(log_ref.shape[0])]
    dot = jnp.concatenate(dots, axis=1)
    grad_g = -(SCALE * (xq * cr + cq * yr - 2.0 * dot)) / jnp.square(g)
    peak = jnp.maximum(
        jnp.max(jnp.max(peak_ref[:, 0], axis=0), axis=1, keepdims=True),
        jnp.max(jnp.abs(grad_g), axis=1, keepdims=True),
    )
    eta = GAMMA / (peak + 1e-06)
    eta_ref[...] = jnp.broadcast_to(eta, eta_ref.shape)
    kern_g = g * jnp.exp(-eta * grad_g)
    log_ref[...] = jnp.concatenate(in_rows(jnp.log(kern_g), log_ref.shape[0]), axis=0)
    for side, grad_ref in enumerate((grad_q_ref, grad_r_ref)):
        part = pl.ds(side * rows, rows)
        kern = all_ref[part, :].astype(F32) * jnp.exp(-eta * grad_ref[...])
        kern_ref[part, :] = kern.astype(BF16)


def new_scalings(ranks, got_ref, v_ref, log_ref):
    t = jnp.sum(got_ref[...].astype(F32), axis=0)
    passed = jnp.log(v_ref[...] * t)
    weights = jnp.exp((log_ref[...] + passed[:ranks] + passed[ranks:]) / 3.0)
    return jnp.concatenate([weights, weights], axis=0) / t, weights


def send_columns(v, mass_ref, own_ref, other_ref, sent_ref, u_ref=None):
    ranks = v.shape[0] // 2
    rows = own_ref.shape[0] // 2

    def kern(member, side):
        return (own_ref, other_ref)[member][pl.ds(side * rows, rows), :]

    v_rows = [stack3(in_lanes(v, side * ranks, ranks)) for side in range(2)]
    sums = []
    for member in range(2):
        for side in range(2):
            part = lax.dot_general(
                v_rows[side], kern(member, side), (((1,), (1,)), ((), ())),
                preferred_element_type=F32,
            )
            sums.append(sum_rows(part))
    u = jnp.exp(POWER * jnp.log(mass_ref[...] / jnp.concatenate(sums, axis=0)))
    if u_ref is not None:
        u_ref[...] = u
    columns = []
    for side in range(2):
        total = None
        for member in range(2):
            row = 2 * member + side
            part = jnp.dot(
                stack3(u[row : row + 1]), kern(member, side), preferred_element_type=F32
            )
            total = part if total is None else total + part
        columns += in_rows(sum_rows(total), ranks)
    part = jnp.concatenate(columns, axis=0).astype(sent_ref.dtype)
    sent_ref[...] = jnp.broadcast_to(part[None], sent_ref.shape)


def first_pass(mass_ref, own_ref, other_ref, sent_ref):
    ones = jnp.ones(sent_ref.shape[1:], F32)
    send_columns(ones, mass_ref, own_ref, other_ref, sent_ref)


def next_pass(
    got_ref, v_ref, log_ref, mass_ref, own_ref, other_ref, sent_ref, new_ref, u_ref=None
):
    v, _ = new_scalings(log_ref.shape[0], got_ref, v_ref, log_ref)
    new_ref[...] = v
    send_columns(v, mass_ref, own_ref, other_ref, sent_ref, u_ref)


def profile_kernel(
    core_ref, got_ref, v_ref, log_ref, u_ref, own_ref, other_ref, expr_ref, more_ref,
    part_ref, new_ref, weights_ref,
):
    ranks = log_ref.shape[0]
    rows = own_ref.shape[0] // 2
    half = own_ref.shape[1] // 2
    v, weights = new_scalings(ranks, got_ref, v_ref, log_ref)
    new_ref[...] = v
    weights_ref[...] = weights
    u_columns = jnp.concatenate([u_ref[...], u_ref[...]], axis=0).T
    core = core_ref[0]
    blocks = [new_ref[pl.ds(ranks + core * (ranks // 2) + i, 1), :] for i in range(ranks // 2)]
    scale = jnp.concatenate(blocks, axis=1)
    lanes = pl.ds(pl.multiple_of(core * half, half), half)
    total = None
    for member, (kern_ref, cells_ref) in enumerate(((own_ref, expr_ref), (other_ref, more_ref))):
        kern = kern_ref[pl.ds(rows, rows), lanes].astype(F32)
        column = u_columns[:, 2 * member + 1 : 2 * member + 2]
        part = contract_rows((kern * scale * column).astype(BF16), cells_ref[...])
        total = part if total is None else total + part
    part_ref[...] = total


def on_chip(kernel, shapes, name, scalars=0, inputs=0, off_chip=0, scratch=(), limit=LIMIT):
    specs = {}
    if scalars:
        specs["in_specs"] = (
            [pl.BlockSpec(memory_space=pltpu.SMEM)] * scalars
            + [pl.BlockSpec(memory_space=pltpu.VMEM)] * inputs
            + [pl.BlockSpec(memory_space=pltpu.HBM)] * off_chip
        )
    return pl.pallas_call(
        kernel,
        out_shape=tuple(jax.ShapeDtypeStruct(shape, dtype) for shape, dtype in shapes),
        scratch_shapes=scratch,
        **specs,
        compiler_params=pltpu.CompilerParams(vmem_limit_bytes=limit),
        name=name,
    )


def shards(x_emb, y_emb, q_factor, r_factor, g_weights, a_mass, b_mass, expr):
    rows, width = q_factor.shape
    dim = x_emb.shape[1]
    genes = expr.shape[1]
    others = lax.axis_size(CHIPS)
    cell_devices = 2 * others
    ranks = lax.axis_size("x")
    cells_total = rows * cell_devices
    share = dim // cell_devices

    here = lax.axis_index("x")
    core = lax.axis_index("c")
    core_index = core.astype(jnp.int32)[None]
    chunk_shape = ((others, 3, share, width), F32)
    keep, give, rounded = on_chip(
        start_kernel,
        (chunk_shape, chunk_shape, ((2, rows, width), BF16)),
        "start",
        scalars=1,
        off_chip=4,
        limit=107 << 19,
        scratch=[
            pltpu.VMEM(x_emb.shape, BF16),
            pltpu.VMEM(y_emb.shape, BF16),
            pltpu.VMEM(q_factor.shape, F32),
            pltpu.VMEM(r_factor.shape, F32),
            pltpu.SemaphoreType.DMA((4, 2)),
        ],
    )(core_index, x_emb, y_emb, q_factor, r_factor)

    def from_shift(shift):
        return lax.ppermute(rounded, "x", [(i, (i + shift) % ranks) for i in range(ranks)])

    outgoing = keep + swap(give)
    columns = ranks * width
    tall = ((rows, columns), F32)
    sent = on_chip(chunk_kernel, (((ranks, 16, width), F32),), "chunk")(
        exchange(outgoing, CHIPS), g_weights[None]
    )[0]
    masses = jnp.stack([a_mass, b_mass])
    got, first, second, third, their_masses = lax.optimization_barrier(
        (exchange(sent, "x"), from_shift(1), from_shift(2), from_shift(3), swap(masses))
    )
    sent, vec, dot = on_chip(
        spread_kernel,
        (((others, 8, columns), BF16), ((8, columns), F32), ((ranks, width), F32)),
        "spread",
    )(got)
    crosses, other_expr = lax.optimization_barrier((exchange(sent, CHIPS), swap(expr)))
    crosses = crosses.reshape(others * 8, columns)
    own_grad = ((rows, width), F32)
    grad_q, grad_r, peak, factors, masses = on_chip(
        grad_kernel,
        (
            tall, tall, ((cell_devices, 1 + ranks, 1, width), F32),
            ((2 * rows, columns), BF16), ((4, rows), F32),
        ),
        "grad",
        scalars=2,
        inputs=8 + ranks,
    )(
        core_index, here.astype(jnp.int32)[None], x_emb, y_emb, crosses, swap(crosses), vec,
        dot, masses, their_masses, rounded, first, second, third,
    )
    kerns, log_g, eta, own_grad_q, own_grad_r = on_chip(
        kern_kernel,
        (((2 * rows, columns), BF16), ((ranks, width), F32), ((1, width), F32), own_grad, own_grad),
        "kern",
        scalars=1,
        inputs=5,
    )(
        here.astype(jnp.int32)[None], exchange(peak, CELLS), grad_q, grad_r, vec, factors
    )
    theirs = swap(kerns)
    sent_shape = ((others, 2 * ranks, width), BF16)
    u_shape = ((4, rows), F32)
    v_shape = ((2 * ranks, width), F32)
    sent = on_chip(first_pass, (sent_shape,), "first_pass")(masses, kerns, theirs)[0]
    v = jnp.ones(v_shape[0], F32)
    for step in range(1, PASSES):
        last = (u_shape,) if step == PASSES - 1 else ()
        sent, v, *u = on_chip(next_pass, (sent_shape, v_shape) + last, "next_pass")(
            exchange(sent, CHIPS), v, log_g, masses, kerns, theirs
        )
    (u,) = u
    part, v, weights = on_chip(
        profile_kernel,
        (((ranks * width // 2, genes), F32), v_shape, ((ranks, width), F32)),
        "profile",
        scalars=1,
        inputs=8,
    )(
        core_index, exchange(sent, CHIPS), v, log_g, u, kerns, theirs,
        expr, other_expr,
    )
    v_q, v_r = v[:ranks], v[ranks:]
    kern_q = q_factor * jnp.exp(-eta * own_grad_q)
    kern_r = r_factor * jnp.exp(-eta * own_grad_r)
    q_new = u[0][:, None] * kern_q * pick(v_q, here)[None, :]
    r_new = u[1][:, None] * kern_r * pick(v_r, here)[None, :]
    mine_q = kerns[:rows].astype(F32)
    s_q = jnp.sum(mine_q * v_q.reshape(1, columns), axis=1)
    scaled = (mine_q * (v_q / weights).reshape(1, columns)).astype(BF16)

    piece = jnp.sum(exchange(part.reshape(others, -1, genes), CHIPS), axis=0)
    mine = to_all(piece.astype(BF16), CHIPS).reshape(columns // 2, genes)
    half = columns // 2
    mixed = jnp.dot(
        lax.dynamic_slice_in_dim(scaled, core * half, half, 1), mine, preferred_element_type=F32
    ) + jnp.dot(
        lax.dynamic_slice_in_dim(scaled, (1 - core) * half, half, 1),
        swap(mine),
        preferred_element_type=F32,
    )
    predicted = (mixed / s_q[:, None]).astype(BF16)
    return (q_new, r_new, pick(weights, here) / cells_total, predicted)


def solution(mesh):
    named = Mesh(mesh.devices.reshape(4, 8, 2, 4), EVERY)
    block = P(CELLS, "x")
    return jax.shard_map(
        shards,
        mesh=named,
        in_specs=(
            P(CELLS, None),
            P(CELLS, None),
            block,
            block,
            P("x"),
            P(CELLS),
            P(CELLS),
            block,
        ),
        out_specs=(block, block, P("x"), block),
        check_vma=False,
    )
```

```python
import jax
import jax.numpy as jnp
from jax import lax
from jax.experimental import pallas as pl
from jax.experimental.pallas import tpu as pltpu
from jax.sharding import Mesh
from jax.sharding import PartitionSpec as P

PASSES = 10
SCALE = 0.0625
GAMMA = 10.0
POWER = 0.8
LIMIT = 12 << 20

CHIPS = ("y", "z")
CELLS = ("y", "z", "c")
EVERY = ("y", "z", "c", "x")
F32 = jnp.float32
BF16 = jnp.bfloat16


def contract_rows(left, right):
    return lax.dot_general(
        left, right, (((0,), (0,)), ((), ())), preferred_element_type=F32
    )


def exchange(chunks, axes):
    return lax.all_to_all(chunks, axes, 0, 0, tiled=False)


def to_all(value, axes):
    count = lax.axis_size(axes)
    return exchange(jnp.broadcast_to(value[None], (count,) + value.shape), axes)


def swap(value):
    return lax.ppermute(value, "c", [(0, 1), (1, 0)])


def pick(value, index):
    return lax.dynamic_index_in_dim(value, index, 0, keepdims=False)


def split3(value):
    high = lax.reduce_precision(value, 8, 7)
    rest = value - high
    middle = lax.reduce_precision(rest, 8, 7)
    low = lax.reduce_precision(rest - middle, 8, 7)
    return jnp.stack([high, middle, low]).astype(BF16)


def join3(rows):
    parts = rows.astype(F32)
    return parts[..., 0, :] + (parts[..., 1, :] + parts[..., 2, :])


def stack3(value):
    high = value.astype(BF16).astype(F32)
    rest = value - high
    middle = rest.astype(BF16).astype(F32)
    return jnp.concatenate([high, middle, rest - middle], axis=0).astype(BF16)


def sum_rows(value):
    return value[0:1] + (value[1:2] + value[2:3])


def in_lanes(blocks, first, count):
    return jnp.concatenate([blocks[first + i : first + i + 1] for i in range(count)], axis=1)


def in_rows(row, count):
    width = row.shape[1] // count
    return [row[:, i * width : (i + 1) * width] for i in range(count)]


def start_kernel(
    core_ref, x_hbm, y_hbm, q_hbm, r_hbm, keep_ref, give_ref, cast_ref,
    x_ref, y_ref, q_ref, r_ref, sems,
):
    pieces = sems.shape[1]
    copies = []
    for i, (source, target) in enumerate(
        ((x_hbm, x_ref), (q_hbm, q_ref), (y_hbm, y_ref), (r_hbm, r_ref))
    ):
        size = source.shape[0] // pieces
        for k in range(pieces):
            part = pl.ds(k * size, size)
            copies.append(pltpu.make_async_copy(source.at[part], target.at[part], sems.at[i, k]))
    for copy in copies:
        copy.start()
    chunks, _, share, width = keep_ref.shape
    half = x_ref.shape[1] // 2
    rows = []
    for side, (emb_ref, factor_ref) in enumerate(((x_ref, q_ref), (y_ref, r_ref))):
        for copy in copies[2 * side * pieces : 2 * (side + 1) * pieces]:
            copy.wait()
        factor = factor_ref[...]
        rounded = factor.astype(BF16)
        cast_ref[side] = rounded
        for position, out_ref in ((core_ref[0], keep_ref), (1 - core_ref[0], give_ref)):
            emb = emb_ref[:, pl.ds(pl.multiple_of(position * half, half), half)]
            cross = contract_rows(emb, rounded)
            for chunk in range(chunks):
                out_ref[chunk, side] = cross[chunk * share : (chunk + 1) * share]
        norms = jnp.sum(jnp.square(emb_ref[...].astype(F32)), axis=1, keepdims=True)
        rows.append(jnp.sum(norms * factor, axis=0, keepdims=True))
        rows.append(jnp.sum(factor, axis=0, keepdims=True))
    vec = jnp.concatenate(rows, axis=0)
    for out_ref in (keep_ref, give_ref):
        out_ref[:, 2] = jnp.broadcast_to(vec[None], (chunks, 4, width))


def chunk_kernel(got_ref, g_ref, sent_ref):
    summed = jnp.sum(got_ref[...], axis=0)
    xq, yr = summed[0], summed[1]
    dot = jnp.sum(xq * yr, axis=0, keepdims=True)
    nothing = jnp.zeros((2, dot.shape[1]), F32)
    chunk = jnp.concatenate([xq, yr, summed[2], dot, g_ref[...], nothing], axis=0)
    sent_ref[...] = jnp.broadcast_to(chunk[None], sent_ref.shape)


def spread_kernel(got_ref, sent_ref, vec_ref, dot_ref):
    ranks = got_ref.shape[0]
    every = jnp.concatenate([got_ref[i] for i in range(ranks)], axis=1)
    sent_ref[...] = jnp.broadcast_to(every[:8].astype(BF16)[None], sent_ref.shape)
    vec_ref[...] = every[8:16]
    dot_ref[...] = jnp.concatenate([got_ref[i, 12:13] for i in range(ranks)], axis=0)


def grad_kernel(
    core_ref, here_ref, x_ref, y_ref, mine_ref, other_ref, vec_ref, dot_ref, mass_ref, mass2_ref,
    *refs
):
    factors = refs[:-5]
    grad_q_ref, grad_r_ref, peak_ref, all_ref, masses_ref = refs[-5:]
    masses_ref[...] = jnp.concatenate([mass_ref[...], mass2_ref[...]], axis=0)
    ranks = len(factors)
    rows, width = factors[0].shape[1:]

    def lanes_of(block):
        return pl.ds(pl.multiple_of(block * width, width), width)

    for shift, factor_ref in enumerate(factors):
        lanes = lanes_of(lax.rem(here_ref[0] + ranks - shift, ranks))
        for side in range(2):
            all_ref[pl.ds(side * rows, rows), lanes] = factor_ref[side]
    half = x_ref.shape[1] // 2
    chunks = mine_ref.shape[0]
    core = core_ref[0]
    g = vec_ref[5:6]
    scale = SCALE / g
    place = lax.broadcasted_iota(jnp.int32, (half, chunks), 1)
    wanted = lax.broadcasted_iota(jnp.int32, (half, chunks), 0)
    wanted = (wanted // 4) * 8 + wanted % 4
    xq, cq, yr, cr = (vec_ref[i : i + 1] for i in range(4))
    top = None
    for emb_ref, offset, count, total, out_ref in (
        (x_ref, 4, cr, yr, grad_q_ref),
        (y_ref, 0, cq, xq, grad_r_ref),
    ):
        select = jnp.where(place == wanted + offset, 1.0, 0.0).astype(BF16)
        product = None
        for position, cross_ref in ((core, mine_ref), (1 - core, other_ref)):
            rows = jnp.dot(select, cross_ref[...], preferred_element_type=F32).astype(BF16)
            emb = emb_ref[:, pl.ds(pl.multiple_of(position * half, half), half)]
            part = jnp.dot(emb, rows, preferred_element_type=F32)
            product = part if product is None else product + part
        norms = jnp.sum(jnp.square(emb_ref[...].astype(F32)), axis=1, keepdims=True)
        grad = scale * (norms * count + total - 2.0 * product)
        out_ref[...] = grad
        here = jnp.max(jnp.abs(grad), axis=0, keepdims=True)
        top = here if top is None else jnp.maximum(top, here)
    blocks = in_rows(top, dot_ref.shape[0])
    peak = blocks[0]
    for block in blocks[1:]:
        peak = jnp.maximum(peak, block)
    count = peak_ref.shape[0]
    peak_ref[:, 0] = jnp.broadcast_to(peak[None], (count,) + peak.shape)
    for i in range(dot_ref.shape[0]):
        row = dot_ref[i : i + 1]
        peak_ref[:, 1 + i] = jnp.broadcast_to(row[None], (count,) + row.shape)


def kern_kernel(
    here_ref, peak_ref, grad_q_ref, grad_r_ref, vec_ref, all_ref,
    kern_ref, log_ref, eta_ref, own_q_ref, own_r_ref,
):
    rows = grad_q_ref.shape[0]
    width = own_q_ref.shape[1]
    mine = pl.ds(pl.multiple_of(here_ref[0] * width, width), width)
    own_q_ref[...] = grad_q_ref[:, mine]
    own_r_ref[...] = grad_r_ref[:, mine]
    xq, cq, yr, cr = (vec_ref[i : i + 1] for i in range(4))
    g = vec_ref[5:6]
    dots = [jnp.sum(peak_ref[:, 1 + i], axis=0) for i in range(log_ref.shape[0])]
    dot = jnp.concatenate(dots, axis=1)
    grad_g = -(SCALE * (xq * cr + cq * yr - 2.0 * dot)) / jnp.square(g)
    peak = jnp.maximum(
        jnp.max(jnp.max(peak_ref[:, 0], axis=0), axis=1, keepdims=True),
        jnp.max(jnp.abs(grad_g), axis=1, keepdims=True),
    )
    eta = GAMMA / (peak + 1e-06)
    eta_ref[...] = jnp.broadcast_to(eta, eta_ref.shape)
    kern_g = g * jnp.exp(-eta * grad_g)
    log_ref[...] = jnp.concatenate(in_rows(jnp.log(kern_g), log_ref.shape[0]), axis=0)
    for side, grad_ref in enumerate((grad_q_ref, grad_r_ref)):
        part = pl.ds(side * rows, rows)
        kern = all_ref[part, :].astype(F32) * jnp.exp(-eta * grad_ref[...])
        kern_ref[part, :] = kern.astype(BF16)


def new_scalings(ranks, got_ref, v_ref, log_ref):
    t = jnp.sum(got_ref[...].astype(F32), axis=0)
    passed = jnp.log(v_ref[...] * t)
    weights = jnp.exp((log_ref[...] + passed[:ranks] + passed[ranks:]) / 3.0)
    return jnp.concatenate([weights, weights], axis=0) / t, weights


def send_columns(v, mass_ref, own_ref, other_ref, sent_ref, u_ref=None):
    ranks = v.shape[0] // 2
    rows = own_ref.shape[0] // 2

    def kern(member, side):
        return (own_ref, other_ref)[member][pl.ds(side * rows, rows), :]

    v_rows = [stack3(in_lanes(v, side * ranks, ranks)) for side in range(2)]
    sums = []
    for member in range(2):
        for side in range(2):
            part = lax.dot_general(
                v_rows[side], kern(member, side), (((1,), (1,)), ((), ())),
                preferred_element_type=F32,
            )
            sums.append(sum_rows(part))
    u = jnp.exp(POWER * jnp.log(mass_ref[...] / jnp.concatenate(sums, axis=0)))
    if u_ref is not None:
        u_ref[...] = u
    columns = []
    for side in range(2):
        total = None
        for member in range(2):
            row = 2 * member + side
            part = jnp.dot(
                stack3(u[row : row + 1]), kern(member, side), preferred_element_type=F32
            )
            total = part if total is None else total + part
        columns += in_rows(sum_rows(total), ranks)
    part = jnp.concatenate(columns, axis=0).astype(sent_ref.dtype)
    sent_ref[...] = jnp.broadcast_to(part[None], sent_ref.shape)


def first_pass(mass_ref, own_ref, other_ref, sent_ref):
    ones = jnp.ones(sent_ref.shape[1:], F32)
    send_columns(ones, mass_ref, own_ref, other_ref, sent_ref)


def next_pass(
    got_ref, v_ref, log_ref, mass_ref, own_ref, other_ref, sent_ref, new_ref, u_ref=None
):
    v, _ = new_scalings(log_ref.shape[0], got_ref, v_ref, log_ref)
    new_ref[...] = v
    send_columns(v, mass_ref, own_ref, other_ref, sent_ref, u_ref)


def profile_kernel(
    core_ref, got_ref, v_ref, log_ref, u_ref, own_ref, other_ref, expr_ref, more_ref,
    part_ref, new_ref, weights_ref,
):
    ranks = log_ref.shape[0]
    rows = own_ref.shape[0] // 2
    half = own_ref.shape[1] // 2
    v, weights = new_scalings(ranks, got_ref, v_ref, log_ref)
    new_ref[...] = v
    weights_ref[...] = weights
    u_columns = jnp.concatenate([u_ref[...], u_ref[...]], axis=0).T
    core = core_ref[0]
    blocks = [new_ref[pl.ds(ranks + core * (ranks // 2) + i, 1), :] for i in range(ranks // 2)]
    scale = jnp.concatenate(blocks, axis=1)
    lanes = pl.ds(pl.multiple_of(core * half, half), half)
    total = None
    for member, (kern_ref, cells_ref) in enumerate(((own_ref, expr_ref), (other_ref, more_ref))):
        kern = kern_ref[pl.ds(rows, rows), lanes].astype(F32)
        column = u_columns[:, 2 * member + 1 : 2 * member + 2]
        part = contract_rows((kern * scale * column).astype(BF16), cells_ref[...])
        total = part if total is None else total + part
    part_ref[...] = total


def on_chip(kernel, shapes, name, scalars=0, inputs=0, off_chip=0, scratch=(), limit=LIMIT):
    specs = {}
    if scalars:
        specs["in_specs"] = (
            [pl.BlockSpec(memory_space=pltpu.SMEM)] * scalars
            + [pl.BlockSpec(memory_space=pltpu.VMEM)] * inputs
            + [pl.BlockSpec(memory_space=pltpu.HBM)] * off_chip
        )
    return pl.pallas_call(
        kernel,
        out_shape=tuple(jax.ShapeDtypeStruct(shape, dtype) for shape, dtype in shapes),
        scratch_shapes=scratch,
        **specs,
        compiler_params=pltpu.CompilerParams(vmem_limit_bytes=limit),
        name=name,
    )


def shards(x_emb, y_emb, q_factor, r_factor, g_weights, a_mass, b_mass, expr):
    rows, width = q_factor.shape
    dim = x_emb.shape[1]
    genes = expr.shape[1]
    others = lax.axis_size(CHIPS)
    cell_devices = 2 * others
    ranks = lax.axis_size("x")
    cells_total = rows * cell_devices
    share = dim // cell_devices

    here = lax.axis_index("x")
    core = lax.axis_index("c")
    core_index = core.astype(jnp.int32)[None]
    chunk_shape = ((others, 3, share, width), F32)
    keep, give, rounded = on_chip(
        start_kernel,
        (chunk_shape, chunk_shape, ((2, rows, width), BF16)),
        "start",
        scalars=1,
        off_chip=4,
        limit=107 << 19,
        scratch=[
            pltpu.VMEM(x_emb.shape, BF16),
            pltpu.VMEM(y_emb.shape, BF16),
            pltpu.VMEM(q_factor.shape, F32),
            pltpu.VMEM(r_factor.shape, F32),
            pltpu.SemaphoreType.DMA((4, 2)),
        ],
    )(core_index, x_emb, y_emb, q_factor, r_factor)

    def from_shift(shift):
        return lax.ppermute(rounded, "x", [(i, (i + shift) % ranks) for i in range(ranks)])

    outgoing = keep + swap(give)
    columns = ranks * width
    tall = ((rows, columns), F32)
    sent = on_chip(chunk_kernel, (((ranks, 16, width), F32),), "chunk")(
        exchange(outgoing, CHIPS), g_weights[None]
    )[0]
    masses = jnp.stack([a_mass, b_mass])
    got, first, second, third, their_masses = lax.optimization_barrier(
        (exchange(sent, "x"), from_shift(1), from_shift(2), from_shift(3), swap(masses))
    )
    sent, vec, dot = on_chip(
        spread_kernel,
        (((others, 8, columns), BF16), ((8, columns), F32), ((ranks, width), F32)),
        "spread",
    )(got)
    crosses, other_expr = lax.optimization_barrier((exchange(sent, CHIPS), swap(expr)))
    crosses = crosses.reshape(others * 8, columns)
    own_grad = ((rows, width), F32)
    grad_q, grad_r, peak, factors, masses = on_chip(
        grad_kernel,
        (
            tall, tall, ((cell_devices, 1 + ranks, 1, width), F32),
            ((2 * rows, columns), BF16), ((4, rows), F32),
        ),
        "grad",
        scalars=2,
        inputs=8 + ranks,
    )(
        core_index, here.astype(jnp.int32)[None], x_emb, y_emb, crosses, swap(crosses), vec,
        dot, masses, their_masses, rounded, first, second, third,
    )
    kerns, log_g, eta, own_grad_q, own_grad_r = on_chip(
        kern_kernel,
        (((2 * rows, columns), BF16), ((ranks, width), F32), ((1, width), F32), own_grad, own_grad),
        "kern",
        scalars=1,
        inputs=5,
    )(
        here.astype(jnp.int32)[None], exchange(peak, CELLS), grad_q, grad_r, vec, factors
    )
    theirs = swap(kerns)
    sent_shape = ((others, 2 * ranks, width), BF16)
    u_shape = ((4, rows), F32)
    v_shape = ((2 * ranks, width), F32)
    sent = on_chip(first_pass, (sent_shape,), "first_pass")(masses, kerns, theirs)[0]
    v = jnp.ones(v_shape[0], F32)
    for step in range(1, PASSES):
        last = (u_shape,) if step == PASSES - 1 else ()
        sent, v, *u = on_chip(next_pass, (sent_shape, v_shape) + last, "next_pass")(
            exchange(sent, CHIPS), v, log_g, masses, kerns, theirs
        )
    (u,) = u
    part, v, weights = on_chip(
        profile_kernel,
        (((ranks * width // 2, genes), F32), v_shape, ((ranks, width), F32)),
        "profile",
        scalars=1,
        inputs=8,
    )(
        core_index, exchange(sent, CHIPS), v, log_g, u, kerns, theirs,
        expr, other_expr,
    )
    part, v, weights, u, eta, core, here = lax.optimization_barrier(
        (part, v, weights, u, eta, core, here)
    )
    v_q, v_r = v[:ranks], v[ranks:]
    kern_q = q_factor * jnp.exp(-eta * own_grad_q)
    kern_r = r_factor * jnp.exp(-eta * own_grad_r)
    q_new = u[0][:, None] * kern_q * pick(v_q, here)[None, :]
    r_new = u[1][:, None] * kern_r * pick(v_r, here)[None, :]
    mine_q = kerns[:rows].astype(F32)
    s_q = jnp.sum(mine_q * v_q.reshape(1, columns), axis=1)
    scaled = (mine_q * (v_q / weights).reshape(1, columns)).astype(BF16)

    half = columns // 2
    mine_scaled = lax.dynamic_slice_in_dim(scaled, core * half, half, 1)
    other_scaled = lax.dynamic_slice_in_dim(scaled, (1 - core) * half, half, 1)
    rank_share = pick(weights, here) / cells_total
    got, q_new, r_new, rank_share, s_q, mine_scaled, other_scaled = lax.optimization_barrier(
        (
            exchange(part.reshape(others, -1, genes), CHIPS),
            q_new, r_new, rank_share, s_q, mine_scaled, other_scaled,
        )
    )
    piece = jnp.sum(got, axis=0)
    mine = to_all(piece.astype(BF16), CHIPS).reshape(half, genes)
    mixed = jnp.dot(mine_scaled, mine, preferred_element_type=F32) + jnp.dot(
        other_scaled, swap(mine), preferred_element_type=F32
    )
    predicted = (mixed / s_q[:, None]).astype(BF16)
    return (q_new, r_new, rank_share, predicted)


def solution(mesh):
    named = Mesh(mesh.devices.reshape(4, 8, 2, 4), EVERY)
    block = P(CELLS, "x")
    return jax.shard_map(
        shards,
        mesh=named,
        in_specs=(
            P(CELLS, None),
            P(CELLS, None),
            block,
            block,
            P("x"),
            P(CELLS),
            P(CELLS),
            block,
        ),
        out_specs=(block, block, P("x"), block),
        check_vma=False,
    )
```

```python
import jax
import jax.numpy as jnp
from jax import lax
from jax.experimental import pallas as pl
from jax.experimental.pallas import tpu as pltpu
from jax.sharding import Mesh
from jax.sharding import PartitionSpec as P

PASSES = 10
SCALE = 0.0625
GAMMA = 10.0
POWER = 0.8
LIMIT = 12 << 20

CHIPS = ("y", "z")
CELLS = ("y", "z", "c")
EVERY = ("y", "z", "c", "x")
F32 = jnp.float32
BF16 = jnp.bfloat16


def contract_rows(left, right):
    return lax.dot_general(
        left, right, (((0,), (0,)), ((), ())), preferred_element_type=F32
    )


def exchange(chunks, axes):
    return lax.all_to_all(chunks, axes, 0, 0, tiled=False)


def to_all(value, axes):
    count = lax.axis_size(axes)
    return exchange(jnp.broadcast_to(value[None], (count,) + value.shape), axes)


def swap(value):
    return lax.ppermute(value, "c", [(0, 1), (1, 0)])


def pick(value, index):
    return lax.dynamic_index_in_dim(value, index, 0, keepdims=False)


def split3(value):
    high = lax.reduce_precision(value, 8, 7)
    rest = value - high
    middle = lax.reduce_precision(rest, 8, 7)
    low = lax.reduce_precision(rest - middle, 8, 7)
    return jnp.stack([high, middle, low]).astype(BF16)


def join3(rows):
    parts = rows.astype(F32)
    return parts[..., 0, :] + (parts[..., 1, :] + parts[..., 2, :])


def stack3(value):
    high = value.astype(BF16).astype(F32)
    rest = value - high
    middle = rest.astype(BF16).astype(F32)
    return jnp.concatenate([high, middle, rest - middle], axis=0).astype(BF16)


def sum_rows(value):
    return value[0:1] + (value[1:2] + value[2:3])


def in_lanes(blocks, first, count):
    return jnp.concatenate([blocks[first + i : first + i + 1] for i in range(count)], axis=1)


def in_rows(row, count):
    width = row.shape[1] // count
    return [row[:, i * width : (i + 1) * width] for i in range(count)]


def start_kernel(
    core_ref, x_hbm, y_hbm, q_hbm, r_hbm, keep_ref, give_ref, cast_ref,
    x_ref, y_ref, q_ref, r_ref, sems,
):
    pieces = sems.shape[1]
    copies = []
    for i, (source, target) in enumerate(
        ((x_hbm, x_ref), (q_hbm, q_ref), (y_hbm, y_ref), (r_hbm, r_ref))
    ):
        size = source.shape[0] // pieces
        for k in range(pieces):
            part = pl.ds(k * size, size)
            copies.append(pltpu.make_async_copy(source.at[part], target.at[part], sems.at[i, k]))
    for copy in copies:
        copy.start()
    chunks, _, share, width = keep_ref.shape
    half = x_ref.shape[1] // 2
    rows = []
    for side, (emb_ref, factor_ref) in enumerate(((x_ref, q_ref), (y_ref, r_ref))):
        for copy in copies[2 * side * pieces : 2 * (side + 1) * pieces]:
            copy.wait()
        factor = factor_ref[...]
        rounded = factor.astype(BF16)
        cast_ref[side] = rounded
        for position, out_ref in ((core_ref[0], keep_ref), (1 - core_ref[0], give_ref)):
            emb = emb_ref[:, pl.ds(pl.multiple_of(position * half, half), half)]
            cross = contract_rows(emb, rounded)
            for chunk in range(chunks):
                out_ref[chunk, side] = cross[chunk * share : (chunk + 1) * share]
        norms = jnp.sum(jnp.square(emb_ref[...].astype(F32)), axis=1, keepdims=True)
        rows.append(jnp.sum(norms * factor, axis=0, keepdims=True))
        rows.append(jnp.sum(factor, axis=0, keepdims=True))
    vec = jnp.concatenate(rows, axis=0)
    for out_ref in (keep_ref, give_ref):
        out_ref[:, 2] = jnp.broadcast_to(vec[None], (chunks, 4, width))


def chunk_kernel(got_ref, g_ref, sent_ref):
    summed = jnp.sum(got_ref[...], axis=0)
    xq, yr = summed[0], summed[1]
    dot = jnp.sum(xq * yr, axis=0, keepdims=True)
    nothing = jnp.zeros((2, dot.shape[1]), F32)
    chunk = jnp.concatenate([xq, yr, summed[2], dot, g_ref[...], nothing], axis=0)
    sent_ref[...] = jnp.broadcast_to(chunk[None], sent_ref.shape)


def spread_kernel(got_ref, sent_ref, vec_ref, dot_ref):
    ranks = got_ref.shape[0]
    every = jnp.concatenate([got_ref[i] for i in range(ranks)], axis=1)
    sent_ref[...] = jnp.broadcast_to(every[:8].astype(BF16)[None], sent_ref.shape)
    vec_ref[...] = every[8:16]
    dot_ref[...] = jnp.concatenate([got_ref[i, 12:13] for i in range(ranks)], axis=0)


def grad_kernel(
    core_ref, here_ref, x_ref, y_ref, mine_ref, other_ref, vec_ref, dot_ref, dot2_ref, mass_ref,
    mass2_ref, *refs
):
    factors = refs[:-5]
    grad_q_ref, grad_r_ref, peak_ref, all_ref, masses_ref = refs[-5:]
    masses_ref[...] = jnp.concatenate([mass_ref[...], mass2_ref[...]], axis=0)
    ranks = len(factors)
    rows, width = factors[0].shape[1:]

    def lanes_of(block):
        return pl.ds(pl.multiple_of(block * width, width), width)

    for shift, factor_ref in enumerate(factors):
        lanes = lanes_of(lax.rem(here_ref[0] + ranks - shift, ranks))
        for side in range(2):
            all_ref[pl.ds(side * rows, rows), lanes] = factor_ref[side]
    half = x_ref.shape[1] // 2
    chunks = mine_ref.shape[0]
    core = core_ref[0]
    g = vec_ref[5:6]
    scale = SCALE / g
    place = lax.broadcasted_iota(jnp.int32, (half, chunks), 1)
    wanted = lax.broadcasted_iota(jnp.int32, (half, chunks), 0)
    wanted = (wanted // 4) * 8 + wanted % 4
    xq, cq, yr, cr = (vec_ref[i : i + 1] for i in range(4))
    top = None
    for emb_ref, offset, count, total, out_ref in (
        (x_ref, 4, cr, yr, grad_q_ref),
        (y_ref, 0, cq, xq, grad_r_ref),
    ):
        select = jnp.where(place == wanted + offset, 1.0, 0.0).astype(BF16)
        product = None
        for position, cross_ref in ((core, mine_ref), (1 - core, other_ref)):
            rows = jnp.dot(select, cross_ref[...], preferred_element_type=F32).astype(BF16)
            emb = emb_ref[:, pl.ds(pl.multiple_of(position * half, half), half)]
            part = jnp.dot(emb, rows, preferred_element_type=F32)
            product = part if product is None else product + part
        norms = jnp.sum(jnp.square(emb_ref[...].astype(F32)), axis=1, keepdims=True)
        grad = scale * (norms * count + total - 2.0 * product)
        out_ref[...] = grad
        here = jnp.max(jnp.abs(grad), axis=0, keepdims=True)
        top = here if top is None else jnp.maximum(top, here)
    blocks = in_rows(top, dot_ref.shape[0])
    peak = blocks[0]
    for block in blocks[1:]:
        peak = jnp.maximum(peak, block)
    count = peak_ref.shape[0]
    peak_ref[:, 0] = jnp.broadcast_to(peak[None], (count,) + peak.shape)
    dots = dot_ref[...] + dot2_ref[...]
    kept = peak_ref.shape[1] - 1
    for i in range(kept):
        row = jnp.where(core == 0, dots[i : i + 1], dots[kept + i : kept + i + 1])
        peak_ref[:, 1 + i] = jnp.broadcast_to(row[None], (count,) + row.shape)


def kern_kernel(
    here_ref, peak_ref, grad_q_ref, grad_r_ref, vec_ref, all_ref,
    kern_ref, log_ref, eta_ref, own_q_ref, own_r_ref,
):
    rows = grad_q_ref.shape[0]
    width = own_q_ref.shape[1]
    mine = pl.ds(pl.multiple_of(here_ref[0] * width, width), width)
    own_q_ref[...] = grad_q_ref[:, mine]
    own_r_ref[...] = grad_r_ref[:, mine]
    xq, cq, yr, cr = (vec_ref[i : i + 1] for i in range(4))
    g = vec_ref[5:6]
    kept = peak_ref.shape[1] - 1
    got = peak_ref[...].reshape((peak_ref.shape[0] // 2, 2) + peak_ref.shape[1:])
    dot = jnp.concatenate(
        [jnp.sum(got[:, member, 1 + i], axis=0) for member in range(2) for i in range(kept)], axis=1
    )
    grad_g = -(SCALE * (xq * cr + cq * yr - 2.0 * dot)) / jnp.square(g)
    peak = jnp.maximum(
        jnp.max(jnp.max(peak_ref[:, 0], axis=0), axis=1, keepdims=True),
        jnp.max(jnp.abs(grad_g), axis=1, keepdims=True),
    )
    eta = GAMMA / (peak + 1e-06)
    eta_ref[...] = jnp.broadcast_to(eta, eta_ref.shape)
    kern_g = g * jnp.exp(-eta * grad_g)
    log_ref[...] = jnp.concatenate(in_rows(jnp.log(kern_g), log_ref.shape[0]), axis=0)
    for side, grad_ref in enumerate((grad_q_ref, grad_r_ref)):
        part = pl.ds(side * rows, rows)
        kern = all_ref[part, :].astype(F32) * jnp.exp(-eta * grad_ref[...])
        kern_ref[part, :] = kern.astype(BF16)


def new_scalings(ranks, got_ref, v_ref, log_ref):
    t = jnp.sum(got_ref[...].astype(F32), axis=0)
    passed = jnp.log(v_ref[...] * t)
    weights = jnp.exp((log_ref[...] + passed[:ranks] + passed[ranks:]) / 3.0)
    return jnp.concatenate([weights, weights], axis=0) / t, weights


def send_columns(v, mass_ref, own_ref, other_ref, sent_ref, u_ref=None):
    ranks = v.shape[0] // 2
    rows = own_ref.shape[0] // 2

    def kern(member, side):
        return (own_ref, other_ref)[member][pl.ds(side * rows, rows), :]

    v_rows = [stack3(in_lanes(v, side * ranks, ranks)) for side in range(2)]
    sums = []
    for member in range(2):
        for side in range(2):
            part = lax.dot_general(
                v_rows[side], kern(member, side), (((1,), (1,)), ((), ())),
                preferred_element_type=F32,
            )
            sums.append(sum_rows(part))
    u = jnp.exp(POWER * jnp.log(mass_ref[...] / jnp.concatenate(sums, axis=0)))
    if u_ref is not None:
        u_ref[...] = u
    columns = []
    for side in range(2):
        total = None
        for member in range(2):
            row = 2 * member + side
            part = jnp.dot(
                stack3(u[row : row + 1]), kern(member, side), preferred_element_type=F32
            )
            total = part if total is None else total + part
        columns += in_rows(sum_rows(total), ranks)
    part = jnp.concatenate(columns, axis=0).astype(sent_ref.dtype)
    sent_ref[...] = jnp.broadcast_to(part[None], sent_ref.shape)


def first_pass(mass_ref, own_ref, other_ref, sent_ref):
    ones = jnp.ones(sent_ref.shape[1:], F32)
    send_columns(ones, mass_ref, own_ref, other_ref, sent_ref)


def next_pass(
    got_ref, v_ref, log_ref, mass_ref, own_ref, other_ref, sent_ref, new_ref, u_ref=None
):
    v, _ = new_scalings(log_ref.shape[0], got_ref, v_ref, log_ref)
    new_ref[...] = v
    send_columns(v, mass_ref, own_ref, other_ref, sent_ref, u_ref)


def profile_kernel(
    core_ref, got_ref, v_ref, log_ref, u_ref, own_ref, other_ref, expr_ref, more_ref,
    part_ref, new_ref, weights_ref,
):
    ranks = log_ref.shape[0]
    rows = own_ref.shape[0] // 2
    half = own_ref.shape[1] // 2
    v, weights = new_scalings(ranks, got_ref, v_ref, log_ref)
    new_ref[...] = v
    weights_ref[...] = weights
    u_columns = jnp.concatenate([u_ref[...], u_ref[...]], axis=0).T
    core = core_ref[0]
    blocks = [new_ref[pl.ds(ranks + core * (ranks // 2) + i, 1), :] for i in range(ranks // 2)]
    scale = jnp.concatenate(blocks, axis=1)
    lanes = pl.ds(pl.multiple_of(core * half, half), half)
    total = None
    for member, (kern_ref, cells_ref) in enumerate(((own_ref, expr_ref), (other_ref, more_ref))):
        kern = kern_ref[pl.ds(rows, rows), lanes].astype(F32)
        column = u_columns[:, 2 * member + 1 : 2 * member + 2]
        part = contract_rows((kern * scale * column).astype(BF16), cells_ref[...])
        total = part if total is None else total + part
    part_ref[...] = total


def on_chip(kernel, shapes, name, scalars=0, inputs=0, off_chip=0, scratch=(), limit=LIMIT):
    specs = {}
    if scalars:
        specs["in_specs"] = (
            [pl.BlockSpec(memory_space=pltpu.SMEM)] * scalars
            + [pl.BlockSpec(memory_space=pltpu.VMEM)] * inputs
            + [pl.BlockSpec(memory_space=pltpu.HBM)] * off_chip
        )
    return pl.pallas_call(
        kernel,
        out_shape=tuple(jax.ShapeDtypeStruct(shape, dtype) for shape, dtype in shapes),
        scratch_shapes=scratch,
        **specs,
        compiler_params=pltpu.CompilerParams(vmem_limit_bytes=limit),
        name=name,
    )


def shards(x_emb, y_emb, q_factor, r_factor, g_weights, a_mass, b_mass, expr):
    rows, width = q_factor.shape
    dim = x_emb.shape[1]
    genes = expr.shape[1]
    others = lax.axis_size(CHIPS)
    cell_devices = 2 * others
    ranks = lax.axis_size("x")
    cells_total = rows * cell_devices
    share = dim // cell_devices

    here = lax.axis_index("x")
    core = lax.axis_index("c")
    core_index = core.astype(jnp.int32)[None]
    chunk_shape = ((others, 3, share, width), F32)
    keep, give, rounded = on_chip(
        start_kernel,
        (chunk_shape, chunk_shape, ((2, rows, width), BF16)),
        "start",
        scalars=1,
        off_chip=4,
        limit=107 << 19,
        scratch=[
            pltpu.VMEM(x_emb.shape, BF16),
            pltpu.VMEM(y_emb.shape, BF16),
            pltpu.VMEM(q_factor.shape, F32),
            pltpu.VMEM(r_factor.shape, F32),
            pltpu.SemaphoreType.DMA((4, 4)),
        ],
    )(core_index, x_emb, y_emb, q_factor, r_factor)

    def from_shift(shift):
        return lax.ppermute(rounded, "x", [(i, (i + shift) % ranks) for i in range(ranks)])

    outgoing = keep + swap(give)
    columns = ranks * width
    tall = ((rows, columns), F32)
    sent = on_chip(chunk_kernel, (((ranks, 16, width), F32),), "chunk")(
        exchange(outgoing, CHIPS), g_weights[None]
    )[0]
    masses = jnp.stack([a_mass, b_mass])
    got, first, second, third, their_masses = lax.optimization_barrier(
        (exchange(sent, "x"), from_shift(1), from_shift(2), from_shift(3), swap(masses))
    )
    sent, vec, dot = on_chip(
        spread_kernel,
        (((others, 8, columns), BF16), ((8, columns), F32), ((ranks, width), F32)),
        "spread",
    )(got)
    crosses, other_expr, their_dot = lax.optimization_barrier(
        (exchange(sent, CHIPS), swap(expr), swap(dot))
    )
    crosses = crosses.reshape(others * 8, columns)
    own_grad = ((rows, width), F32)
    grad_q, grad_r, peak, factors, masses = on_chip(
        grad_kernel,
        (
            tall, tall, ((cell_devices, 1 + ranks // 2, 1, width), F32),
            ((2 * rows, columns), BF16), ((4, rows), F32),
        ),
        "grad",
        scalars=2,
        inputs=9 + ranks,
    )(
        core_index, here.astype(jnp.int32)[None], x_emb, y_emb, crosses, swap(crosses), vec,
        dot, their_dot, masses, their_masses, rounded, first, second, third,
    )
    kerns, log_g, eta, own_grad_q, own_grad_r = on_chip(
        kern_kernel,
        (((2 * rows, columns), BF16), ((ranks, width), F32), ((1, width), F32), own_grad, own_grad),
        "kern",
        scalars=1,
        inputs=5,
    )(
        here.astype(jnp.int32)[None], exchange(peak, CELLS), grad_q, grad_r, vec, factors
    )
    theirs = swap(kerns)
    sent_shape = ((others, 2 * ranks, width), BF16)
    u_shape = ((4, rows), F32)
    v_shape = ((2 * ranks, width), F32)
    sent = on_chip(first_pass, (sent_shape,), "first_pass")(masses, kerns, theirs)[0]
    v = jnp.ones(v_shape[0], F32)
    for step in range(1, PASSES):
        last = (u_shape,) if step == PASSES - 1 else ()
        sent, v, *u = on_chip(next_pass, (sent_shape, v_shape) + last, "next_pass")(
            exchange(sent, CHIPS), v, log_g, masses, kerns, theirs
        )
    (u,) = u
    part, v, weights = on_chip(
        profile_kernel,
        (((ranks * width // 2, genes), F32), v_shape, ((ranks, width), F32)),
        "profile",
        scalars=1,
        inputs=8,
    )(
        core_index, exchange(sent, CHIPS), v, log_g, u, kerns, theirs,
        expr, other_expr,
    )
    part, v, weights, u, eta, core, here = lax.optimization_barrier(
        (part, v, weights, u, eta, core, here)
    )
    v_q, v_r = v[:ranks], v[ranks:]
    kern_q = q_factor * jnp.exp(-eta * own_grad_q)
    kern_r = r_factor * jnp.exp(-eta * own_grad_r)
    q_new = u[0][:, None] * kern_q * pick(v_q, here)[None, :]
    r_new = u[1][:, None] * kern_r * pick(v_r, here)[None, :]
    mine_q = kerns[:rows].astype(F32)
    s_q = jnp.sum(mine_q * v_q.reshape(1, columns), axis=1)
    scaled = (mine_q * (v_q / weights).reshape(1, columns)).astype(BF16)

    half = columns // 2
    mine_scaled = lax.dynamic_slice_in_dim(scaled, core * half, half, 1)
    other_scaled = lax.dynamic_slice_in_dim(scaled, (1 - core) * half, half, 1)
    rank_share = pick(weights, here) / cells_total
    got, q_new, r_new, rank_share, s_q, mine_scaled, other_scaled = lax.optimization_barrier(
        (
            exchange(part.reshape(others, -1, genes), CHIPS),
            q_new, r_new, rank_share, s_q, mine_scaled, other_scaled,
        )
    )
    piece = jnp.sum(got, axis=0)
    mine = to_all(piece.astype(BF16), CHIPS).reshape(half, genes)
    mixed = jnp.dot(mine_scaled, mine, preferred_element_type=F32) + jnp.dot(
        other_scaled, swap(mine), preferred_element_type=F32
    )
    predicted = (mixed / s_q[:, None]).astype(BF16)
    return (q_new, r_new, rank_share, predicted)


def solution(mesh):
    named = Mesh(mesh.devices.reshape(4, 8, 2, 4), EVERY)
    block = P(CELLS, "x")
    return jax.shard_map(
        shards,
        mesh=named,
        in_specs=(
            P(CELLS, None),
            P(CELLS, None),
            block,
            block,
            P("x"),
            P(CELLS),
            P(CELLS),
            block,
        ),
        out_specs=(block, block, P("x"), block),
        check_vma=False,
    )
```

```python
import jax
import jax.numpy as jnp
from jax import lax
from jax.experimental import pallas as pl
from jax.experimental.pallas import tpu as pltpu
from jax.sharding import Mesh
from jax.sharding import PartitionSpec as P

PASSES = 10
SCALE = 0.0625
GAMMA = 10.0
POWER = 0.8
LIMIT = 12 << 20

CHIPS = ("y", "z")
CELLS = ("y", "z", "c")
EVERY = ("y", "z", "c", "x")
F32 = jnp.float32
BF16 = jnp.bfloat16


def contract_rows(left, right):
    return lax.dot_general(
        left, right, (((0,), (0,)), ((), ())), preferred_element_type=F32
    )


def exchange(chunks, axes):
    return lax.all_to_all(chunks, axes, 0, 0, tiled=False)


def to_all(value, axes):
    count = lax.axis_size(axes)
    return exchange(jnp.broadcast_to(value[None], (count,) + value.shape), axes)


def swap(value):
    return lax.ppermute(value, "c", [(0, 1), (1, 0)])


def pick(value, index):
    return lax.dynamic_index_in_dim(value, index, 0, keepdims=False)


def split3(value):
    high = lax.reduce_precision(value, 8, 7)
    rest = value - high
    middle = lax.reduce_precision(rest, 8, 7)
    low = lax.reduce_precision(rest - middle, 8, 7)
    return jnp.stack([high, middle, low]).astype(BF16)


def join3(rows):
    parts = rows.astype(F32)
    return parts[..., 0, :] + (parts[..., 1, :] + parts[..., 2, :])


def stack3(value):
    high = value.astype(BF16).astype(F32)
    rest = value - high
    middle = rest.astype(BF16).astype(F32)
    return jnp.concatenate([high, middle, rest - middle], axis=0).astype(BF16)


def sum_rows(value):
    return value[0:1] + (value[1:2] + value[2:3])


def in_lanes(blocks, first, count):
    return jnp.concatenate([blocks[first + i : first + i + 1] for i in range(count)], axis=1)


def in_rows(row, count):
    width = row.shape[1] // count
    return [row[:, i * width : (i + 1) * width] for i in range(count)]


def start_kernel(
    core_ref, x_hbm, y_hbm, q_hbm, r_hbm, keep_ref, give_ref, cast_ref,
    x_ref, y_ref, q_ref, r_ref, sems,
):
    pieces = sems.shape[1]
    copies = []
    for i, (source, target) in enumerate(
        ((x_hbm, x_ref), (q_hbm, q_ref), (y_hbm, y_ref), (r_hbm, r_ref))
    ):
        size = source.shape[0] // pieces
        for k in range(pieces):
            part = pl.ds(k * size, size)
            copies.append(pltpu.make_async_copy(source.at[part], target.at[part], sems.at[i, k]))
    for copy in copies:
        copy.start()
    chunks, _, share, width = keep_ref.shape
    half = x_ref.shape[1] // 2
    rows = []
    for side, (emb_ref, factor_ref) in enumerate(((x_ref, q_ref), (y_ref, r_ref))):
        for copy in copies[2 * side * pieces : 2 * (side + 1) * pieces]:
            copy.wait()
        factor = factor_ref[...]
        rounded = factor.astype(BF16)
        cast_ref[side] = rounded
        for position, out_ref in ((core_ref[0], keep_ref), (1 - core_ref[0], give_ref)):
            emb = emb_ref[:, pl.ds(pl.multiple_of(position * half, half), half)]
            cross = contract_rows(emb, rounded)
            for chunk in range(chunks):
                out_ref[chunk, side] = cross[chunk * share : (chunk + 1) * share]
        norms = jnp.sum(jnp.square(emb_ref[...].astype(F32)), axis=1, keepdims=True)
        rows.append(jnp.sum(norms * factor, axis=0, keepdims=True))
        rows.append(jnp.sum(factor, axis=0, keepdims=True))
    vec = jnp.concatenate(rows, axis=0)
    for out_ref in (keep_ref, give_ref):
        out_ref[:, 2] = jnp.broadcast_to(vec[None], (chunks, 4, width))


def chunk_kernel(got_ref, g_ref, sent_ref):
    summed = jnp.sum(got_ref[...], axis=0)
    xq, yr = summed[0], summed[1]
    dot = jnp.sum(xq * yr, axis=0, keepdims=True)
    nothing = jnp.zeros((2, dot.shape[1]), F32)
    chunk = jnp.concatenate([xq, yr, summed[2], dot, g_ref[...], nothing], axis=0)
    sent_ref[...] = jnp.broadcast_to(chunk[None], sent_ref.shape)


def spread_kernel(got_ref, sent_ref, vec_ref, dot_ref):
    ranks = got_ref.shape[0]
    every = jnp.concatenate([got_ref[i] for i in range(ranks)], axis=1)
    sent_ref[...] = jnp.broadcast_to(every[:8].astype(BF16)[None], sent_ref.shape)
    vec_ref[...] = every[8:16]
    dot_ref[...] = jnp.concatenate([got_ref[i, 12:13] for i in range(ranks)], axis=0)


def grad_kernel(
    core_ref, here_ref, x_ref, y_ref, mine_ref, other_ref, vec_ref, dot_ref, dot2_ref, mass_ref,
    mass2_ref, *refs
):
    factors = refs[:-5]
    grad_q_ref, grad_r_ref, peak_ref, all_ref, masses_ref = refs[-5:]
    masses_ref[...] = jnp.concatenate([mass_ref[...], mass2_ref[...]], axis=0)
    ranks = len(factors)
    rows, width = factors[0].shape[1:]

    def lanes_of(block):
        return pl.ds(pl.multiple_of(block * width, width), width)

    for shift, factor_ref in enumerate(factors):
        lanes = lanes_of(lax.rem(here_ref[0] + ranks - shift, ranks))
        for side in range(2):
            all_ref[pl.ds(side * rows, rows), lanes] = factor_ref[side]
    half = x_ref.shape[1] // 2
    chunks = mine_ref.shape[0]
    core = core_ref[0]
    g = vec_ref[5:6]
    scale = SCALE / g
    place = lax.broadcasted_iota(jnp.int32, (half, chunks), 1)
    wanted = lax.broadcasted_iota(jnp.int32, (half, chunks), 0)
    wanted = (wanted // 4) * 8 + wanted % 4
    xq, cq, yr, cr = (vec_ref[i : i + 1] for i in range(4))
    top = None
    for emb_ref, offset, count, total, out_ref in (
        (x_ref, 4, cr, yr, grad_q_ref),
        (y_ref, 0, cq, xq, grad_r_ref),
    ):
        select = jnp.where(place == wanted + offset, 1.0, 0.0).astype(BF16)
        product = None
        for position, cross_ref in ((core, mine_ref), (1 - core, other_ref)):
            rows = jnp.dot(select, cross_ref[...], preferred_element_type=F32).astype(BF16)
            emb = emb_ref[:, pl.ds(pl.multiple_of(position * half, half), half)]
            part = jnp.dot(emb, rows, preferred_element_type=F32)
            product = part if product is None else product + part
        norms = jnp.sum(jnp.square(emb_ref[...].astype(F32)), axis=1, keepdims=True)
        grad = scale * (norms * count + total - 2.0 * product)
        out_ref[...] = grad
        here = jnp.max(jnp.abs(grad), axis=0, keepdims=True)
        top = here if top is None else jnp.maximum(top, here)
    blocks = in_rows(top, dot_ref.shape[0])
    peak = blocks[0]
    for block in blocks[1:]:
        peak = jnp.maximum(peak, block)
    count = peak_ref.shape[0]
    peak_ref[:, 0] = jnp.broadcast_to(peak[None], (count,) + peak.shape)
    dots = dot_ref[...] + dot2_ref[...]
    kept = peak_ref.shape[1] - 1
    for i in range(kept):
        row = jnp.where(core == 0, dots[i : i + 1], dots[kept + i : kept + i + 1])
        peak_ref[:, 1 + i] = jnp.broadcast_to(row[None], (count,) + row.shape)


def kern_kernel(
    here_ref, peak_ref, grad_q_ref, grad_r_ref, vec_ref, all_ref,
    kern_ref, log_ref, eta_ref, own_q_ref, own_r_ref,
):
    rows = grad_q_ref.shape[0]
    width = own_q_ref.shape[1]
    mine = pl.ds(pl.multiple_of(here_ref[0] * width, width), width)
    own_q_ref[...] = grad_q_ref[:, mine]
    own_r_ref[...] = grad_r_ref[:, mine]
    xq, cq, yr, cr = (vec_ref[i : i + 1] for i in range(4))
    g = vec_ref[5:6]
    kept = peak_ref.shape[1] - 1
    got = peak_ref[...].reshape((peak_ref.shape[0] // 2, 2) + peak_ref.shape[1:])
    dot = jnp.concatenate(
        [jnp.sum(got[:, member, 1 + i], axis=0) for member in range(2) for i in range(kept)], axis=1
    )
    grad_g = -(SCALE * (xq * cr + cq * yr - 2.0 * dot)) / jnp.square(g)
    peak = jnp.maximum(
        jnp.max(jnp.max(peak_ref[:, 0], axis=0), axis=1, keepdims=True),
        jnp.max(jnp.abs(grad_g), axis=1, keepdims=True),
    )
    eta = GAMMA / (peak + 1e-06)
    eta_ref[...] = jnp.broadcast_to(eta, eta_ref.shape)
    kern_g = g * jnp.exp(-eta * grad_g)
    log_ref[...] = jnp.concatenate(in_rows(jnp.log(kern_g), log_ref.shape[0]), axis=0)
    for side, grad_ref in enumerate((grad_q_ref, grad_r_ref)):
        part = pl.ds(side * rows, rows)
        kern = all_ref[part, :].astype(F32) * jnp.exp(-eta * grad_ref[...])
        kern_ref[part, :] = kern.astype(BF16)


def new_scalings(ranks, got_ref, v_ref, log_ref):
    t = jnp.sum(got_ref[...].astype(F32), axis=0)
    passed = jnp.log(v_ref[...] * t)
    weights = jnp.exp((log_ref[...] + passed[:ranks] + passed[ranks:]) / 3.0)
    return jnp.concatenate([weights, weights], axis=0) / t, weights


def send_columns(v, mass_ref, own_ref, other_ref, sent_ref, u_ref=None):
    ranks = v.shape[0] // 2
    rows = own_ref.shape[0] // 2

    def kern(member, side):
        return (own_ref, other_ref)[member][pl.ds(side * rows, rows), :]

    v_rows = [stack3(in_lanes(v, side * ranks, ranks)) for side in range(2)]
    sums = []
    for member in range(2):
        for side in range(2):
            part = lax.dot_general(
                v_rows[side], kern(member, side), (((1,), (1,)), ((), ())),
                preferred_element_type=F32,
            )
            sums.append(sum_rows(part))
    u = jnp.exp(POWER * jnp.log(mass_ref[...] / jnp.concatenate(sums, axis=0)))
    if u_ref is not None:
        u_ref[...] = u
    columns = []
    for side in range(2):
        total = None
        for member in range(2):
            row = 2 * member + side
            part = jnp.dot(
                stack3(u[row : row + 1]), kern(member, side), preferred_element_type=F32
            )
            total = part if total is None else total + part
        columns += in_rows(sum_rows(total), ranks)
    part = jnp.concatenate(columns, axis=0).astype(sent_ref.dtype)
    sent_ref[...] = jnp.broadcast_to(part[None], sent_ref.shape)


def first_columns(member, mass_ref, kern_ref):
    rows, columns = kern_ref.shape[0] // 2, kern_ref.shape[1]
    ones = jnp.ones((1, columns), BF16)
    parts = []
    for side in range(2):
        kern = kern_ref[pl.ds(side * rows, rows), :]
        s = lax.dot_general(ones, kern, (((1,), (1,)), ((), ())), preferred_element_type=F32)
        row = 2 * member + side
        u = jnp.exp(POWER * jnp.log(mass_ref[row : row + 1] / s))
        part = sum_rows(jnp.dot(stack3(u), kern, preferred_element_type=F32))
        parts += in_rows(part, columns // 128)
    return jnp.concatenate(parts, axis=0)


def first_own(mass_ref, kern_ref, part_ref):
    part_ref[...] = first_columns(0, mass_ref, kern_ref)


def first_other(mass_ref, kern_ref, part_ref, sent_ref):
    part = (part_ref[...] + first_columns(1, mass_ref, kern_ref)).astype(sent_ref.dtype)
    sent_ref[...] = jnp.broadcast_to(part[None], sent_ref.shape)


def next_pass(
    got_ref, v_ref, log_ref, mass_ref, own_ref, other_ref, sent_ref, new_ref, u_ref=None
):
    v, _ = new_scalings(log_ref.shape[0], got_ref, v_ref, log_ref)
    new_ref[...] = v
    send_columns(v, mass_ref, own_ref, other_ref, sent_ref, u_ref)


def profile_kernel(
    core_ref, got_ref, v_ref, log_ref, u_ref, own_ref, other_ref, expr_ref, more_ref,
    part_ref, new_ref, weights_ref,
):
    ranks = log_ref.shape[0]
    rows = own_ref.shape[0] // 2
    half = own_ref.shape[1] // 2
    v, weights = new_scalings(ranks, got_ref, v_ref, log_ref)
    new_ref[...] = v
    weights_ref[...] = weights
    u_columns = jnp.concatenate([u_ref[...], u_ref[...]], axis=0).T
    core = core_ref[0]
    blocks = [new_ref[pl.ds(ranks + core * (ranks // 2) + i, 1), :] for i in range(ranks // 2)]
    scale = jnp.concatenate(blocks, axis=1)
    lanes = pl.ds(pl.multiple_of(core * half, half), half)
    total = None
    for member, (kern_ref, cells_ref) in enumerate(((own_ref, expr_ref), (other_ref, more_ref))):
        kern = kern_ref[pl.ds(rows, rows), lanes].astype(F32)
        column = u_columns[:, 2 * member + 1 : 2 * member + 2]
        part = contract_rows((kern * scale * column).astype(BF16), cells_ref[...])
        total = part if total is None else total + part
    part_ref[...] = total


def on_chip(kernel, shapes, name, scalars=0, inputs=0, off_chip=0, scratch=(), limit=LIMIT):
    specs = {}
    if scalars:
        specs["in_specs"] = (
            [pl.BlockSpec(memory_space=pltpu.SMEM)] * scalars
            + [pl.BlockSpec(memory_space=pltpu.VMEM)] * inputs
            + [pl.BlockSpec(memory_space=pltpu.HBM)] * off_chip
        )
    return pl.pallas_call(
        kernel,
        out_shape=tuple(jax.ShapeDtypeStruct(shape, dtype) for shape, dtype in shapes),
        scratch_shapes=scratch,
        **specs,
        compiler_params=pltpu.CompilerParams(vmem_limit_bytes=limit),
        name=name,
    )


def shards(x_emb, y_emb, q_factor, r_factor, g_weights, a_mass, b_mass, expr):
    rows, width = q_factor.shape
    dim = x_emb.shape[1]
    genes = expr.shape[1]
    others = lax.axis_size(CHIPS)
    cell_devices = 2 * others
    ranks = lax.axis_size("x")
    cells_total = rows * cell_devices
    share = dim // cell_devices

    here = lax.axis_index("x")
    core = lax.axis_index("c")
    core_index = core.astype(jnp.int32)[None]
    chunk_shape = ((others, 3, share, width), F32)
    keep, give, rounded = on_chip(
        start_kernel,
        (chunk_shape, chunk_shape, ((2, rows, width), BF16)),
        "start",
        scalars=1,
        off_chip=4,
        limit=107 << 19,
        scratch=[
            pltpu.VMEM(x_emb.shape, BF16),
            pltpu.VMEM(y_emb.shape, BF16),
            pltpu.VMEM(q_factor.shape, F32),
            pltpu.VMEM(r_factor.shape, F32),
            pltpu.SemaphoreType.DMA((4, 4)),
        ],
    )(core_index, x_emb, y_emb, q_factor, r_factor)

    def from_shift(shift):
        return lax.ppermute(rounded, "x", [(i, (i + shift) % ranks) for i in range(ranks)])

    outgoing = keep + swap(give)
    columns = ranks * width
    tall = ((rows, columns), F32)
    sent = on_chip(chunk_kernel, (((ranks, 16, width), F32),), "chunk")(
        exchange(outgoing, CHIPS), g_weights[None]
    )[0]
    masses = jnp.stack([a_mass, b_mass])
    got, first, second, third, their_masses = lax.optimization_barrier(
        (exchange(sent, "x"), from_shift(1), from_shift(2), from_shift(3), swap(masses))
    )
    sent, vec, dot = on_chip(
        spread_kernel,
        (((others, 8, columns), BF16), ((8, columns), F32), ((ranks, width), F32)),
        "spread",
    )(got)
    crosses, other_expr, their_dot = lax.optimization_barrier(
        (exchange(sent, CHIPS), swap(expr), swap(dot))
    )
    crosses = crosses.reshape(others * 8, columns)
    own_grad = ((rows, width), F32)
    grad_q, grad_r, peak, factors, masses = on_chip(
        grad_kernel,
        (
            tall, tall, ((cell_devices, 1 + ranks // 2, 1, width), F32),
            ((2 * rows, columns), BF16), ((4, rows), F32),
        ),
        "grad",
        scalars=2,
        inputs=9 + ranks,
    )(
        core_index, here.astype(jnp.int32)[None], x_emb, y_emb, crosses, swap(crosses), vec,
        dot, their_dot, masses, their_masses, rounded, first, second, third,
    )
    kerns, log_g, eta, own_grad_q, own_grad_r = on_chip(
        kern_kernel,
        (((2 * rows, columns), BF16), ((ranks, width), F32), ((1, width), F32), own_grad, own_grad),
        "kern",
        scalars=1,
        inputs=5,
    )(
        here.astype(jnp.int32)[None], exchange(peak, CELLS), grad_q, grad_r, vec, factors
    )
    theirs = swap(kerns)
    sent_shape = ((others, 2 * ranks, width), BF16)
    u_shape = ((4, rows), F32)
    v_shape = ((2 * ranks, width), F32)
    part = on_chip(first_own, (v_shape,), "first_own")(masses, kerns)[0]
    sent = on_chip(first_other, (sent_shape,), "first_other")(masses, theirs, part)[0]
    v = jnp.ones(v_shape[0], F32)
    for step in range(1, PASSES):
        last = (u_shape,) if step == PASSES - 1 else ()
        sent, v, *u = on_chip(next_pass, (sent_shape, v_shape) + last, "next_pass")(
            exchange(sent, CHIPS), v, log_g, masses, kerns, theirs
        )
    (u,) = u
    part, v, weights = on_chip(
        profile_kernel,
        (((ranks * width // 2, genes), F32), v_shape, ((ranks, width), F32)),
        "profile",
        scalars=1,
        inputs=8,
    )(
        core_index, exchange(sent, CHIPS), v, log_g, u, kerns, theirs,
        expr, other_expr,
    )
    part, v, weights, u, eta, core, here = lax.optimization_barrier(
        (part, v, weights, u, eta, core, here)
    )
    v_q, v_r = v[:ranks], v[ranks:]
    kern_q = q_factor * jnp.exp(-eta * own_grad_q)
    kern_r = r_factor * jnp.exp(-eta * own_grad_r)
    q_new = u[0][:, None] * kern_q * pick(v_q, here)[None, :]
    r_new = u[1][:, None] * kern_r * pick(v_r, here)[None, :]
    mine_q = kerns[:rows].astype(F32)
    s_q = jnp.sum(mine_q * v_q.reshape(1, columns), axis=1)
    scaled = (mine_q * (v_q / weights).reshape(1, columns)).astype(BF16)

    half = columns // 2
    mine_scaled = lax.dynamic_slice_in_dim(scaled, core * half, half, 1)
    other_scaled = lax.dynamic_slice_in_dim(scaled, (1 - core) * half, half, 1)
    rank_share = pick(weights, here) / cells_total
    got, q_new, r_new, rank_share, s_q, mine_scaled, other_scaled = lax.optimization_barrier(
        (
            exchange(part.reshape(others, -1, genes), CHIPS),
            q_new, r_new, rank_share, s_q, mine_scaled, other_scaled,
        )
    )
    piece = jnp.sum(got, axis=0)
    mine = to_all(piece.astype(BF16), CHIPS).reshape(half, genes)
    mixed = jnp.dot(mine_scaled, mine, preferred_element_type=F32) + jnp.dot(
        other_scaled, swap(mine), preferred_element_type=F32
    )
    predicted = (mixed / s_q[:, None]).astype(BF16)
    return (q_new, r_new, rank_share, predicted)


def solution(mesh):
    named = Mesh(mesh.devices.reshape(4, 8, 2, 4), EVERY)
    block = P(CELLS, "x")
    return jax.shard_map(
        shards,
        mesh=named,
        in_specs=(
            P(CELLS, None),
            P(CELLS, None),
            block,
            block,
            P("x"),
            P(CELLS),
            P(CELLS),
            block,
        ),
        out_specs=(block, block, P("x"), block),
        check_vma=False,
    )
```

```python
import jax
import jax.numpy as jnp
from jax import lax
from jax.experimental import pallas as pl
from jax.experimental.pallas import tpu as pltpu
from jax.sharding import Mesh
from jax.sharding import PartitionSpec as P

PASSES = 10
SCALE = 0.0625
GAMMA = 10.0
POWER = 0.8
LIMIT = 12 << 20

CHIPS = ("y", "z")
CELLS = ("y", "z", "c")
EVERY = ("y", "z", "c", "x")
F32 = jnp.float32
BF16 = jnp.bfloat16


def contract_rows(left, right):
    return lax.dot_general(
        left, right, (((0,), (0,)), ((), ())), preferred_element_type=F32
    )


def exchange(chunks, axes):
    return lax.all_to_all(chunks, axes, 0, 0, tiled=False)


def to_all(value, axes):
    count = lax.axis_size(axes)
    return exchange(jnp.broadcast_to(value[None], (count,) + value.shape), axes)


def swap(value):
    return lax.ppermute(value, "c", [(0, 1), (1, 0)])


def pick(value, index):
    return lax.dynamic_index_in_dim(value, index, 0, keepdims=False)


def split3(value):
    high = lax.reduce_precision(value, 8, 7)
    rest = value - high
    middle = lax.reduce_precision(rest, 8, 7)
    low = lax.reduce_precision(rest - middle, 8, 7)
    return jnp.stack([high, middle, low]).astype(BF16)


def join3(rows):
    parts = rows.astype(F32)
    return parts[..., 0, :] + (parts[..., 1, :] + parts[..., 2, :])


def stack3(value):
    high = value.astype(BF16).astype(F32)
    rest = value - high
    middle = rest.astype(BF16).astype(F32)
    return jnp.concatenate([high, middle, rest - middle], axis=0).astype(BF16)


def sum_rows(value):
    return value[0:1] + (value[1:2] + value[2:3])


def in_lanes(blocks, first, count):
    return jnp.concatenate([blocks[first + i : first + i + 1] for i in range(count)], axis=1)


def in_rows(row, count):
    width = row.shape[1] // count
    return [row[:, i * width : (i + 1) * width] for i in range(count)]


def start_kernel(
    core_ref, x_hbm, y_hbm, q_hbm, r_hbm, keep_ref, give_ref, cast_ref,
    x_ref, y_ref, q_ref, r_ref, sems,
):
    pieces = sems.shape[1]
    copies = []
    for i, (source, target) in enumerate(
        ((x_hbm, x_ref), (q_hbm, q_ref), (y_hbm, y_ref), (r_hbm, r_ref))
    ):
        size = source.shape[0] // pieces
        for k in range(pieces):
            part = pl.ds(k * size, size)
            copies.append(pltpu.make_async_copy(source.at[part], target.at[part], sems.at[i, k]))
    for copy in copies:
        copy.start()
    chunks, _, share, width = keep_ref.shape
    half = x_ref.shape[1] // 2
    rows = []
    for side, (emb_ref, factor_ref) in enumerate(((x_ref, q_ref), (y_ref, r_ref))):
        for copy in copies[2 * side * pieces : 2 * (side + 1) * pieces]:
            copy.wait()
        factor = factor_ref[...]
        rounded = factor.astype(BF16)
        cast_ref[side] = rounded
        for position, out_ref in ((core_ref[0], keep_ref), (1 - core_ref[0], give_ref)):
            emb = emb_ref[:, pl.ds(pl.multiple_of(position * half, half), half)]
            cross = contract_rows(emb, rounded)
            for chunk in range(chunks):
                out_ref[chunk, side] = cross[chunk * share : (chunk + 1) * share]
        norms = jnp.sum(jnp.square(emb_ref[...].astype(F32)), axis=1, keepdims=True)
        rows.append(jnp.sum(norms * factor, axis=0, keepdims=True))
        rows.append(jnp.sum(factor, axis=0, keepdims=True))
    vec = jnp.concatenate(rows, axis=0)
    for out_ref in (keep_ref, give_ref):
        out_ref[:, 2] = jnp.broadcast_to(vec[None], (chunks, 4, width))


def chunk_kernel(got_ref, g_ref, sent_ref):
    summed = jnp.sum(got_ref[...], axis=0)
    xq, yr = summed[0], summed[1]
    dot = jnp.sum(xq * yr, axis=0, keepdims=True)
    nothing = jnp.zeros((2, dot.shape[1]), F32)
    chunk = jnp.concatenate([xq, yr, summed[2], dot, g_ref[...], nothing], axis=0)
    sent_ref[...] = jnp.broadcast_to(chunk[None], sent_ref.shape)


def spread_kernel(got_ref, sent_ref, vec_ref, dot_ref):
    ranks = got_ref.shape[0]
    every = jnp.concatenate([got_ref[i] for i in range(ranks)], axis=1)
    sent_ref[...] = jnp.broadcast_to(every[:8].astype(BF16)[None], sent_ref.shape)
    vec_ref[...] = every[8:16]
    dot_ref[...] = jnp.concatenate([got_ref[i, 12:13] for i in range(ranks)], axis=0)


def grad_kernel(
    core_ref, here_ref, x_ref, y_ref, mine_ref, other_ref, vec_ref, dot_ref, dot2_ref, mass_ref,
    mass2_ref, *refs
):
    factors = refs[:-5]
    grad_q_ref, grad_r_ref, peak_ref, all_ref, masses_ref = refs[-5:]
    masses_ref[...] = jnp.concatenate([mass_ref[...], mass2_ref[...]], axis=0)
    ranks = len(factors)
    rows, width = factors[0].shape[1:]

    def lanes_of(block):
        return pl.ds(pl.multiple_of(block * width, width), width)

    for shift, factor_ref in enumerate(factors):
        lanes = lanes_of(lax.rem(here_ref[0] + ranks - shift, ranks))
        for side in range(2):
            all_ref[pl.ds(side * rows, rows), lanes] = factor_ref[side]
    half = x_ref.shape[1] // 2
    chunks = mine_ref.shape[0]
    core = core_ref[0]
    g = vec_ref[5:6]
    scale = SCALE / g
    place = lax.broadcasted_iota(jnp.int32, (half, chunks), 1)
    wanted = lax.broadcasted_iota(jnp.int32, (half, chunks), 0)
    wanted = (wanted // 4) * 8 + wanted % 4
    xq, cq, yr, cr = (vec_ref[i : i + 1] for i in range(4))
    top = None
    for emb_ref, offset, count, total, out_ref in (
        (x_ref, 4, cr, yr, grad_q_ref),
        (y_ref, 0, cq, xq, grad_r_ref),
    ):
        select = jnp.where(place == wanted + offset, 1.0, 0.0).astype(BF16)
        product = None
        for position, cross_ref in ((core, mine_ref), (1 - core, other_ref)):
            rows = jnp.dot(select, cross_ref[...], preferred_element_type=F32).astype(BF16)
            emb = emb_ref[:, pl.ds(pl.multiple_of(position * half, half), half)]
            part = jnp.dot(emb, rows, preferred_element_type=F32)
            product = part if product is None else product + part
        norms = jnp.sum(jnp.square(emb_ref[...].astype(F32)), axis=1, keepdims=True)
        grad = scale * (norms * count + total - 2.0 * product)
        out_ref[...] = grad
        here = jnp.max(jnp.abs(grad), axis=0, keepdims=True)
        top = here if top is None else jnp.maximum(top, here)
    blocks = in_rows(top, dot_ref.shape[0])
    peak = blocks[0]
    for block in blocks[1:]:
        peak = jnp.maximum(peak, block)
    count = peak_ref.shape[0]
    peak_ref[:, 0] = jnp.broadcast_to(peak[None], (count,) + peak.shape)
    dots = dot_ref[...] + dot2_ref[...]
    kept = peak_ref.shape[1] - 1
    for i in range(kept):
        row = jnp.where(core == 0, dots[i : i + 1], dots[kept + i : kept + i + 1])
        peak_ref[:, 1 + i] = jnp.broadcast_to(row[None], (count,) + row.shape)


def kern_kernel(
    here_ref, peak_ref, grad_q_ref, grad_r_ref, vec_ref, all_ref,
    kern_ref, log_ref, eta_ref, own_q_ref, own_r_ref,
):
    rows = grad_q_ref.shape[0]
    width = own_q_ref.shape[1]
    mine = pl.ds(pl.multiple_of(here_ref[0] * width, width), width)
    own_q_ref[...] = grad_q_ref[:, mine]
    own_r_ref[...] = grad_r_ref[:, mine]
    xq, cq, yr, cr = (vec_ref[i : i + 1] for i in range(4))
    g = vec_ref[5:6]
    kept = peak_ref.shape[1] - 1
    got = peak_ref[...].reshape((peak_ref.shape[0] // 2, 2) + peak_ref.shape[1:])
    dot = jnp.concatenate(
        [jnp.sum(got[:, member, 1 + i], axis=0) for member in range(2) for i in range(kept)], axis=1
    )
    grad_g = -(SCALE * (xq * cr + cq * yr - 2.0 * dot)) / jnp.square(g)
    peak = jnp.maximum(
        jnp.max(jnp.max(peak_ref[:, 0], axis=0), axis=1, keepdims=True),
        jnp.max(jnp.abs(grad_g), axis=1, keepdims=True),
    )
    eta = GAMMA / (peak + 1e-06)
    eta_ref[...] = jnp.broadcast_to(eta, eta_ref.shape)
    kern_g = g * jnp.exp(-eta * grad_g)
    log_ref[...] = jnp.concatenate(in_rows(jnp.log(kern_g), log_ref.shape[0]), axis=0)
    for side, grad_ref in enumerate((grad_q_ref, grad_r_ref)):
        part = pl.ds(side * rows, rows)
        kern = all_ref[part, :].astype(F32) * jnp.exp(-eta * grad_ref[...])
        kern_ref[part, :] = kern.astype(BF16)


def new_scalings(ranks, got_ref, v_ref, log_ref):
    t = jnp.sum(got_ref[...].astype(F32), axis=0)
    passed = jnp.log(v_ref[...] * t)
    weights = jnp.exp((log_ref[...] + passed[:ranks] + passed[ranks:]) / 3.0)
    return jnp.concatenate([weights, weights], axis=0) / t, weights


def send_columns(v, mass_ref, own_ref, other_ref, sent_ref, u_ref=None):
    ranks = v.shape[0] // 2
    rows = own_ref.shape[0] // 2

    def kern(member, side):
        return (own_ref, other_ref)[member][pl.ds(side * rows, rows), :]

    v_rows = [stack3(in_lanes(v, side * ranks, ranks)) for side in range(2)]
    sums = []
    for member in range(2):
        for side in range(2):
            part = lax.dot_general(
                v_rows[side], kern(member, side), (((1,), (1,)), ((), ())),
                preferred_element_type=F32,
            )
            sums.append(sum_rows(part))
    u = jnp.exp(POWER * jnp.log(mass_ref[...] / jnp.concatenate(sums, axis=0)))
    if u_ref is not None:
        u_ref[...] = u
    columns = []
    for side in range(2):
        total = None
        for member in range(2):
            row = 2 * member + side
            part = jnp.dot(
                stack3(u[row : row + 1]), kern(member, side), preferred_element_type=F32
            )
            total = part if total is None else total + part
        columns += in_rows(sum_rows(total), ranks)
    part = jnp.concatenate(columns, axis=0).astype(sent_ref.dtype)
    sent_ref[...] = jnp.broadcast_to(part[None], sent_ref.shape)


def first_columns(member, mass_ref, kern_ref):
    rows, columns = kern_ref.shape[0] // 2, kern_ref.shape[1]
    ones = jnp.ones((1, columns), BF16)
    parts = []
    for side in range(2):
        kern = kern_ref[pl.ds(side * rows, rows), :]
        s = lax.dot_general(ones, kern, (((1,), (1,)), ((), ())), preferred_element_type=F32)
        row = 2 * member + side
        u = jnp.exp(POWER * jnp.log(mass_ref[row : row + 1] / s))
        part = sum_rows(jnp.dot(stack3(u), kern, preferred_element_type=F32))
        parts += in_rows(part, columns // 128)
    return jnp.concatenate(parts, axis=0)


def first_own(mass_ref, kern_ref, part_ref):
    part_ref[...] = first_columns(0, mass_ref, kern_ref)


def first_other(mass_ref, kern_ref, part_ref, sent_ref):
    part = (part_ref[...] + first_columns(1, mass_ref, kern_ref)).astype(sent_ref.dtype)
    sent_ref[...] = jnp.broadcast_to(part[None], sent_ref.shape)


def next_pass(
    got_ref, v_ref, log_ref, mass_ref, own_ref, other_ref, sent_ref, new_ref, u_ref=None
):
    v, _ = new_scalings(log_ref.shape[0], got_ref, v_ref, log_ref)
    new_ref[...] = v
    send_columns(v, mass_ref, own_ref, other_ref, sent_ref, u_ref)


def profile_kernel(
    core_ref, got_ref, v_ref, log_ref, u_ref, own_ref, other_ref, expr_ref, more_ref,
    part_ref, new_ref, weights_ref,
):
    ranks = log_ref.shape[0]
    rows = own_ref.shape[0] // 2
    half = own_ref.shape[1] // 2
    v, weights = new_scalings(ranks, got_ref, v_ref, log_ref)
    new_ref[...] = v
    weights_ref[...] = weights
    u_columns = jnp.concatenate([u_ref[...], u_ref[...]], axis=0).T
    core = core_ref[0]
    blocks = [new_ref[pl.ds(ranks + core * (ranks // 2) + i, 1), :] for i in range(ranks // 2)]
    scale = jnp.concatenate(blocks, axis=1)
    lanes = pl.ds(pl.multiple_of(core * half, half), half)
    total = None
    for member, (kern_ref, cells_ref) in enumerate(((own_ref, expr_ref), (other_ref, more_ref))):
        kern = kern_ref[pl.ds(rows, rows), lanes].astype(F32)
        column = u_columns[:, 2 * member + 1 : 2 * member + 2]
        part = contract_rows((kern * scale * column).astype(BF16), cells_ref[...])
        total = part if total is None else total + part
    part_ref[...] = total


def on_chip(kernel, shapes, name, scalars=0, inputs=0, off_chip=0, scratch=(), limit=LIMIT):
    specs = {}
    if scalars:
        specs["in_specs"] = (
            [pl.BlockSpec(memory_space=pltpu.SMEM)] * scalars
            + [pl.BlockSpec(memory_space=pltpu.VMEM)] * inputs
            + [pl.BlockSpec(memory_space=pltpu.HBM)] * off_chip
        )
    return pl.pallas_call(
        kernel,
        out_shape=tuple(jax.ShapeDtypeStruct(shape, dtype) for shape, dtype in shapes),
        scratch_shapes=scratch,
        **specs,
        compiler_params=pltpu.CompilerParams(vmem_limit_bytes=limit),
        name=name,
    )


def shards(x_emb, y_emb, q_factor, r_factor, g_weights, a_mass, b_mass, expr):
    rows, width = q_factor.shape
    dim = x_emb.shape[1]
    genes = expr.shape[1]
    others = lax.axis_size(CHIPS)
    cell_devices = 2 * others
    ranks = lax.axis_size("x")
    cells_total = rows * cell_devices
    share = dim // cell_devices

    here = lax.axis_index("x")
    core = lax.axis_index("c")
    core_index = core.astype(jnp.int32)[None]
    chunk_shape = ((others, 3, share, width), F32)
    keep, give, rounded = on_chip(
        start_kernel,
        (chunk_shape, chunk_shape, ((2, rows, width), BF16)),
        "start",
        scalars=1,
        off_chip=4,
        limit=107 << 19,
        scratch=[
            pltpu.VMEM(x_emb.shape, BF16),
            pltpu.VMEM(y_emb.shape, BF16),
            pltpu.VMEM(q_factor.shape, F32),
            pltpu.VMEM(r_factor.shape, F32),
            pltpu.SemaphoreType.DMA((4, 4)),
        ],
    )(core_index, x_emb, y_emb, q_factor, r_factor)

    def from_shift(shift):
        return lax.ppermute(rounded, "x", [(i, (i + shift) % ranks) for i in range(ranks)])

    outgoing = keep + swap(give)
    columns = ranks * width
    tall = ((rows, columns), F32)
    sent = on_chip(chunk_kernel, (((ranks, 16, width), F32),), "chunk")(
        exchange(outgoing, CHIPS), g_weights[None]
    )[0]
    masses = jnp.stack([a_mass, b_mass])
    got, first, second, third = lax.optimization_barrier(
        (exchange(sent, "x"), from_shift(1), from_shift(2), from_shift(3))
    )
    sent, vec, dot = on_chip(
        spread_kernel,
        (((others, 8, columns), BF16), ((8, columns), F32), ((ranks, width), F32)),
        "spread",
    )(got)
    crosses, other_expr, their_dot, their_masses = lax.optimization_barrier(
        (exchange(sent, CHIPS), swap(expr), swap(dot), swap(masses))
    )
    crosses = crosses.reshape(others * 8, columns)
    own_grad = ((rows, width), F32)
    grad_q, grad_r, peak, factors, masses = on_chip(
        grad_kernel,
        (
            tall, tall, ((cell_devices, 1 + ranks // 2, 1, width), F32),
            ((2 * rows, columns), BF16), ((4, rows), F32),
        ),
        "grad",
        scalars=2,
        inputs=9 + ranks,
    )(
        core_index, here.astype(jnp.int32)[None], x_emb, y_emb, crosses, swap(crosses), vec,
        dot, their_dot, masses, their_masses, rounded, first, second, third,
    )
    kerns, log_g, eta, own_grad_q, own_grad_r = on_chip(
        kern_kernel,
        (((2 * rows, columns), BF16), ((ranks, width), F32), ((1, width), F32), own_grad, own_grad),
        "kern",
        scalars=1,
        inputs=5,
    )(
        here.astype(jnp.int32)[None], exchange(peak, CELLS), grad_q, grad_r, vec, factors
    )
    theirs = swap(kerns)
    sent_shape = ((others, 2 * ranks, width), BF16)
    u_shape = ((4, rows), F32)
    v_shape = ((2 * ranks, width), F32)
    part = on_chip(first_own, (v_shape,), "first_own")(masses, kerns)[0]
    sent = on_chip(first_other, (sent_shape,), "first_other")(masses, theirs, part)[0]
    v = jnp.ones(v_shape[0], F32)
    for step in range(1, PASSES):
        last = (u_shape,) if step == PASSES - 1 else ()
        sent, v, *u = on_chip(next_pass, (sent_shape, v_shape) + last, "next_pass")(
            exchange(sent, CHIPS), v, log_g, masses, kerns, theirs
        )
    (u,) = u
    part, v, weights = on_chip(
        profile_kernel,
        (((ranks * width // 2, genes), F32), v_shape, ((ranks, width), F32)),
        "profile",
        scalars=1,
        inputs=8,
    )(
        core_index, exchange(sent, CHIPS), v, log_g, u, kerns, theirs,
        expr, other_expr,
    )
    part, v, weights, u, eta, core, here = lax.optimization_barrier(
        (part, v, weights, u, eta, core, here)
    )
    v_q, v_r = v[:ranks], v[ranks:]
    kern_q = q_factor * jnp.exp(-eta * own_grad_q)
    kern_r = r_factor * jnp.exp(-eta * own_grad_r)
    q_new = u[0][:, None] * kern_q * pick(v_q, here)[None, :]
    r_new = u[1][:, None] * kern_r * pick(v_r, here)[None, :]
    mine_q = kerns[:rows].astype(F32)
    s_q = jnp.sum(mine_q * v_q.reshape(1, columns), axis=1)
    scaled = (mine_q * (v_q / weights).reshape(1, columns)).astype(BF16)

    half = columns // 2
    mine_scaled = lax.dynamic_slice_in_dim(scaled, core * half, half, 1)
    other_scaled = lax.dynamic_slice_in_dim(scaled, (1 - core) * half, half, 1)
    rank_share = pick(weights, here) / cells_total
    got, q_new, r_new, rank_share, s_q, mine_scaled, other_scaled = lax.optimization_barrier(
        (
            exchange(part.reshape(others, -1, genes), CHIPS),
            q_new, r_new, rank_share, s_q, mine_scaled, other_scaled,
        )
    )
    piece = jnp.sum(got, axis=0)
    mine = to_all(piece.astype(BF16), CHIPS).reshape(half, genes)
    mixed = jnp.dot(mine_scaled, mine, preferred_element_type=F32) + jnp.dot(
        other_scaled, swap(mine), preferred_element_type=F32
    )
    predicted = (mixed / s_q[:, None]).astype(BF16)
    return (q_new, r_new, rank_share, predicted)


def solution(mesh):
    named = Mesh(mesh.devices.reshape(4, 8, 2, 4), EVERY)
    block = P(CELLS, "x")
    return jax.shard_map(
        shards,
        mesh=named,
        in_specs=(
            P(CELLS, None),
            P(CELLS, None),
            block,
            block,
            P("x"),
            P(CELLS),
            P(CELLS),
            block,
        ),
        out_specs=(block, block, P("x"), block),
        check_vma=False,
    )
```
